32 devices in a mesh: dp: 8 (over y, x, core), tensor: 4 (over z).
Axes of the slice: x: 2, y: 2, z: 4, core: 2. Of those that a mesh axis runs over, the one named last changes fastest.
Arguments:
- hidden_in: bfloat16 [16384, 1024], P(('dp', 'tensor')), may hold values from -6 to 6
- cotangent: bfloat16 [16384, 1024], P(('dp', 'tensor')), may hold values from -6 to 6
- norm_gains: bfloat16 [1024, 2], P('dp'), may hold values from 0.5 to 1.5
- mixer_in: bfloat16 [1024, 1536], P('dp', 'tensor'), may hold values from -0.1875 to 0.1875
- branch_gate: bfloat16 [1024, 1536], P('dp', 'tensor'), may hold values from -0.1875 to 0.1875
- mixer_out: bfloat16 [1024, 1536], P('dp', 'tensor'), may hold values from -0.4375 to 0.4375
- input_gate: bfloat16 [128, 12, 128], P('dp', 'tensor'), may hold values from -0.5 to 0.5
- recur_gate: bfloat16 [128, 12, 128], P('dp', 'tensor'), may hold values from -0.5 to 0.5
- conv_kernel: bfloat16 [128, 4, 12], P('dp', None, 'tensor'), may hold values from -3 to 3
- conv_bias: bfloat16 [128, 12], P('dp', 'tensor'), may hold values from -4 to 4
- input_bias: bfloat16 [128, 12], P('dp', 'tensor'), may hold values from -6 to 6
- recur_bias: bfloat16 [128, 12], P('dp', 'tensor'), may hold values from -6 to 6
- decay_param: bfloat16 [128, 12], P('dp', 'tensor'), may hold values from 2 to 9
- mlp_gate: bfloat16 [1024, 3072], P('dp', 'tensor'), may hold values from -0.1875 to 0.1875
- mlp_up: bfloat16 [1024, 3072], P('dp', 'tensor'), may hold values from -0.1875 to 0.1875
- mlp_down: bfloat16 [1024, 3072], P('dp', 'tensor'), may hold values from -0.15625 to 0.15625
Outputs:
- hidden_out: bfloat16 [16384, 1024], P(('dp', 'tensor'))
- hidden_grad: float32 [16384, 1024], P(('dp', 'tensor'))
- norm_gains_grad: float32 [1024, 2], P(('dp', 'tensor'))
- mixer_in_grad: float32 [1024, 1536], P('dp', 'tensor')
- branch_gate_grad: float32 [1024, 1536], P('dp', 'tensor')
- mixer_out_grad: float32 [1024, 1536], P('dp', 'tensor')
- input_gate_grad: float32 [128, 12, 128], P('dp', 'tensor')
- recur_gate_grad: float32 [128, 12, 128], P('dp', 'tensor')
- conv_kernel_grad: float32 [128, 4, 12], P('dp', None, 'tensor')
- conv_bias_grad: float32 [128, 12], P('dp', 'tensor')
- input_bias_grad: float32 [128, 12], P('dp', 'tensor')
- recur_bias_grad: float32 [128, 12], P('dp', 'tensor')
- decay_param_grad: float32 [128, 12], P('dp', 'tensor')
- mlp_gate_grad: float32 [1024, 3072], P('dp', 'tensor')
- mlp_up_grad: float32 [1024, 3072], P('dp', 'tensor')
- mlp_down_grad: float32 [1024, 3072], P('dp', 'tensor')
The draws below stay inside these ranges and needn't reach their ends.
All inputs are finite; a program needn't handle non-finite values.
Results may differ from the reference program's by a relative error of at most 0.02.
Values may be sent and summed in bfloat16 or wider, within the bound.
No kernel may reach another device: no remote copies, remote signals or barrier semaphores. Data moves between devices by JAX's collectives and lax.ppermute only.
A program may use at most 256 MiB of HBM per device.

```python
import jax
import jax.numpy as jnp
from jax import lax

D = 1024
R = 1536
FF = 3072
BLOCK = 128
CONV = 4
SEQ_LEN = 2048
BLOCKS = 12
TOKENS = 16384
N_DP = 8


def with_spikes(array, rng, source, target, blocks, factor):
    owner, partner = [(jnp.arange(array.shape[axis_at]) // (array.shape[axis_at] // blocks)).reshape([-1 if axis == axis_at else 1 for axis in range(array.ndim)]) for axis_at in (source, target)]
    chosen = jax.random.permutation(rng, blocks)[partner]
    strong = (owner == chosen) | (owner == (partner + blocks // 2) % blocks)
    return jnp.where(strong, factor * array, array)


def shard_levels(key, dims, cuts, least, top_value):
    gain, own = 1.0, jax.random.fold_in(key, 6)
    for position, parts in cuts:
        draws = jnp.exp(jax.random.uniform(jax.random.fold_in(own, position), (parts,), jnp.float32, least / len(cuts), top_value / len(cuts)))
        gain = gain * jnp.repeat(draws, dims[position] // parts).reshape([-1 if axis == position else 1 for axis in range(len(dims))])
    return gain


def bell_draw(rng, shape, scale, bound, cuts=(), held_as=jnp.bfloat16):
    values = jax.random.normal(rng, shape, jnp.float32) * scale
    if len(cuts) > 0:
        values = shard_levels(rng, shape, cuts, -0.22, 0.18) * values
    return jnp.clip(values, min=-bound, max=bound).astype(held_as)


def bell_draw_with(stream_key, dims, deviation, limit, cuts, heavy, kind=jnp.bfloat16):
    values = deviation * jax.random.normal(stream_key, dims, jnp.float32)
    if cuts:
        values = values * shard_levels(stream_key, dims, cuts, -0.22, 0.18)
    return jnp.clip(with_spikes(values, jax.random.fold_in(stream_key, 3), *heavy), -limit, limit).astype(kind)


def setup_inputs(seed: int = 0) -> dict:
    key_of = jax.random.split(jax.random.key(seed), 17)
    return {
        "hidden_in": bell_draw(key_of[0], (TOKENS, D), 1.0, 6.0, ((0, 32),)),
        "cotangent": bell_draw_with(key_of[1], (TOKENS, D), 1.0, 6.0, ((0, 32),), (0, 1, 32, 2.75)),
        "norm_gains": jnp.clip(1.0 + 0.1 * jax.random.normal(key_of[2], (D, 2), jnp.float32), 0.5, 1.5).astype(jnp.bfloat16),
        "mixer_in": bell_draw(key_of[3], (D, R), D ** -0.5, 0.1875, ((0, 8), (1, 4))),
        "branch_gate": bell_draw(key_of[4], (D, R), D ** -0.5, 0.1875, ((0, 8), (1, 4))),
        "mixer_out": bell_draw(key_of[5], (D, R), (R // 8) ** -0.5, 0.4375, ((0, 8), (1, 4))),
        "input_gate": bell_draw(key_of[6], (BLOCK, BLOCKS, BLOCK), BLOCK ** -0.5, 0.5, ((0, 8), (1, 4))),
        "recur_gate": bell_draw(key_of[7], (BLOCK, BLOCKS, BLOCK), BLOCK ** -0.5, 0.5, ((0, 8), (1, 4))),
        "conv_kernel": bell_draw(key_of[8], (BLOCK, CONV, BLOCKS), CONV ** -0.5, 3.0, ((0, 8), (2, 4))),
        "conv_bias": bell_draw(key_of[9], (BLOCK, BLOCKS), 0.3, 4.0, ((0, 8), (1, 4))),
        "input_bias": bell_draw(key_of[10], (BLOCK, BLOCKS), 0.5, 6.0, ((0, 8), (1, 4))),
        "recur_bias": bell_draw(key_of[11], (BLOCK, BLOCKS), 0.5, 6.0, ((0, 8), (1, 4))),
        "decay_param": jnp.clip(2.0 + 7.0 * jax.random.uniform(key_of[12], (BLOCK, BLOCKS), jnp.float32) ** shard_levels(key_of[12], (BLOCK, BLOCKS), ((0, 8), (1, 4)), -0.2, 0.2), 2.0, 9.0).astype(jnp.bfloat16),
        "mlp_gate": bell_draw(key_of[13], (D, FF), D ** -0.5, 0.1875, ((0, 8), (1, 4))),
        "mlp_up": bell_draw(key_of[14], (D, FF), D ** -0.5, 0.1875, ((0, 8), (1, 4))),
        "mlp_down": bell_draw(key_of[15], (D, FF), (FF // 2) ** -0.5, 0.15625, ((0, 8), (1, 4))),
    }


@jax.custom_vjp
def low(v):
    return lax.optimization_barrier(v.astype(jnp.bfloat16)).astype(jnp.float32)

@jax.custom_vjp
def low_back(v):
    return v

def low_keep(v):
    return (low(v), None)

def low_pass(kept, grad):
    return (grad,)

def back_keep(v):
    return (v, None)

def back_low(kept, grad):
    return (low(grad),)
low.defvjp(low_keep, low_pass)
low_back.defvjp(back_keep, back_low)
epsilon = 1e-06
highest = lax.Precision.HIGHEST

def matmul(left_side, right_side):
    return jnp.dot(left_side, right_side, precision=highest, preferred_element_type=jnp.float32)

def matmul_nt(left_side, right_side):
    return lax.dot_general(left_side, right_side, (((1,), (1,)), ((), ())), precision=highest, preferred_element_type=jnp.float32)

def rms_scale(values):
    return values * lax.rsqrt(lax.optimization_barrier(jnp.mean(values * values, axis=1, keepdims=True)) + epsilon)

def channels(table_rows):
    return table_rows.T.reshape(-1)

def causal_conv(signal, kernel, conv_shift):
    length = signal.shape[0]
    padded = jnp.pad(signal, ((CONV - 1, 0), (0, 0)))
    result = conv_shift + kernel[0] * signal
    for offset in range(1, CONV):
        result = result + kernel[offset] * padded[CONV - 1 - offset:CONV - 1 - offset + length]
    return result

def combine(earlier_part, later_part):
    return (earlier_part[0] * later_part[0], later_part[0] * earlier_part[1] + later_part[1])

def mixer(conv_out, rec_pre, inp_pre, rec_shift, inp_shift, decay_rate, gate_pre):
    recur_open = jax.nn.sigmoid(rec_pre + rec_shift)
    inflow = jax.nn.sigmoid(inp_pre + inp_shift)
    log_decay = -8.0 * recur_open * jax.nn.softplus(-decay_rate)
    multiplier = jnp.sqrt(-jnp.expm1(2.0 * log_decay))
    states = lax.associative_scan(combine, (jnp.exp(log_decay), multiplier * inflow * conv_out), axis=0)[1]
    return states * jax.nn.gelu(gate_pre)

def forward(hidden, gain_table, mixer_in, branch_gate, mixer_out, input_gate, recur_gate, conv_kernel, conv_bias, input_bias, recur_bias, decay_param, mlp_gate, mlp_up, mlp_down):
    length = hidden.shape[0]
    normed = low(rms_scale(hidden) * gain_table[:, 0])
    branch_in = low_back(matmul(normed, mixer_in))
    gate_pre = low_back(matmul(normed, branch_gate))
    kernel = conv_kernel.transpose(1, 2, 0).reshape(CONV, R)
    conv_out = causal_conv(branch_in, kernel, channels(conv_bias))
    blocked = low(conv_out).reshape(length, BLOCKS, BLOCK)
    rec_pre = low_back(jnp.einsum('tbj,jbk->tbk', blocked, recur_gate, precision=highest).reshape(length, R))
    inp_pre = low_back(jnp.einsum('tbj,jbk->tbk', blocked, input_gate, precision=highest).reshape(length, R))
    mixed_out = low(mixer(conv_out, rec_pre, inp_pre, channels(recur_bias), channels(input_bias), channels(decay_param), gate_pre))
    middle = hidden + low_back(matmul_nt(mixed_out, mixer_out))
    normed_two = low(rms_scale(middle) * gain_table[:, 1])
    gate_val = low_back(matmul(normed_two, mlp_gate))
    up_val = low_back(matmul(normed_two, mlp_up))
    hidden_mlp = low(jax.nn.gelu(gate_val) * up_val)
    return middle + matmul_nt(hidden_mlp, mlp_down)

def reference(hidden_in, cotangent, norm_gains, mixer_in, branch_gate, mixer_out, input_gate, recur_gate, conv_kernel, conv_bias, input_bias, recur_bias, decay_param, mlp_gate, mlp_up, mlp_down):
    weights = jax.tree.map(lambda values: values.astype(jnp.float32), (norm_gains, mixer_in, branch_gate, mixer_out, input_gate, recur_gate, conv_kernel, conv_bias, input_bias, recur_bias, decay_param, mlp_gate, mlp_up, mlp_down))
    sequences = hidden_in.astype(jnp.float32).reshape(N_DP, SEQ_LEN, D)
    seq_cots = cotangent.astype(jnp.float32).reshape(N_DP, SEQ_LEN, D)
    zeros_all = jax.tree.map(jnp.zeros_like, weights)

    def per_sequence(totals, inputs_pair):
        seq_in, seq_cot = inputs_pair
        result, pullback = jax.vjp(forward, seq_in, *weights)
        gradients = pullback(seq_cot)
        new_totals = jax.tree.map(jnp.add, totals, tuple(gradients[1:]))
        return (new_totals, (result.astype(jnp.bfloat16), gradients[0]))
    totals, outputs = lax.scan(per_sequence, zeros_all, (sequences, seq_cots))
    return (outputs[0].reshape(TOKENS, D), outputs[1].reshape(TOKENS, D), totals[0], totals[1], totals[2], totals[3], totals[4], totals[5], totals[6], totals[7], totals[8], totals[9], totals[10], totals[11], totals[12], totals[13])
```

```python
import jax
import jax.numpy as jnp
from jax import lax
from jax.experimental import pallas as pl
from jax.experimental.pallas import tpu as pltpu
from jax.sharding import PartitionSpec as P

BLOCK = 128
CONV = 4
HALO = 16
TILE = 64
GROUP = 256
epsilon = 1e-06
f32 = jnp.float32
bf16 = jnp.bfloat16
ROOT = 0.7978845608028654
CUBIC = 0.044715


def nn(left, right):
    return lax.dot_general(left, right, (((1,), (0,)), ((), ())), preferred_element_type=f32)


def nt(left, right):
    return lax.dot_general(left, right, (((1,), (1,)), ((), ())), preferred_element_type=f32)


def tn(left, right):
    return lax.dot_general(left, right, (((0,), (0,)), ((), ())), preferred_element_type=f32)


def gelu_parts(value):
    square = value * value
    curve = jnp.tanh(ROOT * value * (1.0 + CUBIC * square))
    half = 0.5 * (1.0 + curve)
    slope = half + (0.5 * ROOT) * value * (1.0 - curve * curve) * (1.0 + 3.0 * CUBIC * square)
    return value * half, slope


def one_minus_exp(value):
    series = 1.0 + value * (1.0 / 7.0)
    for term in (6.0, 5.0, 4.0, 3.0, 2.0):
        series = 1.0 + value * (1.0 / term) * series
    return jnp.where(value > -0.25, -value * series, 1.0 - jnp.exp(value))


def scan_rows(decay_ref, drive_ref, offset, out_ref, out_offset, total_ref, length, reverse):
    width = drive_ref.shape[1]
    rows = lax.broadcasted_iota(jnp.int32, (8, width), 0)
    steps = length // 8

    def body(step, carry):
        state, product = carry
        at = (steps - 1 - step) if reverse else step
        start = pl.multiple_of(at * 8, 8)
        decay = decay_ref[pl.ds(start, 8 + 8 * (offset > 0)), :][offset : offset + 8]
        drive = drive_ref[pl.ds(start, 8), :]
        for shift in (1, 2, 4):
            if reverse:
                inside = rows < 8 - shift
                amount = 8 - shift
            else:
                inside = rows >= shift
                amount = shift
            drive = drive + decay * jnp.where(inside, pltpu.roll(drive, amount, 0), 0.0)
            decay = decay * jnp.where(inside, pltpu.roll(decay, amount, 0), 1.0)
        state = drive + decay * state
        product = decay * product
        out_ref[pl.ds(start + out_offset, 8), :] = state
        total_ref[pl.ds(start, 8), :] = product
        edge = 0 if reverse else 7
        return (
            jnp.broadcast_to(state[edge : edge + 1], (8, width)),
            jnp.broadcast_to(product[edge : edge + 1], (8, width)),
        )

    lax.fori_loop(0, steps, body, (jnp.zeros((8, width), f32), jnp.ones((8, width), f32)))


def tiles(length, body):
    def step(index, carry):
        body(pl.multiple_of(index * TILE, TILE))
        return carry

    lax.fori_loop(0, length // TILE, step, 0)


def mix_in_kernel(
    normed_ref, low_ref, high_ref, rgate_ref, igate_ref, table_ref,
    branch_ref, conv_ref, open_ref, flow_ref, local_ref, product_ref,
    conv_low, rec_buf, inp_buf, decay_buf,
):
    length = conv_ref.shape[0]
    half = low_ref.shape[0]
    branch_ref[...] = nn(normed_ref[:, :half], low_ref[...]) + nn(normed_ref[:, half:], high_ref[...])
    for part in range(GROUP // BLOCK):
        lanes = slice(part * BLOCK, (part + 1) * BLOCK)

        def convolve(start):
            window = branch_ref[pl.ds(start + HALO - 8, TILE + 8), lanes]
            result = table_ref[4:5, lanes] + table_ref[0:1, lanes] * window[8:]
            for offset in range(1, CONV):
                result = result + table_ref[offset : offset + 1, lanes] * window[8 - offset : 8 - offset + TILE]
            conv_ref[pl.ds(start, TILE), lanes] = result
            conv_low[pl.ds(start, TILE), lanes] = result.astype(bf16)

        tiles(length, convolve)
        rec_buf[:, lanes] = nn(conv_low[:, lanes], rgate_ref[part])
        inp_buf[:, lanes] = nn(conv_low[:, lanes], igate_ref[part])

        def gates(start):
            rows = pl.ds(start, TILE)
            recur_open = jax.nn.sigmoid(rec_buf[rows, lanes] + table_ref[6:7, lanes])
            inflow = jax.nn.sigmoid(inp_buf[rows, lanes] + table_ref[5:6, lanes])
            log_decay = recur_open * table_ref[7:8, lanes]
            multiplier = jnp.sqrt(one_minus_exp(2.0 * log_decay))
            open_ref[rows, lanes] = recur_open
            flow_ref[rows, lanes] = inflow
            decay_buf[rows, lanes] = jnp.exp(log_decay)
            rec_buf[rows, lanes] = multiplier * inflow * conv_ref[rows, lanes]

        tiles(length, gates)
    scan_rows(decay_buf, rec_buf, 0, local_ref, 0, product_ref, length, False)


def mix_out_kernel(
    normed_ref, low_ref, high_ref, local_ref, product_ref, enter_ref, sum_ref,
    pre_ref, states_ref, mixed_ref, total_ref,
):
    length = local_ref.shape[0]
    half = low_ref.shape[0]

    @pl.when(pl.program_id(0) == 0)
    def _():
        total_ref[...] = sum_ref[...]

    pre_ref[...] = nn(normed_ref[HALO:, :half], low_ref[:, :GROUP]) + nn(normed_ref[HALO:, half:], high_ref[:, :GROUP])
    states_ref[0:8, :] = jnp.broadcast_to(enter_ref[0:1, :], (8, GROUP))
    for part in range(GROUP // BLOCK):
        lanes = slice(part * BLOCK, (part + 1) * BLOCK)

        def mix(start):
            rows = pl.ds(start, TILE)
            states = local_ref[rows, lanes] + product_ref[rows, lanes] * enter_ref[0:1, lanes]
            states_ref[pl.ds(start + 8, TILE), lanes] = states
            gate = pre_ref[rows, lanes]
            curve = jnp.tanh(ROOT * gate * (1.0 + CUBIC * gate * gate))
            mixed_ref[rows, lanes] = (states * (gate * (0.5 * (1.0 + curve)))).astype(bf16)

        tiles(length, mix)
    total_ref[:, :half] += nt(mixed_ref[...], low_ref[:, GROUP:])
    total_ref[:, half:] += nt(mixed_ref[...], high_ref[:, GROUP:])


def mlp_kernel(
    normed_ref, normed_t_ref, cot_ref, cot_t_ref, low_ref, high_ref, sum_ref, back_ref,
    total_ref, grad_ref, low_grad_ref, high_grad_ref,
    pre, hidden, pre_low, act,
):
    length = normed_ref.shape[0]
    half = low_ref.shape[0]

    @pl.when(pl.program_id(0) == 0)
    def _():
        total_ref[...] = sum_ref[...]
        grad_ref[...] = back_ref[...]

    pre[...] = nn(normed_ref[:, :half], low_ref[:, : 2 * GROUP]) + nn(normed_ref[:, half:], high_ref[:, : 2 * GROUP])
    act[...] = nn(cot_ref[:, :half], low_ref[:, 2 * GROUP :]) + nn(cot_ref[:, half:], high_ref[:, 2 * GROUP :])
    for part in range(GROUP // BLOCK):
        lanes = slice(part * BLOCK, (part + 1) * BLOCK)
        up_lanes = slice(GROUP + part * BLOCK, GROUP + (part + 1) * BLOCK)

        def activate(start):
            rows = pl.ds(start, TILE)
            value, slope = gelu_parts(pre[rows, lanes])
            up = pre[rows, up_lanes]
            grad = act[rows, lanes]
            hidden[rows, lanes] = (value * up).astype(bf16)
            pre_low[rows, lanes] = (grad * up * slope).astype(bf16)
            pre_low[rows, up_lanes] = (grad * value).astype(bf16)

        tiles(length, activate)
    total_ref[:, :half] += nt(hidden[...], low_ref[:, 2 * GROUP :])
    total_ref[:, half:] += nt(hidden[...], high_ref[:, 2 * GROUP :])
    grad_ref[:, :half] += nt(pre_low[...], low_ref[:, : 2 * GROUP])
    grad_ref[:, half:] += nt(pre_low[...], high_ref[:, : 2 * GROUP])
    low_grad_ref[:, : 2 * GROUP] = nn(normed_t_ref[:half], pre_low[...]).astype(bf16)
    high_grad_ref[:, : 2 * GROUP] = nn(normed_t_ref[half:], pre_low[...]).astype(bf16)
    low_grad_ref[:, 2 * GROUP :] = nn(cot_t_ref[:half], hidden[...]).astype(bf16)
    high_grad_ref[:, 2 * GROUP :] = nn(cot_t_ref[half:], hidden[...]).astype(bf16)


def mix_back_kernel(
    grad_low_ref, grad_t_ref, normed_t_ref, low_ref, high_ref, pre_ref, states_ref, mixed_ref, open_ref, table_ref, sum_ref,
    total_ref, local_ref, product_ref, edge_ref, low_grad_ref, high_grad_ref,
    mixed_grad, drive, pre_low, decay_buf,
):
    length = pre_ref.shape[0]
    half = low_ref.shape[0]

    @pl.when(pl.program_id(0) == 0)
    def _():
        total_ref[...] = sum_ref[...]

    mixed_grad[...] = nn(grad_low_ref[:, :half], low_ref[:, GROUP:]) + nn(grad_low_ref[:, half:], high_ref[:, GROUP:])
    decay_buf[pl.ds(length, 8), :] = jnp.ones((8, GROUP), f32)
    for part in range(GROUP // BLOCK):
        lanes = slice(part * BLOCK, (part + 1) * BLOCK)

        def back(start):
            rows = pl.ds(start, TILE)
            value, slope = gelu_parts(pre_ref[rows, lanes])
            grad = mixed_grad[rows, lanes]
            pre_low[rows, lanes] = (grad * states_ref[pl.ds(start + 8, TILE), lanes] * slope).astype(bf16)
            drive[rows, lanes] = grad * value
            decay_buf[rows, lanes] = jnp.exp(open_ref[rows, lanes] * table_ref[7:8, lanes])

        tiles(length, back)
    scan_rows(decay_buf, drive, 1, local_ref, 0, product_ref, length, True)
    edge_ref[0:1, :] = decay_buf[0:1, :] * local_ref[0:1, :]
    edge_ref[1:2, :] = decay_buf[0:1, :] * product_ref[0:1, :]
    total_ref[:, :half] += nt(pre_low[...], low_ref[:, :GROUP])
    total_ref[:, half:] += nt(pre_low[...], high_ref[:, :GROUP])
    low_grad_ref[:, :GROUP] = nn(normed_t_ref[:half, HALO:], pre_low[...]).astype(bf16)
    high_grad_ref[:, :GROUP] = nn(normed_t_ref[half:, HALO:], pre_low[...]).astype(bf16)
    low_grad_ref[:, GROUP:] = nn(grad_t_ref[:half], mixed_ref[...]).astype(bf16)
    high_grad_ref[:, GROUP:] = nn(grad_t_ref[half:], mixed_ref[...]).astype(bf16)


def gate_back_kernel(
    local_ref, product_ref, enter_ref, states_ref, open_ref, flow_ref, conv_ref, branch_ref, rgate_ref, igate_ref, table_ref,
    conv_grad_ref, rgrad_ref, igrad_ref, sums_ref,
    rec_low, inp_low, conv_low,
):
    length = local_ref.shape[0]
    for part in range(GROUP // BLOCK):
        lanes = slice(part * BLOCK, (part + 1) * BLOCK)

        def back(index, sums):
            start = pl.multiple_of(index * TILE, TILE)
            rows = pl.ds(start, TILE)
            carried = local_ref[rows, lanes] + product_ref[rows, lanes] * enter_ref[0:1, lanes]
            recur_open = open_ref[rows, lanes]
            inflow = flow_ref[rows, lanes]
            conv_out = conv_ref[rows, lanes]
            rate = table_ref[7:8, lanes]
            log_decay = recur_open * rate
            decay = jnp.exp(log_decay)
            multiplier = jnp.sqrt(one_minus_exp(2.0 * log_decay))
            before = states_ref[pl.ds(start, TILE + 8), lanes][7 : 7 + TILE]
            weighted = carried * inflow
            decay_grad = carried * before * decay - weighted * conv_out * decay * decay / multiplier
            scaled = decay_grad * recur_open
            rec_grad = rate * scaled * (1.0 - recur_open)
            direct = weighted * multiplier
            inp_grad = direct * conv_out * (1.0 - inflow)
            rec_low[rows, lanes] = rec_grad.astype(bf16)
            inp_low[rows, lanes] = inp_grad.astype(bf16)
            conv_low[rows, lanes] = conv_out.astype(bf16)
            conv_grad_ref[rows, lanes] = direct

            def fold(value):
                return jnp.sum(value.reshape(TILE // 8, 8, BLOCK), axis=0)

            return (sums[0] + fold(rec_grad), sums[1] + fold(inp_grad), sums[2] + fold(scaled))

        zero = jnp.zeros((8, BLOCK), f32)
        sums = lax.fori_loop(0, length // TILE, back, (zero, zero, zero))
        for row, value in zip((2, 1, 3), sums):
            sums_ref[row : row + 1, lanes] = jnp.sum(value, axis=0, keepdims=True)
        rgrad_ref[part] = tn(conv_low[:, lanes], rec_low[:, lanes])
        igrad_ref[part] = tn(conv_low[:, lanes], inp_low[:, lanes])
        conv_grad_ref[:, lanes] += nt(rec_low[:, lanes], rgate_ref[part]) + nt(inp_low[:, lanes], igate_ref[part])

        def taps(index, sums):
            start = pl.multiple_of(index * TILE, TILE)
            grad = conv_grad_ref[pl.ds(start, TILE), lanes]

            def fold(value):
                return jnp.sum(value.reshape(TILE // 8, 8, BLOCK), axis=0)

            window = branch_ref[pl.ds(start + HALO - 8, TILE + 8), lanes]
            new = [sums[0] + fold(grad)]
            for offset in range(CONV):
                new.append(sums[offset + 1] + fold(grad * window[8 - offset : 8 - offset + TILE]))
            return tuple(new)

        sums = lax.fori_loop(0, length // TILE, taps, (zero,) * (CONV + 1))
        for row, value in zip((0, 4, 5, 6, 7), sums):
            sums_ref[row : row + 1, lanes] = jnp.sum(value, axis=0, keepdims=True)


def branch_back_kernel(
    conv_grad_ref, after_ref, table_ref, normed_t_ref, low_ref, high_ref, sum_ref,
    total_ref, low_grad_ref, high_grad_ref,
    padded, branch_low,
):
    length = conv_grad_ref.shape[0]
    half = low_ref.shape[0]

    @pl.when(pl.program_id(0) == 0)
    def _():
        total_ref[...] = sum_ref[...]

    padded[pl.ds(0, length), :] = conv_grad_ref[...]
    padded[pl.ds(length, 8), :] = after_ref[...]
    for part in range(GROUP // BLOCK):
        lanes = slice(part * BLOCK, (part + 1) * BLOCK)

        def back(start):
            window = padded[pl.ds(start, TILE + 8), lanes]
            result = table_ref[0:1, lanes] * window[:TILE]
            for offset in range(1, CONV):
                result = result + table_ref[offset : offset + 1, lanes] * window[offset : offset + TILE]
            branch_low[pl.ds(start, TILE), lanes] = result.astype(bf16)

        tiles(length, back)
    total_ref[:, :half] += nt(branch_low[...], low_ref[...])
    total_ref[:, half:] += nt(branch_low[...], high_ref[...])
    low_grad_ref[...] = nn(normed_t_ref[:half, HALO:], branch_low[...]).astype(bf16)
    high_grad_ref[...] = nn(normed_t_ref[half:, HALO:], branch_low[...]).astype(bf16)


def fixed(shape):
    return pl.BlockSpec(shape, lambda g: (0,) * len(shape))


def lanes_of(rows, width=GROUP):
    return pl.BlockSpec((rows, width), lambda g: (0, g))


def blocks_of():
    return pl.BlockSpec((GROUP // BLOCK, BLOCK, BLOCK), lambda g: (g, 0, 0))


def shaped(*dims, kind=f32):
    return jax.ShapeDtypeStruct(dims, kind)


PARAMS = pltpu.CompilerParams(dimension_semantics=("arbitrary",), vmem_limit_bytes=56 * 1024 * 1024)


def call(kernel, steps, in_specs, out_specs, out_shape, scratch, aliases=None):
    return pl.pallas_call(
        kernel,
        grid=(steps,),
        in_specs=in_specs,
        out_specs=out_specs,
        out_shape=out_shape,
        scratch_shapes=scratch,
        compiler_params=PARAMS,
        input_output_aliases=aliases or {},
    )


def rms_parts(values):
    scaling = lax.rsqrt(jnp.mean(values * values, axis=1, keepdims=True) + epsilon)
    return (values * scaling, scaling)


def make_per_device(dp_size, tensor_size):
    pairs = tensor_size // 2
    dp_bits = [1 << bit for bit in range(dp_size.bit_length() - 1)]
    order_one = dp_bits[1:] + dp_bits[:1]
    order_two = dp_bits[2:3] + dp_bits[1:2] + dp_bits[3:] + dp_bits[:1]
    position_of = {bit: place for place, bit in enumerate(order_one)}

    def swap_dp(values, bit):
        return lax.ppermute(values, "dp", [(at, at ^ bit) for at in range(dp_size)])

    def swap_tensor(values, bit):
        return lax.ppermute(values, "tensor", [(at, at ^ bit) for at in range(tensor_size)])

    def set_bit(index, bit):
        return (index & bit) != 0

    def relative(pieces, index, bits):
        for bit, place in bits:
            flag = set_bit(index, bit)
            pieces = [jnp.where(flag, pieces[at ^ place], piece) for at, piece in enumerate(pieces)]
        return pieces

    dp_places = [(bit, 1 << position_of[bit]) for bit in dp_bits]
    tensor_places = [(1 << bit, 1 << bit) for bit in range(tensor_size.bit_length() - 1)]

    def place_index(place):
        return sum(bit for bit, at in dp_places if place & at)

    def to_places(pieces, index):
        return relative([pieces[place_index(place)] for place in range(dp_size)], index, dp_places)

    def from_places(pieces, index):
        pieces = relative(pieces, index, dp_places)
        found = [None] * dp_size
        for place in range(dp_size):
            found[place_index(place)] = pieces[place]
        return found

    def split_lanes(values, count):
        width = values.shape[1] // count
        return [values[:, at * width : (at + 1) * width] for at in range(count)]

    def gather_dp(values, order):
        rows = values.shape[0]
        done = []
        for bit in order[:-1]:
            received = swap_dp(values, bit)
            low_place = position_of[bit]
            if all(position_of[other] < low_place for other in done):
                values = jnp.concatenate([values, received], axis=0)
            else:
                pieces = []
                for at in range(values.shape[0] // rows):
                    pieces += [values[at * rows : (at + 1) * rows], received[at * rows : (at + 1) * rows]]
                values = jnp.concatenate(pieces, axis=0)
            done.append(bit)
        return values, swap_dp(values, order[-1])

    def add(one, two):
        return (one.astype(f32) + two.astype(f32)).astype(bf16)

    def scatter_dp(own, other, order, block_rows):
        values = add(own, swap_dp(other, order[-1]))
        left = list(order[:-1])
        while left:
            bit = left.pop()
            place = position_of[bit]
            rows = values.shape[0]
            if all(position_of[o] < place for o in left):
                keep, send = values[: rows // 2], values[rows // 2 :]
            else:
                count = rows // block_rows
                take = lambda start: jnp.concatenate(
                    [values[at * block_rows : (at + 1) * block_rows] for at in range(start, count, 2)], axis=0
                )
                keep, send = take(0), take(1)
            values = add(keep, swap_dp(send, bit))
        return values

    def per_device(
        hidden_in, cotangent, norm_gains, mixer_in, branch_gate, mixer_out, input_gate, recur_gate,
        conv_kernel, conv_bias, input_bias, recur_bias, decay_param, mlp_gate, mlp_up, mlp_down,
    ):
        dp_at = lax.axis_index("dp")
        tensor_at = lax.axis_index("tensor")
        length, model = hidden_in.shape
        block_rows, chunk = mixer_in.shape
        half = model // 2
        hidden_chunk = mlp_gate.shape[1]
        sub = block_rows * BLOCK // model
        local_blocks = chunk // BLOCK
        pair_width = 2 * chunk
        groups = pair_width // GROUP
        mlp_groups = hidden_chunk // GROUP

        def rows_first(table):
            return table.transpose(1, 0, 2).reshape(-1, BLOCK)

        taps = conv_kernel.transpose(1, 2, 0).reshape(-1)
        vectors = [table.T.reshape(-1) for table in (conv_bias, input_bias, recur_bias, decay_param)]
        flat = jnp.concatenate([taps, *vectors, norm_gains.T.reshape(-1)])
        gate_rows = 2 * local_blocks * sub
        spare = (block_rows - gate_rows) * BLOCK - flat.shape[0]
        small = jnp.concatenate(
            [rows_first(recur_gate), rows_first(input_gate), jnp.pad(flat, (0, spare)).reshape(-1, BLOCK)], axis=0
        )
        first_rows = lax.ppermute(
            hidden_in[length - HALO :], "tensor", [(at, at + 1) for at in range(tensor_size - 1)]
        )

        def spread_tensor(values):
            found = [values]
            for bit, _ in tensor_places:
                received = swap_tensor(jnp.concatenate(found, axis=1), bit)
                found = found + split_lanes(received, len(found))
            return found

        small_all = jnp.concatenate(spread_tensor(small), axis=1)
        small_low, small_high = gather_dp(small_all, order_one)

        def gather_pairs(values, arrange):
            found = spread_tensor(values)
            result = []
            for pair in range(pairs):
                packed = arrange(found[2 * pair], found[2 * pair + 1])
                result.append(gather_dp(packed, order_one if pair % 2 == 0 else order_two))
            return result

        in_pairs = gather_pairs(mixer_in, lambda one, two: jnp.concatenate([one, two], axis=1))

        def interleave(one, two):
            gate = jnp.concatenate([one[:, :chunk], two[:, :chunk]], axis=1)
            out = jnp.concatenate([one[:, chunk:], two[:, chunk:]], axis=1)
            pieces = []
            for at in range(groups):
                pieces += [gate[:, at * GROUP : (at + 1) * GROUP], out[:, at * GROUP : (at + 1) * GROUP]]
            return jnp.concatenate(pieces, axis=1)

        out_pairs = gather_pairs(jnp.concatenate([branch_gate, mixer_out], axis=1), interleave)
        mlp_pieces = []
        for at in range(mlp_groups):
            mlp_pieces += [w[:, at * GROUP : (at + 1) * GROUP] for w in (mlp_gate, mlp_up, mlp_down)]
        mlp_chunks = [
            gather_dp(values, order_one if at % 2 == 0 else order_two)
            for at, values in enumerate(spread_tensor(jnp.concatenate(mlp_pieces, axis=1)))
        ]

        tables_at = jnp.concatenate([small_low, small_high], axis=0).reshape(dp_size, block_rows, tensor_size * BLOCK)
        vector_rows = tables_at[:, gate_rows:]
        natural = jnp.stack(from_places([tables_at[at] for at in range(dp_size)], dp_at), axis=0)
        gates = natural[:, :gate_rows].reshape(dp_size, 2, local_blocks, sub, tensor_size, BLOCK)
        gates = gates.transpose(1, 4, 2, 0, 3, 5).reshape(2, tensor_size * local_blocks, BLOCK, BLOCK)
        rgates, igates = gates[0], gates[1]
        flat_all = natural[:, gate_rows:].reshape(dp_size, -1, tensor_size, BLOCK).transpose(0, 2, 1, 3)
        flat_all = flat_all.reshape(dp_size, tensor_size, -1)
        count = 2 * CONV * local_blocks * sub
        table = flat_all[:, :, :count].reshape(dp_size, tensor_size, 2 * CONV, local_blocks, sub)
        table = table.transpose(2, 1, 3, 0, 4).reshape(2 * CONV, tensor_size * chunk).astype(f32)
        decay_rates = table[7]
        table = jnp.concatenate([table[:7], -8.0 * jax.nn.softplus(-decay_rates)[None]], axis=0)
        gain_rows = vector_rows[:, :, :BLOCK].reshape(dp_size, -1)[:, count : count + 2 * block_rows]
        gains = gain_rows.reshape(dp_size, 2, block_rows).transpose(1, 0, 2).reshape(2, model).astype(f32)

        def reorder(values, mover):
            return jnp.concatenate(mover(split_lanes(values, dp_size), dp_at), axis=1)

        hidden_all = reorder(jnp.concatenate([first_rows, hidden_in], axis=0), to_places).astype(f32)
        cot_low = reorder(cotangent, to_places)
        unit_all, scale_all = rms_parts(hidden_all)
        residual = hidden_all[HALO:]
        unit_one, scale_one = unit_all[HALO:], scale_all[HALO:]
        normed_one = (unit_all * gains[0]).astype(bf16)
        normed_one_t = normed_one.T
        cot_t = cot_low.T

        full = length + HALO
        fed = []
        for pair in range(pairs):
            low, high = in_pairs[pair]
            blocks = slice(2 * pair * local_blocks, 2 * (pair + 1) * local_blocks)
            lanes = slice(pair * pair_width, (pair + 1) * pair_width)
            fed.append(
                call(
                    mix_in_kernel,
                    groups,
                    [fixed((full, model)), lanes_of(half), lanes_of(half), blocks_of(), blocks_of(), lanes_of(8)],
                    [lanes_of(full)] + [lanes_of(length)] * 5,
                    [shaped(full, pair_width)] + [shaped(length, pair_width)] * 5,
                    [pltpu.VMEM((length, GROUP), bf16)] + [pltpu.VMEM((length, GROUP), f32)] * 3,
                )(normed_one, low, high, rgates[blocks], igates[blocks], table[:, lanes])
            )

        def exchange(products, ends, later):
            mine = jnp.concatenate([products, ends], axis=0)
            found = [mine]
            for other in range(1, tensor_size):
                pieces = split_lanes(swap_tensor(mine, other), tensor_size)
                found.append(jnp.concatenate([pieces[at ^ other] for at in range(tensor_size)], axis=1))
            found = relative(found, tensor_at, tensor_places)
            state = jnp.zeros_like(ends)
            turn = range(tensor_size - 1, 0, -1) if later else range(tensor_size - 1)
            for at in turn:
                use = (at > tensor_at) if later else (at < tensor_at)
                state = jnp.where(use, found[at][0:1] * state + found[at][1:2], state)
            return state

        enter = exchange(
            jnp.concatenate([one[5][length - 1 :] for one in fed], axis=1),
            jnp.concatenate([one[4][length - 1 :] for one in fed], axis=1),
            False,
        )
        middle = residual
        mixed = []
        for pair in range(pairs):
            low, high = out_pairs[pair]
            lanes = slice(pair * pair_width, (pair + 1) * pair_width)
            gate_pre, states, mixed_low, middle = call(
                mix_out_kernel,
                groups,
                [fixed((full, model)), lanes_of(half, 2 * GROUP), lanes_of(half, 2 * GROUP), lanes_of(length), lanes_of(length), lanes_of(1), fixed((length, model))],
                [lanes_of(length), lanes_of(length + 8), lanes_of(length), fixed((length, model))],
                [shaped(length, pair_width), shaped(length + 8, pair_width), shaped(length, pair_width, kind=bf16), shaped(length, model)],
                [],
            )(normed_one, low, high, fed[pair][4], fed[pair][5], enter[:, lanes], middle)
            mixed.append((gate_pre, states, mixed_low))

        unit_two, scale_two = rms_parts(middle)
        normed_two = (unit_two * gains[1]).astype(bf16)
        normed_two_t = normed_two.T

        total = middle
        normed_grad = jnp.zeros((length, model), f32)
        chunk_grads = []
        whole = fixed((length, model))
        turned = fixed((model, length))
        for low, high in mlp_chunks:
            total, normed_grad, low_grad, high_grad = call(
                mlp_kernel,
                mlp_groups,
                [whole, turned, whole, turned, lanes_of(half, 3 * GROUP), lanes_of(half, 3 * GROUP), whole, whole],
                [whole, whole, lanes_of(half, 3 * GROUP), lanes_of(half, 3 * GROUP)],
                [shaped(length, model), shaped(length, model), shaped(half, 3 * hidden_chunk, kind=bf16), shaped(half, 3 * hidden_chunk, kind=bf16)],
                [pltpu.VMEM((length, 2 * GROUP), f32), pltpu.VMEM((length, GROUP), bf16), pltpu.VMEM((length, 2 * GROUP), bf16), pltpu.VMEM((length, GROUP), f32)],
            )(normed_two, normed_two_t, cot_low, cot_t, low, high, total, normed_grad)
            chunk_grads.append((low_grad, high_grad))
        hidden_out = reorder(total.astype(bf16), from_places)

        scaled_two = normed_grad * gains[1]
        gain_two_part = jnp.sum(normed_grad * unit_two, axis=0)
        middle_grad = cot_low.astype(f32) + scale_two * (
            scaled_two - unit_two * jnp.mean(scaled_two * unit_two, axis=1, keepdims=True)
        )
        middle_low = middle_grad.astype(bf16)
        middle_low_t = middle_low.T

        def join_tensor(parts):
            for bit in reversed([bit for bit, _ in tensor_places]):
                received = split_lanes(swap_tensor(jnp.concatenate(parts[bit:], axis=1), bit), bit)
                last = bit == 1
                parts = [
                    (one.astype(f32) + two.astype(f32)) if last else add(one, two)
                    for one, two in zip(parts[:bit], received)
                ]
            return parts[0]

        mlp_sum = join_tensor(
            [
                scatter_dp(low_grad, high_grad, order_one if at % 2 == 0 else order_two, block_rows)
                for at, (low_grad, high_grad) in enumerate(chunk_grads)
            ]
        )
        mlp_grads = [
            jnp.concatenate(
                [mlp_sum[:, (3 * at + which) * GROUP : (3 * at + which + 1) * GROUP] for at in range(mlp_groups)], axis=1
            )
            for which in range(3)
        ]

        normed_grad = jnp.zeros((length, model), f32)
        backs = []
        out_grads = []
        for pair in range(pairs):
            low, high = out_pairs[pair]
            gate_pre, states, mixed_low = mixed[pair]
            lanes = slice(pair * pair_width, (pair + 1) * pair_width)
            normed_grad, local, product, edge, low_grad, high_grad = call(
                mix_back_kernel,
                groups,
                [whole, turned, fixed((model, full)), lanes_of(half, 2 * GROUP), lanes_of(half, 2 * GROUP), lanes_of(length), lanes_of(length + 8), lanes_of(length), lanes_of(length), lanes_of(8), whole],
                [whole, lanes_of(length), lanes_of(length), lanes_of(8), lanes_of(half, 2 * GROUP), lanes_of(half, 2 * GROUP)],
                [shaped(length, model), shaped(length, pair_width), shaped(length, pair_width), shaped(8, pair_width), shaped(half, 2 * pair_width, kind=bf16), shaped(half, 2 * pair_width, kind=bf16)],
                [pltpu.VMEM((length, GROUP), f32), pltpu.VMEM((length, GROUP), f32), pltpu.VMEM((length, GROUP), bf16), pltpu.VMEM((length + 8, GROUP), f32)],
            )(middle_low, middle_low_t, normed_one_t, low, high, gate_pre, states, mixed_low, fed[pair][2], table[:, lanes], normed_grad)
            backs.append((local, product, edge))
            out_grads.append((low_grad, high_grad))

        def separate(values):
            gate = [values[:, 2 * at * GROUP : (2 * at + 1) * GROUP] for at in range(groups)]
            out = [values[:, (2 * at + 1) * GROUP : (2 * at + 2) * GROUP] for at in range(groups)]
            gate, out = jnp.concatenate(gate, axis=1), jnp.concatenate(out, axis=1)
            return [jnp.concatenate([gate[:, :chunk], out[:, :chunk]], axis=1), jnp.concatenate([gate[:, chunk:], out[:, chunk:]], axis=1)]

        parts = []
        for pair, (low_grad, high_grad) in enumerate(out_grads):
            parts += separate(scatter_dp(low_grad, high_grad, order_one if pair % 2 == 0 else order_two, block_rows))
        out_sum = join_tensor(parts)

        leave = exchange(
            jnp.concatenate([one[2][1:2] for one in backs], axis=1),
            jnp.concatenate([one[2][0:1] for one in backs], axis=1),
            True,
        )
        gate_backs = []
        for pair in range(pairs):
            blocks = slice(2 * pair * local_blocks, 2 * (pair + 1) * local_blocks)
            lanes = slice(pair * pair_width, (pair + 1) * pair_width)
            branch, conv_out, recur_open, inflow = fed[pair][:4]
            local, product, _ = backs[pair]
            gate_backs.append(
                call(
                    gate_back_kernel,
                    groups,
                    [lanes_of(length), lanes_of(length), lanes_of(1), lanes_of(length + 8)] + [lanes_of(length)] * 3 + [lanes_of(full), blocks_of(), blocks_of(), lanes_of(8)],
                    [lanes_of(length), blocks_of(), blocks_of(), lanes_of(8)],
                    [shaped(length, pair_width), shaped(2 * local_blocks, BLOCK, BLOCK), shaped(2 * local_blocks, BLOCK, BLOCK), shaped(8, pair_width)],
                    [pltpu.VMEM((length, GROUP), bf16)] * 3,
                )(local, product, leave[:, lanes], mixed[pair][1], recur_open, inflow, conv_out, branch, rgates[blocks], igates[blocks], table[:, lanes])
            )
        heads = jnp.concatenate([one[0][:8] for one in gate_backs], axis=1)
        heads = jnp.concatenate(relative(split_lanes(heads, tensor_size), tensor_at, tensor_places), axis=1)
        heads = lax.ppermute(heads, "tensor", [(at + 1, at) for at in range(tensor_size - 1)])
        after = jnp.concatenate(relative(split_lanes(heads, tensor_size), tensor_at, tensor_places), axis=1)
        parts = []
        for pair in range(pairs):
            low, high = in_pairs[pair]
            lanes = slice(pair * pair_width, (pair + 1) * pair_width)
            normed_grad, low_grad, high_grad = call(
                branch_back_kernel,
                groups,
                [lanes_of(length), lanes_of(8), lanes_of(8), fixed((model, full)), lanes_of(half), lanes_of(half), whole],
                [whole, lanes_of(half), lanes_of(half)],
                [shaped(length, model), shaped(half, pair_width, kind=bf16), shaped(half, pair_width, kind=bf16)],
                [pltpu.VMEM((length + 8, GROUP), f32), pltpu.VMEM((length, GROUP), bf16)],
            )(gate_backs[pair][0], after[:, lanes], table[:, lanes], normed_one_t, low, high, normed_grad)
            parts += split_lanes(scatter_dp(low_grad, high_grad, order_one if pair % 2 == 0 else order_two, block_rows), 2)
        in_sum = join_tensor(parts)

        scaled_one = normed_grad * gains[0]
        gain_one_part = jnp.sum(normed_grad * unit_one, axis=0)
        hidden_grad = middle_grad + scale_one * (
            scaled_one - unit_one * jnp.mean(scaled_one * unit_one, axis=1, keepdims=True)
        )
        hidden_grad = reorder(hidden_grad, from_places)

        rgrads = jnp.concatenate([one[1] for one in gate_backs], axis=0)
        igrads = jnp.concatenate([one[2] for one in gate_backs], axis=0)
        gate_grads = jnp.stack([rgrads, igrads], axis=0).reshape(2, tensor_size, local_blocks, dp_size, sub, BLOCK)
        gate_grads = gate_grads.transpose(3, 0, 2, 4, 1, 5).reshape(dp_size, gate_rows, tensor_size * BLOCK)
        sums = jnp.concatenate([one[3] for one in gate_backs], axis=1)
        decay_row = sums[3:4] * (8.0 * jax.nn.sigmoid(-decay_rates))[None]
        sums = jnp.concatenate([sums[4:8], sums[0:3], decay_row], axis=0)
        sums = sums.reshape(2 * CONV, tensor_size, local_blocks, dp_size, sub).transpose(3, 1, 0, 2, 4)
        sums = sums.reshape(dp_size, tensor_size, count)
        gate_grads = jnp.stack(to_places([gate_grads[at] for at in range(dp_size)], dp_at), axis=0)
        sums = jnp.stack(to_places([sums[at] for at in range(dp_size)], dp_at), axis=0)
        gain_parts = jnp.stack([gain_one_part, gain_two_part], axis=0).reshape(2, dp_size, tensor_size, -1)
        gain_parts = jnp.stack(relative([gain_parts[:, :, at] for at in range(tensor_size)], tensor_at, tensor_places), axis=0)
        gain_parts = gain_parts.transpose(2, 0, 1, 3).reshape(dp_size, tensor_size, -1)
        flat = jnp.concatenate([sums, gain_parts], axis=2)
        flat = jnp.pad(flat, ((0, 0), (0, 0), (0, (block_rows - gate_rows) * BLOCK - flat.shape[2])))
        flat = flat.reshape(dp_size, tensor_size, -1, BLOCK).transpose(0, 2, 1, 3).reshape(dp_size, -1, tensor_size * BLOCK)
        small_grads = jnp.concatenate([gate_grads, flat], axis=1).reshape(model, tensor_size * BLOCK).astype(bf16)
        small_sum = scatter_dp(small_grads[:half], small_grads[half:], order_one, block_rows)
        small_sum = join_tensor(split_lanes(small_sum, tensor_size))
        gate_sum = small_sum[:gate_rows].reshape(2, local_blocks, sub, BLOCK).transpose(0, 2, 1, 3)
        flat_sum = small_sum[gate_rows:].reshape(-1)
        vector_sum = flat_sum[:count].reshape(2 * CONV, local_blocks, sub)
        gain_sum = flat_sum[count : count + 2 * block_rows // tensor_size].reshape(2, -1).T

        return (
            hidden_out,
            hidden_grad,
            gain_sum,
            in_sum,
            out_sum[:, :chunk],
            out_sum[:, chunk:],
            gate_sum[1],
            gate_sum[0],
            vector_sum[:CONV].transpose(2, 0, 1),
            vector_sum[4].T,
            vector_sum[5].T,
            vector_sum[6].T,
            vector_sum[7].T,
            mlp_grads[0],
            mlp_grads[1],
            mlp_grads[2],
        )

    return per_device


def solution(mesh):
    rows = P(("dp", "tensor"), None)
    matrix = P("dp", "tensor")
    gate = P("dp", "tensor", None)
    kernel = P("dp", None, "tensor")
    placed = (rows, rows, P("dp", None), matrix, matrix, matrix, gate, gate, kernel) + (matrix,) * 7
    made = (rows, rows, rows, matrix, matrix, matrix, gate, gate, kernel) + (matrix,) * 7
    return jax.shard_map(
        make_per_device(mesh.shape["dp"], mesh.shape["tensor"]),
        mesh=mesh,
        in_specs=placed,
        out_specs=made,
        check_vma=False,
    )
```

```python
import jax
import jax.numpy as jnp
from jax import lax
from jax.experimental import pallas as pl
from jax.experimental.pallas import tpu as pltpu
from jax.sharding import PartitionSpec as P

BLOCK = 128
CONV = 4
HALO = 16
TILE = 64
GROUP = 256
epsilon = 1e-06
f32 = jnp.float32
bf16 = jnp.bfloat16
ROOT = 0.7978845608028654
CUBIC = 0.044715


def nn(left, right):
    return lax.dot_general(left, right, (((1,), (0,)), ((), ())), preferred_element_type=f32)


def nt(left, right):
    return lax.dot_general(left, right, (((1,), (1,)), ((), ())), preferred_element_type=f32)


def tn(left, right):
    return lax.dot_general(left, right, (((0,), (0,)), ((), ())), preferred_element_type=f32)


def gelu_parts(value):
    square = value * value
    curve = jnp.tanh(ROOT * value * (1.0 + CUBIC * square))
    half = 0.5 * (1.0 + curve)
    slope = half + (0.5 * ROOT) * value * (1.0 - curve * curve) * (1.0 + 3.0 * CUBIC * square)
    return value * half, slope


def one_minus_exp(value):
    series = 1.0 + value * (1.0 / 7.0)
    for term in (6.0, 5.0, 4.0, 3.0, 2.0):
        series = 1.0 + value * (1.0 / term) * series
    return jnp.where(value > -0.25, -value * series, 1.0 - jnp.exp(value))


def scan_rows(decay_ref, drive_ref, offset, out_ref, out_offset, total_ref, length, reverse):
    width = drive_ref.shape[1]
    rows = lax.broadcasted_iota(jnp.int32, (8, width), 0)
    steps = length // 8

    def body(step, carry):
        state, product = carry
        at = (steps - 1 - step) if reverse else step
        start = pl.multiple_of(at * 8, 8)
        decay = decay_ref[pl.ds(start, 8 + 8 * (offset > 0)), :][offset : offset + 8]
        drive = drive_ref[pl.ds(start, 8), :]
        for shift in (1, 2, 4):
            if reverse:
                inside = rows < 8 - shift
                amount = 8 - shift
            else:
                inside = rows >= shift
                amount = shift
            drive = drive + decay * jnp.where(inside, pltpu.roll(drive, amount, 0), 0.0)
            decay = decay * jnp.where(inside, pltpu.roll(decay, amount, 0), 1.0)
        state = drive + decay * state
        product = decay * product
        out_ref[pl.ds(start + out_offset, 8), :] = state
        total_ref[pl.ds(start, 8), :] = product
        edge = 0 if reverse else 7
        return (
            jnp.broadcast_to(state[edge : edge + 1], (8, width)),
            jnp.broadcast_to(product[edge : edge + 1], (8, width)),
        )

    lax.fori_loop(0, steps, body, (jnp.zeros((8, width), f32), jnp.ones((8, width), f32)))


def tiles(length, body):
    def step(index, carry):
        body(pl.multiple_of(index * TILE, TILE))
        return carry

    lax.fori_loop(0, length // TILE, step, 0)


def mix_in_kernel(
    normed_ref, low_ref, high_ref, rgate_ref, igate_ref, table_ref,
    branch_ref, conv_ref, open_ref, flow_ref, local_ref, product_ref,
    conv_low, rec_buf, inp_buf, decay_buf,
):
    length = conv_ref.shape[0]
    half = low_ref.shape[0]
    branch_ref[...] = nn(normed_ref[:, :half], low_ref[...]) + nn(normed_ref[:, half:], high_ref[...])
    for part in range(GROUP // BLOCK):
        lanes = slice(part * BLOCK, (part + 1) * BLOCK)

        def convolve(start):
            window = branch_ref[pl.ds(start + HALO - 8, TILE + 8), lanes]
            result = table_ref[4:5, lanes] + table_ref[0:1, lanes] * window[8:]
            for offset in range(1, CONV):
                result = result + table_ref[offset : offset + 1, lanes] * window[8 - offset : 8 - offset + TILE]
            conv_ref[pl.ds(start, TILE), lanes] = result
            conv_low[pl.ds(start, TILE), lanes] = result.astype(bf16)

        tiles(length, convolve)
        rec_buf[:, lanes] = nn(conv_low[:, lanes], rgate_ref[part])
        inp_buf[:, lanes] = nn(conv_low[:, lanes], igate_ref[part])

        def gates(start):
            rows = pl.ds(start, TILE)
            recur_open = jax.nn.sigmoid(rec_buf[rows, lanes] + table_ref[6:7, lanes])
            inflow = jax.nn.sigmoid(inp_buf[rows, lanes] + table_ref[5:6, lanes])
            log_decay = recur_open * table_ref[7:8, lanes]
            multiplier = jnp.sqrt(one_minus_exp(2.0 * log_decay))
            open_ref[rows, lanes] = recur_open
            flow_ref[rows, lanes] = inflow
            decay_buf[rows, lanes] = jnp.exp(log_decay)
            rec_buf[rows, lanes] = multiplier * inflow * conv_ref[rows, lanes]

        tiles(length, gates)
    scan_rows(decay_buf, rec_buf, 0, local_ref, 0, product_ref, length, False)


def mix_out_kernel(
    normed_ref, low_ref, high_ref, local_ref, product_ref, enter_ref, sum_ref,
    pre_ref, states_ref, mixed_ref, total_ref,
):
    length = local_ref.shape[0]
    half = low_ref.shape[0]

    @pl.when(pl.program_id(0) == 0)
    def _():
        total_ref[...] = sum_ref[...]

    pre_ref[...] = nn(normed_ref[HALO:, :half], low_ref[:, :GROUP]) + nn(normed_ref[HALO:, half:], high_ref[:, :GROUP])
    states_ref[0:8, :] = jnp.broadcast_to(enter_ref[0:1, :], (8, GROUP))
    for part in range(GROUP // BLOCK):
        lanes = slice(part * BLOCK, (part + 1) * BLOCK)

        def mix(start):
            rows = pl.ds(start, TILE)
            states = local_ref[rows, lanes] + product_ref[rows, lanes] * enter_ref[0:1, lanes]
            states_ref[pl.ds(start + 8, TILE), lanes] = states
            gate = pre_ref[rows, lanes]
            curve = jnp.tanh(ROOT * gate * (1.0 + CUBIC * gate * gate))
            mixed_ref[rows, lanes] = (states * (gate * (0.5 * (1.0 + curve)))).astype(bf16)

        tiles(length, mix)
    total_ref[:, :half] += nt(mixed_ref[...], low_ref[:, GROUP:])
    total_ref[:, half:] += nt(mixed_ref[...], high_ref[:, GROUP:])


def mlp_kernel(
    normed_ref, normed_t_ref, cot_ref, cot_t_ref, low_ref, high_ref, sum_ref, back_ref,
    total_ref, grad_ref, low_grad_ref, high_grad_ref,
    pre, hidden, pre_low, act, first=False,
):
    length = normed_ref.shape[0]
    half = low_ref.shape[0]

    @pl.when(pl.program_id(0) == 0)
    def _():
        if first:
            total_ref[...] = jnp.zeros_like(total_ref)
            grad_ref[...] = jnp.zeros_like(grad_ref)
        else:
            total_ref[...] = sum_ref[...]
            grad_ref[...] = back_ref[...]

    pre[...] = nn(normed_ref[:, :half], low_ref[:, : 2 * GROUP]) + nn(normed_ref[:, half:], high_ref[:, : 2 * GROUP])
    act[...] = nn(cot_ref[:, :half], low_ref[:, 2 * GROUP :]) + nn(cot_ref[:, half:], high_ref[:, 2 * GROUP :])
    for part in range(GROUP // BLOCK):
        lanes = slice(part * BLOCK, (part + 1) * BLOCK)
        up_lanes = slice(GROUP + part * BLOCK, GROUP + (part + 1) * BLOCK)

        def activate(start):
            rows = pl.ds(start, TILE)
            value, slope = gelu_parts(pre[rows, lanes])
            up = pre[rows, up_lanes]
            grad = act[rows, lanes]
            hidden[rows, lanes] = (value * up).astype(bf16)
            pre_low[rows, lanes] = (grad * up * slope).astype(bf16)
            pre_low[rows, up_lanes] = (grad * value).astype(bf16)

        tiles(length, activate)
    total_ref[:, :half] += nt(hidden[...], low_ref[:, 2 * GROUP :])
    total_ref[:, half:] += nt(hidden[...], high_ref[:, 2 * GROUP :])
    grad_ref[:, :half] += nt(pre_low[...], low_ref[:, : 2 * GROUP])
    grad_ref[:, half:] += nt(pre_low[...], high_ref[:, : 2 * GROUP])
    low_grad_ref[:, : 2 * GROUP] = nn(normed_t_ref[:half], pre_low[...]).astype(bf16)
    high_grad_ref[:, : 2 * GROUP] = nn(normed_t_ref[half:], pre_low[...]).astype(bf16)
    low_grad_ref[:, 2 * GROUP :] = nn(cot_t_ref[:half], hidden[...]).astype(bf16)
    high_grad_ref[:, 2 * GROUP :] = nn(cot_t_ref[half:], hidden[...]).astype(bf16)


def lane_block(index):
    return pl.ds(pl.multiple_of(index * BLOCK, BLOCK), BLOCK)


def order_kernel(places_ref, hidden_ref, cot_ref, hidden_out_ref, cot_out_ref, cot_t_ref):
    for place in range(hidden_ref.shape[1] // BLOCK):
        lanes = slice(place * BLOCK, (place + 1) * BLOCK)
        hidden_out_ref[:, lanes] = hidden_ref[:, lane_block(places_ref[place])]
        cot_out_ref[:, lanes] = cot_ref[:, lane_block(places_ref[place])]
    cot_t_ref[...] = cot_out_ref[...].T


def row_loop(length, rows, body, start):
    def step(index, carry):
        return body(pl.ds(pl.multiple_of(index * rows, rows), rows), carry)

    return lax.fori_loop(0, length // rows, step, start)


def scale_of(values):
    return lax.rsqrt(jnp.mean(values * values, axis=1, keepdims=True) + epsilon)


def norm_kernel(places_ref, hidden_ref, first_ref, gains_ref, normed_ref, normed_t_ref, first_buf):
    length = hidden_ref.shape[0]
    for place in range(hidden_ref.shape[1] // BLOCK):
        lanes = slice(place * BLOCK, (place + 1) * BLOCK)
        first_buf[:, lanes] = first_ref[:, lane_block(places_ref[place])].astype(f32)
    first = first_buf[...]
    normed_ref[:HALO, :] = (first * scale_of(first) * gains_ref[0:1, :]).astype(bf16)

    def body(rows, carry):
        values = hidden_ref[rows, :].astype(f32)
        normed_ref[pl.ds(rows.start + HALO, rows.size), :] = (values * scale_of(values) * gains_ref[0:1, :]).astype(bf16)
        return carry

    row_loop(length, 16, body, 0)
    normed_t_ref[...] = normed_ref[HALO:, :].T


def second_norm_kernel(middle_ref, gains_ref, normed_ref, normed_t_ref):
    def body(rows, carry):
        values = middle_ref[rows, :]
        normed_ref[rows, :] = (values * scale_of(values) * gains_ref[1:2, :]).astype(bf16)
        return carry

    row_loop(middle_ref.shape[0], 16, body, 0)
    normed_t_ref[...] = normed_ref[...].T


def norm_back(values, grad, gain):
    scale = scale_of(values)
    unit = values * scale
    scaled = grad * gain
    return scale * (scaled - unit * jnp.mean(scaled * unit, axis=1, keepdims=True)), grad * unit


def fold_rows(value):
    rows, width = value.shape
    return jnp.sum(value.reshape(rows // 8, 8, width), axis=0)


def middle_kernel(
    places_ref, middle_ref, total_ref, grad_ref, cot_ref, gains_ref,
    out_ref, middle_grad_ref, low_ref, low_t_ref, gain_ref, buffer,
):
    length, model = middle_ref.shape

    def body(rows, carry):
        middle = middle_ref[rows, :]
        change, part = norm_back(middle, grad_ref[rows, :], gains_ref[1:2, :])
        middle_grad = cot_ref[rows, :].astype(f32) + change
        middle_grad_ref[rows, :] = middle_grad
        low_ref[rows, :] = middle_grad.astype(bf16)
        buffer[rows, :] = (middle + total_ref[rows, :]).astype(bf16)
        return carry + fold_rows(part)

    total = row_loop(length, 16, body, jnp.zeros((8, model), f32))
    gain_ref[...] = jnp.sum(total, axis=0, keepdims=True)
    low_t_ref[...] = low_ref[...].T
    for place in range(model // BLOCK):
        out_ref[:, lane_block(places_ref[place])] = buffer[:, place * BLOCK : (place + 1) * BLOCK]


def final_kernel(places_ref, hidden_ref, grad_ref, middle_grad_ref, gains_ref, out_ref, gain_ref, buffer):
    length, model = hidden_ref.shape

    def body(rows, carry):
        change, part = norm_back(hidden_ref[rows, :].astype(f32), grad_ref[rows, :], gains_ref[0:1, :])
        buffer[rows, :] = middle_grad_ref[rows, :] + change
        return carry + fold_rows(part)

    total = row_loop(length, 16, body, jnp.zeros((8, model), f32))
    gain_ref[...] = jnp.sum(total, axis=0, keepdims=True)
    for place in range(model // BLOCK):
        out_ref[:, lane_block(places_ref[place])] = buffer[:, place * BLOCK : (place + 1) * BLOCK]


def tables_kernel(places_ref, low_ref, high_ref, rgate_ref, igate_ref, table_ref, gains_ref, *, sub, local_blocks, chunks):
    rows_each = 2 * local_blocks * sub
    kinds = 2 * CONV
    count = places_ref.shape[0]
    size = low_ref.shape[0] * 2 // count
    sums = [jnp.zeros((kinds * local_blocks, BLOCK), f32)] * chunks
    for place in range(count):
        source = low_ref if place < count // 2 else high_ref
        top = (place % (count // 2)) * size
        natural = places_ref[place]
        for at in range(chunks):
            lanes = slice(at * BLOCK, (at + 1) * BLOCK)
            for which, gate_ref in enumerate((rgate_ref, igate_ref)):
                for block in range(local_blocks):
                    start = top + (which * local_blocks + block) * sub
                    gate_ref[at * local_blocks + block, pl.ds(pl.multiple_of(natural * sub, sub), sub), :] = source[start : start + sub, lanes]
            sums[at] = sums[at] + source[top + rows_each : top + rows_each + kinds * local_blocks, lanes].astype(f32)
        start = top + rows_each + kinds * local_blocks
        gains_ref[:, place * BLOCK : (place + 1) * BLOCK] = source[start : start + 2, :BLOCK].astype(f32)
    for at in range(chunks):
        for block in range(local_blocks):
            column = (at * local_blocks + block) * BLOCK
            for kind in range(kinds):
                row = kind * local_blocks + block
                table_ref[kind : kind + 1, column : column + BLOCK] = sums[at][row : row + 1]


def small_grads_kernel(places_ref, rgrad_ref, igrad_ref, sums_ref, gains_ref, low_ref, high_ref, *, sub, local_blocks, chunks):
    kinds = 2 * CONV
    rows_each = 2 * local_blocks * sub
    count = places_ref.shape[0]
    size = low_ref.shape[0] * 2 // count
    spare = size - rows_each - kinds * local_blocks - 2
    vectors = []
    for at in range(chunks):
        rows = []
        for kind in range(kinds):
            for block in range(local_blocks):
                column = (at * local_blocks + block) * BLOCK
                rows.append(sums_ref[kind : kind + 1, column : column + BLOCK])
        vectors.append(jnp.concatenate(rows, axis=0))
    for place in range(count):
        target = low_ref if place < count // 2 else high_ref
        top = (place % (count // 2)) * size
        natural = places_ref[place]
        gains = gains_ref[:, place * BLOCK : (place + 1) * BLOCK]
        for at in range(chunks):
            lanes = slice(at * BLOCK, (at + 1) * BLOCK)
            for which, grad_ref in enumerate((rgrad_ref, igrad_ref)):
                for block in range(local_blocks):
                    start = top + (which * local_blocks + block) * sub
                    target[start : start + sub, lanes] = grad_ref[
                        at * local_blocks + block, pl.ds(pl.multiple_of(natural * sub, sub), sub), :
                    ].astype(bf16)
            rest = jnp.concatenate([vectors[at], gains, jnp.zeros((spare, BLOCK), f32)], axis=0)
            target[top + rows_each : top + size, lanes] = rest.astype(bf16)


def mix_back_kernel(
    grad_low_ref, grad_t_ref, normed_t_ref, low_ref, high_ref, pre_ref, states_ref, mixed_ref, open_ref, table_ref, sum_ref,
    total_ref, local_ref, product_ref, edge_ref, low_grad_ref, high_grad_ref,
    mixed_grad, drive, pre_low, decay_buf,
):
    length = pre_ref.shape[0]
    half = low_ref.shape[0]

    @pl.when(pl.program_id(0) == 0)
    def _():
        total_ref[...] = sum_ref[...]

    mixed_grad[...] = nn(grad_low_ref[:, :half], low_ref[:, GROUP:]) + nn(grad_low_ref[:, half:], high_ref[:, GROUP:])
    decay_buf[pl.ds(length, 8), :] = jnp.ones((8, GROUP), f32)
    for part in range(GROUP // BLOCK):
        lanes = slice(part * BLOCK, (part + 1) * BLOCK)

        def back(start):
            rows = pl.ds(start, TILE)
            value, slope = gelu_parts(pre_ref[rows, lanes])
            grad = mixed_grad[rows, lanes]
            pre_low[rows, lanes] = (grad * states_ref[pl.ds(start + 8, TILE), lanes] * slope).astype(bf16)
            drive[rows, lanes] = grad * value
            decay_buf[rows, lanes] = jnp.exp(open_ref[rows, lanes] * table_ref[7:8, lanes])

        tiles(length, back)
    scan_rows(decay_buf, drive, 1, local_ref, 0, product_ref, length, True)
    edge_ref[0:1, :] = decay_buf[0:1, :] * local_ref[0:1, :]
    edge_ref[1:2, :] = decay_buf[0:1, :] * product_ref[0:1, :]
    total_ref[:, :half] += nt(pre_low[...], low_ref[:, :GROUP])
    total_ref[:, half:] += nt(pre_low[...], high_ref[:, :GROUP])
    low_grad_ref[:, :GROUP] = nn(normed_t_ref[:half], pre_low[...]).astype(bf16)
    high_grad_ref[:, :GROUP] = nn(normed_t_ref[half:], pre_low[...]).astype(bf16)
    low_grad_ref[:, GROUP:] = nn(grad_t_ref[:half], mixed_ref[...]).astype(bf16)
    high_grad_ref[:, GROUP:] = nn(grad_t_ref[half:], mixed_ref[...]).astype(bf16)


def gate_back_kernel(
    local_ref, product_ref, enter_ref, states_ref, open_ref, flow_ref, conv_ref, branch_ref, rgate_ref, igate_ref, table_ref,
    conv_grad_ref, rgrad_ref, igrad_ref, sums_ref,
    rec_low, inp_low, conv_low,
):
    length = local_ref.shape[0]
    for part in range(GROUP // BLOCK):
        lanes = slice(part * BLOCK, (part + 1) * BLOCK)

        def back(index, sums):
            start = pl.multiple_of(index * TILE, TILE)
            rows = pl.ds(start, TILE)
            carried = local_ref[rows, lanes] + product_ref[rows, lanes] * enter_ref[0:1, lanes]
            recur_open = open_ref[rows, lanes]
            inflow = flow_ref[rows, lanes]
            conv_out = conv_ref[rows, lanes]
            rate = table_ref[7:8, lanes]
            log_decay = recur_open * rate
            decay = jnp.exp(log_decay)
            multiplier = jnp.sqrt(one_minus_exp(2.0 * log_decay))
            before = states_ref[pl.ds(start, TILE + 8), lanes][7 : 7 + TILE]
            weighted = carried * inflow
            decay_grad = carried * before * decay - weighted * conv_out * decay * decay / multiplier
            scaled = decay_grad * recur_open
            rec_grad = rate * scaled * (1.0 - recur_open)
            direct = weighted * multiplier
            inp_grad = direct * conv_out * (1.0 - inflow)
            rec_low[rows, lanes] = rec_grad.astype(bf16)
            inp_low[rows, lanes] = inp_grad.astype(bf16)
            conv_low[rows, lanes] = conv_out.astype(bf16)
            conv_grad_ref[rows, lanes] = direct

            def fold(value):
                return jnp.sum(value.reshape(TILE // 8, 8, BLOCK), axis=0)

            return (sums[0] + fold(rec_grad), sums[1] + fold(inp_grad), sums[2] + fold(scaled))

        zero = jnp.zeros((8, BLOCK), f32)
        sums = lax.fori_loop(0, length // TILE, back, (zero, zero, zero))
        for row, value in zip((2, 1, 3), sums):
            sums_ref[row : row + 1, lanes] = jnp.sum(value, axis=0, keepdims=True)
        rgrad_ref[part] = tn(conv_low[:, lanes], rec_low[:, lanes])
        igrad_ref[part] = tn(conv_low[:, lanes], inp_low[:, lanes])
        conv_grad_ref[:, lanes] += nt(rec_low[:, lanes], rgate_ref[part]) + nt(inp_low[:, lanes], igate_ref[part])

        def taps(index, sums):
            start = pl.multiple_of(index * TILE, TILE)
            grad = conv_grad_ref[pl.ds(start, TILE), lanes]

            def fold(value):
                return jnp.sum(value.reshape(TILE // 8, 8, BLOCK), axis=0)

            window = branch_ref[pl.ds(start + HALO - 8, TILE + 8), lanes]
            new = [sums[0] + fold(grad)]
            for offset in range(CONV):
                new.append(sums[offset + 1] + fold(grad * window[8 - offset : 8 - offset + TILE]))
            return tuple(new)

        sums = lax.fori_loop(0, length // TILE, taps, (zero,) * (CONV + 1))
        for row, value in zip((0, 4, 5, 6, 7), sums):
            sums_ref[row : row + 1, lanes] = jnp.sum(value, axis=0, keepdims=True)


def branch_back_kernel(
    conv_grad_ref, after_ref, table_ref, normed_t_ref, low_ref, high_ref, sum_ref,
    total_ref, low_grad_ref, high_grad_ref,
    padded, branch_low,
):
    length = conv_grad_ref.shape[0]
    half = low_ref.shape[0]

    @pl.when(pl.program_id(0) == 0)
    def _():
        total_ref[...] = sum_ref[...]

    padded[pl.ds(0, length), :] = conv_grad_ref[...]
    padded[pl.ds(length, 8), :] = after_ref[...]
    for part in range(GROUP // BLOCK):
        lanes = slice(part * BLOCK, (part + 1) * BLOCK)

        def back(start):
            window = padded[pl.ds(start, TILE + 8), lanes]
            result = table_ref[0:1, lanes] * window[:TILE]
            for offset in range(1, CONV):
                result = result + table_ref[offset : offset + 1, lanes] * window[offset : offset + TILE]
            branch_low[pl.ds(start, TILE), lanes] = result.astype(bf16)

        tiles(length, back)
    total_ref[:, :half] += nt(branch_low[...], low_ref[...])
    total_ref[:, half:] += nt(branch_low[...], high_ref[...])
    low_grad_ref[...] = nn(normed_t_ref[:half], branch_low[...]).astype(bf16)
    high_grad_ref[...] = nn(normed_t_ref[half:], branch_low[...]).astype(bf16)


def fixed(shape):
    return pl.BlockSpec(shape, lambda g: (0,) * len(shape))


def lanes_of(rows, width=GROUP):
    return pl.BlockSpec((rows, width), lambda g: (0, g))


def blocks_of():
    return pl.BlockSpec((GROUP // BLOCK, BLOCK, BLOCK), lambda g: (g, 0, 0))


def shaped(*dims, kind=f32):
    return jax.ShapeDtypeStruct(dims, kind)


PARAMS = pltpu.CompilerParams(dimension_semantics=("arbitrary",), vmem_limit_bytes=56 * 1024 * 1024)


ANYWHERE = pl.BlockSpec(memory_space=pl.ANY)
SCALARS = pl.BlockSpec(memory_space=pltpu.SMEM)


def call(kernel, steps, in_specs, out_specs, out_shape, scratch, hold=()):
    count = len(in_specs)

    def body(*refs):
        kernel(*refs[:count], *refs[count + len(hold) :])

    run = pl.pallas_call(
        body,
        grid=(steps,),
        in_specs=list(in_specs) + [ANYWHERE] * len(hold),
        out_specs=out_specs,
        out_shape=out_shape,
        scratch_shapes=scratch,
        compiler_params=PARAMS,
        name=getattr(kernel, "func", kernel).__name__,
    )
    return lambda *args: run(*args, *hold)


def make_per_device(dp_size, tensor_size):
    pairs = tensor_size // 2
    dp_bits = [1 << bit for bit in range(dp_size.bit_length() - 1)]
    order_one = dp_bits[1:] + dp_bits[:1]
    order_two = dp_bits[2:3] + dp_bits[1:2] + dp_bits[3:] + dp_bits[:1]
    orders = (order_one, order_two)
    position_of = {bit: place for place, bit in enumerate(order_one)}

    def swap_dp(values, bit):
        return lax.ppermute(values, "dp", [(at, at ^ bit) for at in range(dp_size)])

    def swap_tensor(values, bit):
        return lax.ppermute(values, "tensor", [(at, at ^ bit) for at in range(tensor_size)])

    def relative(pieces, index):
        bit = 1
        while bit < len(pieces):
            flag = (index & bit) != 0
            pieces = [jnp.where(flag, pieces[at ^ bit], piece) for at, piece in enumerate(pieces)]
            bit *= 2
        return pieces

    place_index = [
        sum(bit for bit in dp_bits if place & (1 << position_of[bit])) for place in range(dp_size)
    ]

    def split_lanes(values, count):
        width = values.shape[1] // count
        return [values[:, at * width : (at + 1) * width] for at in range(count)]

    def gather_dp(values, order):
        rows = values.shape[0]
        done, marks = [], []
        for bit in order[:-1]:
            received = swap_dp(values, bit)
            marks.append(received)
            low_place = position_of[bit]
            if all(position_of[other] < low_place for other in done):
                values = jnp.concatenate([values, received], axis=0)
            else:
                pieces = []
                for at in range(values.shape[0] // rows):
                    pieces += [values[at * rows : (at + 1) * rows], received[at * rows : (at + 1) * rows]]
                values = jnp.concatenate(pieces, axis=0)
            done.append(bit)
        last = swap_dp(values, order[-1])
        return values, last, marks + [last]

    def add(one, two):
        return (one.astype(f32) + two.astype(f32)).astype(bf16)

    def scatter_dp(own, other, order, block_rows):
        values = add(own, swap_dp(other, order[-1]))
        marks = [values]
        left = list(order[:-1])
        while left:
            bit = left.pop()
            place = position_of[bit]
            rows = values.shape[0]
            if all(position_of[o] < place for o in left):
                keep, send = values[: rows // 2], values[rows // 2 :]
            else:
                count = rows // block_rows
                take = lambda start: jnp.concatenate(
                    [values[at * block_rows : (at + 1) * block_rows] for at in range(start, count, 2)], axis=0
                )
                keep, send = take(0), take(1)
            values = add(keep, swap_dp(send, bit))
            marks.append(values)
        return values, marks

    def spread_tensor(values):
        return [values] + [swap_tensor(values, other) for other in range(1, tensor_size)]

    def join_tensor(parts):
        total = parts[0].astype(f32)
        received = []
        for other in range(1, tensor_size):
            received.append(swap_tensor(parts[other], other))
            total = total + received[-1].astype(f32)
        return total, received

    def per_device(
        hidden_in, cotangent, norm_gains, mixer_in, branch_gate, mixer_out, input_gate, recur_gate,
        conv_kernel, conv_bias, input_bias, recur_bias, decay_param, mlp_gate, mlp_up, mlp_down,
    ):
        dp_at = lax.axis_index("dp")
        tensor_at = lax.axis_index("tensor")
        length, model = hidden_in.shape
        block_rows, chunk = mixer_in.shape
        half = model // 2
        hidden_chunk = mlp_gate.shape[1]
        sub = block_rows * BLOCK // model
        local_blocks = chunk // BLOCK
        pair_width = 2 * chunk
        groups = pair_width // GROUP
        mlp_groups = hidden_chunk // GROUP
        fast = block_rows == BLOCK and sub % 16 == 0
        natural_at = jnp.array(place_index, jnp.int32) ^ dp_at
        places = natural_at if fast else jnp.arange(model // BLOCK, dtype=jnp.int32)

        def features(values, back=False):
            if fast:
                return values
            pieces = jnp.stack(split_lanes(values, dp_size), axis=0)
            order = natural_at
            if back:
                order = jnp.zeros_like(natural_at).at[natural_at].set(jnp.arange(dp_size, dtype=jnp.int32))
            return jnp.concatenate(list(jnp.take(pieces, order, axis=0)), axis=1)

        first_rows = lax.ppermute(
            hidden_in[length - HALO :], "tensor", [(at, at + 1) for at in range(tensor_size - 1)]
        )

        def rows_first(table):
            return table.transpose(1, 0, 2).reshape(-1, BLOCK)

        vectors = jnp.concatenate(
            [conv_kernel.transpose(1, 2, 0).reshape(-1, sub)]
            + [table.T for table in (conv_bias, input_bias, recur_bias, decay_param)],
            axis=0,
        )
        owner = lax.broadcasted_iota(jnp.int32, (1, BLOCK), 1) // sub
        vectors = jnp.where(owner == dp_at, jnp.tile(vectors, (1, BLOCK // sub)), jnp.zeros((), bf16))
        gate_rows = 2 * local_blocks * sub
        vector_rows = vectors.shape[0]
        small_rows = (gate_rows + vector_rows + 2 + 15) // 16 * 16
        small = jnp.concatenate(
            [
                rows_first(recur_gate),
                rows_first(input_gate),
                vectors,
                jnp.pad(norm_gains.T, ((0, 0), (0, BLOCK - block_rows))),
                jnp.zeros((small_rows - gate_rows - vector_rows - 2, BLOCK), bf16),
            ],
            axis=0,
        )
        small_low, small_high, _ = gather_dp(jnp.concatenate(spread_tensor(small), axis=1), order_one)

        def gather_pairs(values, arrange):
            found = spread_tensor(values)
            result = []
            for pair in range(pairs):
                packed = arrange(found[2 * pair], found[2 * pair + 1])
                result.append(gather_dp(packed, orders[pair % 2]))
            return result, found[1:]

        def interleave(one, two):
            gate = jnp.concatenate([one[:, :chunk], two[:, :chunk]], axis=1)
            out = jnp.concatenate([one[:, chunk:], two[:, chunk:]], axis=1)
            pieces = []
            for at in range(groups):
                pieces += [gate[:, at * GROUP : (at + 1) * GROUP], out[:, at * GROUP : (at + 1) * GROUP]]
            return jnp.concatenate(pieces, axis=1)

        in_pairs, in_far = gather_pairs(mixer_in, lambda one, two: jnp.concatenate([one, two], axis=1))
        out_pairs, out_far = gather_pairs(jnp.concatenate([branch_gate, mixer_out], axis=1), interleave)
        mlp_pieces = []
        for at in range(mlp_groups):
            mlp_pieces += [w[:, at * GROUP : (at + 1) * GROUP] for w in (mlp_gate, mlp_up, mlp_down)]
        mlp_near = spread_tensor(jnp.concatenate(mlp_pieces, axis=1))
        mlp_chunks = [gather_dp(values, orders[at % 2]) for at, values in enumerate(mlp_near)]

        whole = fixed((length, model))
        turned = fixed((model, length))
        hidden_low, cot_low, cot_t = call(
            order_kernel, 1, [SCALARS, whole, whole], [whole, whole, turned],
            [shaped(length, model, kind=bf16), shaped(length, model, kind=bf16), shaped(model, length, kind=bf16)], [],
        )(places, features(hidden_in), features(cotangent))

        kinds = 2 * CONV
        channels = tensor_size * chunk
        blocks = tensor_size * local_blocks
        if fast:
            small_spec = fixed((model // 2 // block_rows * small_rows, tensor_size * BLOCK))
            gate_spec = fixed((blocks, BLOCK, BLOCK))
            def tables_of(*args, **sizes):
                tables_kernel(*args, sub=sub, local_blocks=local_blocks, chunks=tensor_size)
            rgates, igates, table, gains = call(
                tables_of, 1, [SCALARS, small_spec, small_spec], [gate_spec, gate_spec, fixed((kinds, channels)), fixed((2, model))],
                [shaped(blocks, BLOCK, BLOCK, kind=bf16), shaped(blocks, BLOCK, BLOCK, kind=bf16), shaped(kinds, channels), shaped(2, model)], [],
                hold=out_far,
            )(places, small_low, small_high)
        else:
            stacked = jnp.concatenate([small_low, small_high], axis=0).reshape(dp_size, small_rows, -1)
            order = jnp.zeros_like(natural_at).at[natural_at].set(jnp.arange(dp_size, dtype=jnp.int32))
            gates = jnp.take(stacked[:, :gate_rows], order, axis=0).reshape(dp_size, 2, local_blocks, sub, tensor_size, BLOCK)
            gates = gates.transpose(1, 4, 2, 0, 3, 5).reshape(2, blocks, BLOCK, BLOCK)
            rgates, igates = gates[0], gates[1]
            table = jnp.sum(stacked[:, gate_rows : gate_rows + vector_rows].astype(f32), axis=0)
            table = table.reshape(kinds, local_blocks, tensor_size, BLOCK).transpose(0, 2, 1, 3).reshape(kinds, channels)
            gains = stacked[:, gate_rows + vector_rows : gate_rows + vector_rows + 2, :block_rows]
            gains = gains.transpose(1, 0, 2).reshape(2, model).astype(f32)
        decay_rates = table[7:8]
        table = jnp.concatenate([table[:7], -8.0 * jax.nn.softplus(-decay_rates)], axis=0)

        full = length + HALO
        normed_one, normed_one_t = call(
            norm_kernel, 1, [SCALARS, whole, fixed((HALO, model)), fixed((2, model))], [fixed((full, model)), turned],
            [shaped(full, model, kind=bf16), shaped(model, length, kind=bf16)], [pltpu.VMEM((HALO, model), f32)],
        )(places, hidden_low, features(first_rows), gains)

        fed = []
        fed_holds = [
            [out_pairs[0][2][0], out_pairs[1][2][0], mlp_near[1]],
            [out_pairs[0][2][1], out_pairs[1][2][1], mlp_near[2]],
        ]
        for pair in range(pairs):
            low, high, _ = in_pairs[pair]
            part = slice(2 * pair * local_blocks, 2 * (pair + 1) * local_blocks)
            lanes = slice(pair * pair_width, (pair + 1) * pair_width)
            fed.append(
                call(
                    mix_in_kernel,
                    groups,
                    [fixed((full, model)), lanes_of(half), lanes_of(half), blocks_of(), blocks_of(), lanes_of(8)],
                    [lanes_of(full)] + [lanes_of(length)] * 5,
                    [shaped(full, pair_width)] + [shaped(length, pair_width)] * 5,
                    [pltpu.VMEM((length, GROUP), bf16)] + [pltpu.VMEM((length, GROUP), f32)] * 3,
                    hold=fed_holds[pair],
                )(normed_one, low, high, rgates[part], igates[part], table[:, lanes])
            )

        def exchange(products, ends, later):
            mine = jnp.concatenate([products, ends], axis=0)
            found = [mine]
            for other in range(1, tensor_size):
                pieces = split_lanes(swap_tensor(mine, other), tensor_size)
                found.append(jnp.concatenate([pieces[at ^ other] for at in range(tensor_size)], axis=1))
            found = relative(found, tensor_at)
            state = jnp.zeros_like(ends)
            turn = range(tensor_size - 1, 0, -1) if later else range(tensor_size - 1)
            for at in turn:
                use = (at > tensor_at) if later else (at < tensor_at)
                state = jnp.where(use, found[at][0:1] * state + found[at][1:2], state)
            return state

        enter = exchange(
            jnp.concatenate([one[5][length - 1 :] for one in fed], axis=1),
            jnp.concatenate([one[4][length - 1 :] for one in fed], axis=1),
            False,
        )
        middle = hidden_low.astype(f32)
        mixed = []
        mixed_holds = [
            [mlp_chunks[0][2][0], mlp_chunks[1][2][0], mlp_near[3]],
            [mlp_chunks[0][2][1], mlp_chunks[1][2][1]],
        ]
        for pair in range(pairs):
            low, high, _ = out_pairs[pair]
            lanes = slice(pair * pair_width, (pair + 1) * pair_width)
            gate_pre, states, mixed_low, middle = call(
                mix_out_kernel,
                groups,
                [fixed((full, model)), lanes_of(half, 2 * GROUP), lanes_of(half, 2 * GROUP), lanes_of(length), lanes_of(length), lanes_of(1), whole],
                [lanes_of(length), lanes_of(length + 8), lanes_of(length), whole],
                [shaped(length, pair_width), shaped(length + 8, pair_width), shaped(length, pair_width, kind=bf16), shaped(length, model)],
                [],
                hold=mixed_holds[pair],
            )(normed_one, low, high, fed[pair][4], fed[pair][5], enter[:, lanes], middle)
            mixed.append((gate_pre, states, mixed_low))
        normed_two, normed_two_t = call(
            second_norm_kernel, 1, [whole, fixed((2, model))], [whole, turned],
            [shaped(length, model, kind=bf16), shaped(model, length, kind=bf16)], [],
        )(middle, gains)

        total = normed_grad = None
        moved = []
        sums = []
        for at, (low, high, _) in enumerate(mlp_chunks):
            holds = [
                [mlp_chunks[2][2][0], mlp_chunks[3][2][0]],
                [mlp_chunks[2][2][1]],
                [lambda: moved[0][1][0]],
                [lambda: moved[1][1][0]],
            ][at]
            holds = [hold() if callable(hold) else hold for hold in holds]
            before = [] if at == 0 else [total, normed_grad]
            width = 3 * GROUP

            def kernel(*refs, at=at):
                if at == 0:
                    mlp_kernel(*refs[:6], None, None, *refs[6:], first=True)
                else:
                    mlp_kernel(*refs)

            total, normed_grad, low_grad, high_grad = call(
                kernel,
                mlp_groups,
                [whole, turned, whole, turned, lanes_of(half, width), lanes_of(half, width)] + [whole] * len(before),
                [whole, whole, lanes_of(half, width), lanes_of(half, width)],
                [shaped(length, model), shaped(length, model), shaped(half, 3 * hidden_chunk, kind=bf16), shaped(half, 3 * hidden_chunk, kind=bf16)],
                [pltpu.VMEM((length, 2 * GROUP), f32), pltpu.VMEM((length, GROUP), bf16), pltpu.VMEM((length, 2 * GROUP), bf16), pltpu.VMEM((length, GROUP), f32)],
                hold=holds,
            )(normed_two, normed_two_t, cot_low, cot_t, low, high, *before)
            moved.append(scatter_dp(low_grad, high_grad, orders[at % 2], block_rows))
        mlp_sum, mlp_far = join_tensor([one[0] for one in moved])
        mlp_grads = [
            jnp.concatenate(
                [mlp_sum[:, (3 * at + which) * GROUP : (3 * at + which + 1) * GROUP] for at in range(mlp_groups)], axis=1
            )
            for which in range(3)
        ]

        hidden_out, middle_grad, middle_low, middle_low_t, gain_two = call(
            middle_kernel, 1, [SCALARS, whole, whole, whole, whole, fixed((2, model))],
            [whole, whole, whole, turned, fixed((1, model))],
            [shaped(length, model, kind=bf16), shaped(length, model), shaped(length, model, kind=bf16), shaped(model, length, kind=bf16), shaped(1, model)],
            [pltpu.VMEM((length, model), bf16)],
            hold=[moved[0][1][1], moved[2][1][0]],
        )(places, middle, total, normed_grad, cot_low, gains)
        hidden_out = features(hidden_out, True)

        normed_grad = jnp.zeros((length, model), f32)
        backs = []
        out_grads = []
        out_moved = []
        back_holds = [
            [moved[1][1][1], moved[3][1][0]],
            [moved[0][1][2], moved[1][1][2], moved[2][1][1]],
        ]
        for pair in range(pairs):
            low, high, _ = out_pairs[pair]
            gate_pre, states, mixed_low = mixed[pair]
            lanes = slice(pair * pair_width, (pair + 1) * pair_width)
            normed_grad, local, product, edge, low_grad, high_grad = call(
                mix_back_kernel,
                groups,
                [whole, turned, turned, lanes_of(half, 2 * GROUP), lanes_of(half, 2 * GROUP), lanes_of(length), lanes_of(length + 8), lanes_of(length), lanes_of(length), lanes_of(8), whole],
                [whole, lanes_of(length), lanes_of(length), lanes_of(8), lanes_of(half, 2 * GROUP), lanes_of(half, 2 * GROUP)],
                [shaped(length, model), shaped(length, pair_width), shaped(length, pair_width), shaped(8, pair_width), shaped(half, 2 * pair_width, kind=bf16), shaped(half, 2 * pair_width, kind=bf16)],
                [pltpu.VMEM((length, GROUP), f32), pltpu.VMEM((length, GROUP), f32), pltpu.VMEM((length, GROUP), bf16), pltpu.VMEM((length + 8, GROUP), f32)],
                hold=back_holds[pair],
            )(middle_low, middle_low_t, normed_one_t, low, high, gate_pre, states, mixed_low, fed[pair][2], table[:, lanes], normed_grad)
            backs.append((local, product, edge))
            out_moved.append(scatter_dp(low_grad, high_grad, orders[pair % 2], block_rows))

        def separate(values):
            gate = [values[:, 2 * at * GROUP : (2 * at + 1) * GROUP] for at in range(groups)]
            out = [values[:, (2 * at + 1) * GROUP : (2 * at + 2) * GROUP] for at in range(groups)]
            gate, out = jnp.concatenate(gate, axis=1), jnp.concatenate(out, axis=1)
            return [jnp.concatenate([gate[:, :chunk], out[:, :chunk]], axis=1), jnp.concatenate([gate[:, chunk:], out[:, chunk:]], axis=1)]

        out_sum, out_back = join_tensor([part for one in out_moved for part in separate(one[0])])

        leave = exchange(
            jnp.concatenate([one[2][1:2] for one in backs], axis=1),
            jnp.concatenate([one[2][0:1] for one in backs], axis=1),
            True,
        )
        gate_backs = []
        gate_holds = [
            [moved[3][1][1], mlp_far[0], out_moved[0][1][0]],
            [moved[2][1][2], out_moved[1][1][0]],
        ]
        for pair in range(pairs):
            part = slice(2 * pair * local_blocks, 2 * (pair + 1) * local_blocks)
            lanes = slice(pair * pair_width, (pair + 1) * pair_width)
            branch, conv_out, recur_open, inflow = fed[pair][:4]
            local, product, _ = backs[pair]
            gate_backs.append(
                call(
                    gate_back_kernel,
                    groups,
                    [lanes_of(length), lanes_of(length), lanes_of(1), lanes_of(length + 8)] + [lanes_of(length)] * 3 + [lanes_of(full), blocks_of(), blocks_of(), lanes_of(8)],
                    [lanes_of(length), blocks_of(), blocks_of(), lanes_of(8)],
                    [shaped(length, pair_width), shaped(2 * local_blocks, BLOCK, BLOCK), shaped(2 * local_blocks, BLOCK, BLOCK), shaped(8, pair_width)],
                    [pltpu.VMEM((length, GROUP), bf16)] * 3,
                    hold=gate_holds[pair],
                )(local, product, leave[:, lanes], mixed[pair][1], recur_open, inflow, conv_out, branch, rgates[part], igates[part], table[:, lanes])
            )
        heads = jnp.concatenate([one[0][:8] for one in gate_backs], axis=1)
        heads = jnp.concatenate(relative(split_lanes(heads, tensor_size), tensor_at), axis=1)
        heads = lax.ppermute(heads, "tensor", [(at + 1, at) for at in range(tensor_size - 1)])
        after = jnp.concatenate(relative(split_lanes(heads, tensor_size), tensor_at), axis=1)
        in_parts = []
        branch_holds = [
            [moved[3][1][2], mlp_far[1], out_moved[0][1][1]],
            [out_moved[1][1][1]],
        ]
        for pair in range(pairs):
            low, high, _ = in_pairs[pair]
            lanes = slice(pair * pair_width, (pair + 1) * pair_width)
            normed_grad, low_grad, high_grad = call(
                branch_back_kernel,
                groups,
                [lanes_of(length), lanes_of(8), lanes_of(8), turned, lanes_of(half), lanes_of(half), whole],
                [whole, lanes_of(half), lanes_of(half)],
                [shaped(length, model), shaped(half, pair_width, kind=bf16), shaped(half, pair_width, kind=bf16)],
                [pltpu.VMEM((length + 8, GROUP), f32), pltpu.VMEM((length, GROUP), bf16)],
                hold=branch_holds[pair],
            )(gate_backs[pair][0], after[:, lanes], table[:, lanes], normed_one_t, low, high, normed_grad)
            in_parts += split_lanes(scatter_dp(low_grad, high_grad, orders[pair % 2], block_rows)[0], 2)
        in_sum, _ = join_tensor(in_parts)

        hidden_grad, gain_one = call(
            final_kernel, 1, [SCALARS, whole, whole, whole, fixed((2, model))], [whole, fixed((1, model))],
            [shaped(length, model), shaped(1, model)], [pltpu.VMEM((length, model), f32)],
            hold=[],
        )(places, hidden_low, normed_grad, middle_grad, gains)
        hidden_grad = features(hidden_grad, True)

        rgrads = jnp.concatenate([one[1] for one in gate_backs], axis=0)
        igrads = jnp.concatenate([one[2] for one in gate_backs], axis=0)
        rows = jnp.concatenate([one[3] for one in gate_backs], axis=1)
        decay_row = rows[3:4] * (8.0 * jax.nn.sigmoid(-decay_rates))
        rows = jnp.concatenate([rows[4:8], rows[0:3], decay_row], axis=0)
        gain_parts = jnp.concatenate([gain_one, gain_two], axis=0)
        if fast:
            def small_grads(*args, **sizes):
                small_grads_kernel(*args, sub=sub, local_blocks=local_blocks, chunks=tensor_size)
            small_own, small_other = call(
                small_grads, 1, [SCALARS, gate_spec, gate_spec, fixed((kinds, channels)), fixed((2, model))], [small_spec, small_spec],
                [shaped(*small_spec.block_shape, kind=bf16)] * 2, [],
            )(places, rgrads, igrads, rows, gain_parts)
        else:
            gate_grads = jnp.stack([rgrads, igrads], axis=0).reshape(2, tensor_size, local_blocks, dp_size, sub, BLOCK)
            gate_grads = gate_grads.transpose(3, 0, 2, 4, 1, 5).reshape(dp_size, gate_rows, tensor_size * BLOCK)
            gate_grads = jnp.take(gate_grads, natural_at, axis=0)
            rows = rows.reshape(kinds, tensor_size, local_blocks, BLOCK).transpose(0, 2, 1, 3).reshape(1, vector_rows, -1)
            gain_parts = gain_parts.reshape(2, dp_size, block_rows).transpose(1, 0, 2)
            gain_parts = jnp.pad(gain_parts, ((0, 0), (0, 0), (0, BLOCK - block_rows)))
            rest = small_rows - gate_rows - vector_rows - 2
            pieces = [
                gate_grads,
                jnp.broadcast_to(rows, (dp_size,) + rows.shape[1:]),
                jnp.tile(gain_parts, (1, 1, tensor_size)),
                jnp.zeros((dp_size, rest, tensor_size * BLOCK), f32),
            ]
            small_grads = jnp.concatenate(pieces, axis=1).reshape(dp_size * small_rows, -1).astype(bf16)
            small_own, small_other = jnp.split(small_grads, 2, axis=0)
        small_sum, _ = scatter_dp(small_own, small_other, order_one, small_rows)
        small_sum, _ = join_tensor(split_lanes(small_sum, tensor_size))
        gate_sum = small_sum[:gate_rows].reshape(2, local_blocks, sub, BLOCK).transpose(0, 2, 1, 3)
        vector_sum = lax.dynamic_slice(small_sum, (gate_rows, dp_at * sub), (vector_rows, sub))
        vector_sum = vector_sum.reshape(kinds, local_blocks, sub)
        gain_rows = block_rows // tensor_size
        gain_sum = lax.dynamic_slice(small_sum, (gate_rows + vector_rows, tensor_at * gain_rows), (2, gain_rows)).T

        return (
            hidden_out,
            hidden_grad,
            gain_sum,
            in_sum,
            out_sum[:, :chunk],
            out_sum[:, chunk:],
            gate_sum[1],
            gate_sum[0],
            vector_sum[:CONV].transpose(2, 0, 1),
            vector_sum[4].T,
            vector_sum[5].T,
            vector_sum[6].T,
            vector_sum[7].T,
            mlp_grads[0],
            mlp_grads[1],
            mlp_grads[2],
        )

    return per_device


def solution(mesh):
    rows = P(("dp", "tensor"), None)
    matrix = P("dp", "tensor")
    gate = P("dp", "tensor", None)
    kernel = P("dp", None, "tensor")
    placed = (rows, rows, P("dp", None), matrix, matrix, matrix, gate, gate, kernel) + (matrix,) * 7
    made = (rows, rows, rows, matrix, matrix, matrix, gate, gate, kernel) + (matrix,) * 7
    return jax.shard_map(
        make_per_device(mesh.shape["dp"], mesh.shape["tensor"]),
        mesh=mesh,
        in_specs=placed,
        out_specs=made,
        check_vma=False,
    )
```

```python
import jax
import jax.numpy as jnp
from jax import lax
from jax.experimental import pallas as pl
from jax.experimental.pallas import tpu as pltpu
from jax.sharding import PartitionSpec as P

BLOCK = 128
CONV = 4
HALO = 16
TILE = 64
GROUP = 256
epsilon = 1e-06
f32 = jnp.float32
bf16 = jnp.bfloat16
ROOT = 0.7978845608028654
CUBIC = 0.044715


def nn(left, right):
    return lax.dot_general(left, right, (((1,), (0,)), ((), ())), preferred_element_type=f32)


def nt(left, right):
    return lax.dot_general(left, right, (((1,), (1,)), ((), ())), preferred_element_type=f32)


def tn(left, right):
    return lax.dot_general(left, right, (((0,), (0,)), ((), ())), preferred_element_type=f32)


def gelu_parts(value):
    square = value * value
    curve = jnp.tanh(ROOT * value * (1.0 + CUBIC * square))
    half = 0.5 * (1.0 + curve)
    slope = half + (0.5 * ROOT) * value * (1.0 - curve * curve) * (1.0 + 3.0 * CUBIC * square)
    return value * half, slope


def one_minus_exp(value):
    series = 1.0 + value * (1.0 / 7.0)
    for term in (6.0, 5.0, 4.0, 3.0, 2.0):
        series = 1.0 + value * (1.0 / term) * series
    return jnp.where(value > -0.25, -value * series, 1.0 - jnp.exp(value))


def scan_rows(decay_ref, drive_ref, offset, out_ref, out_offset, total_ref, length, reverse):
    width = drive_ref.shape[1]
    rows = lax.broadcasted_iota(jnp.int32, (8, width), 0)
    steps = length // 8

    def body(step, carry):
        state, product = carry
        at = (steps - 1 - step) if reverse else step
        start = pl.multiple_of(at * 8, 8)
        decay = decay_ref[pl.ds(start, 8 + 8 * (offset > 0)), :][offset : offset + 8]
        drive = drive_ref[pl.ds(start, 8), :]
        for shift in (1, 2, 4):
            if reverse:
                inside = rows < 8 - shift
                amount = 8 - shift
            else:
                inside = rows >= shift
                amount = shift
            drive = drive + decay * jnp.where(inside, pltpu.roll(drive, amount, 0), 0.0)
            decay = decay * jnp.where(inside, pltpu.roll(decay, amount, 0), 1.0)
        state = drive + decay * state
        product = decay * product
        out_ref[pl.ds(start + out_offset, 8), :] = state
        total_ref[pl.ds(start, 8), :] = product
        edge = 0 if reverse else 7
        return (
            jnp.broadcast_to(state[edge : edge + 1], (8, width)),
            jnp.broadcast_to(product[edge : edge + 1], (8, width)),
        )

    lax.fori_loop(0, steps, body, (jnp.zeros((8, width), f32), jnp.ones((8, width), f32)))


def tiles(length, body):
    def step(index, carry):
        body(pl.multiple_of(index * TILE, TILE))
        return carry

    lax.fori_loop(0, length // TILE, step, 0)


def mix_in_kernel(
    normed_ref, low_ref, high_ref, rgate_ref, igate_ref, table_ref,
    branch_ref, conv_ref, open_ref, flow_ref, local_ref, product_ref,
    conv_low, rec_buf, inp_buf, decay_buf,
):
    length = conv_ref.shape[0]
    half = low_ref.shape[0]
    branch_ref[...] = nn(normed_ref[:, :half], low_ref[...]) + nn(normed_ref[:, half:], high_ref[...])
    for part in range(GROUP // BLOCK):
        lanes = slice(part * BLOCK, (part + 1) * BLOCK)

        def convolve(start):
            window = branch_ref[pl.ds(start + HALO - 8, TILE + 8), lanes]
            result = table_ref[4:5, lanes] + table_ref[0:1, lanes] * window[8:]
            for offset in range(1, CONV):
                result = result + table_ref[offset : offset + 1, lanes] * window[8 - offset : 8 - offset + TILE]
            conv_ref[pl.ds(start, TILE), lanes] = result
            conv_low[pl.ds(start, TILE), lanes] = result.astype(bf16)

        tiles(length, convolve)
        rec_buf[:, lanes] = nn(conv_low[:, lanes], rgate_ref[part])
        inp_buf[:, lanes] = nn(conv_low[:, lanes], igate_ref[part])

        def gates(start):
            rows = pl.ds(start, TILE)
            recur_open = jax.nn.sigmoid(rec_buf[rows, lanes] + table_ref[6:7, lanes])
            inflow = jax.nn.sigmoid(inp_buf[rows, lanes] + table_ref[5:6, lanes])
            log_decay = recur_open * table_ref[7:8, lanes]
            multiplier = jnp.sqrt(one_minus_exp(2.0 * log_decay))
            open_ref[rows, lanes] = recur_open
            flow_ref[rows, lanes] = inflow
            decay_buf[rows, lanes] = jnp.exp(log_decay)
            rec_buf[rows, lanes] = multiplier * inflow * conv_ref[rows, lanes]

        tiles(length, gates)
    scan_rows(decay_buf, rec_buf, 0, local_ref, 0, product_ref, length, False)


def mix_out_kernel(
    normed_ref, low_ref, high_ref, local_ref, product_ref, enter_ref, sum_ref,
    pre_ref, states_ref, mixed_ref, total_ref,
):
    length = local_ref.shape[0]
    half = low_ref.shape[0]

    @pl.when(pl.program_id(0) == 0)
    def _():
        total_ref[...] = sum_ref[...]

    pre_ref[...] = nn(normed_ref[HALO:, :half], low_ref[:, :GROUP]) + nn(normed_ref[HALO:, half:], high_ref[:, :GROUP])
    states_ref[0:8, :] = jnp.broadcast_to(enter_ref[0:1, :], (8, GROUP))
    for part in range(GROUP // BLOCK):
        lanes = slice(part * BLOCK, (part + 1) * BLOCK)

        def mix(start):
            rows = pl.ds(start, TILE)
            states = local_ref[rows, lanes] + product_ref[rows, lanes] * enter_ref[0:1, lanes]
            states_ref[pl.ds(start + 8, TILE), lanes] = states
            gate = pre_ref[rows, lanes]
            curve = jnp.tanh(ROOT * gate * (1.0 + CUBIC * gate * gate))
            mixed_ref[rows, lanes] = (states * (gate * (0.5 * (1.0 + curve)))).astype(bf16)

        tiles(length, mix)
    total_ref[:, :half] += nt(mixed_ref[...], low_ref[:, GROUP:])
    total_ref[:, half:] += nt(mixed_ref[...], high_ref[:, GROUP:])


def mlp_kernel(
    chunks_ref, normed_ref, normed_t_ref, cot_ref, cot_t_ref, weights_ref, sum_ref, back_ref,
    total_ref, grad_ref, low_grad_ref, high_grad_ref,
    pre, hidden, pre_low, act,
):
    length, model = normed_ref.shape
    half = model // 2
    first = sum_ref is None

    @pl.when(pl.program_id(0) == 0)
    def _():
        if first:
            total_ref[...] = jnp.zeros_like(total_ref)
            grad_ref[...] = jnp.zeros_like(grad_ref)
        else:
            total_ref[...] = sum_ref[...]
            grad_ref[...] = back_ref[...]

    weights = weights_ref[...].reshape(model, 3 * GROUP)
    pre[...] = nn(normed_ref[...], weights[:, : 2 * GROUP])
    act[...] = nn(cot_ref[...], weights[:, 2 * GROUP :])
    for part in range(GROUP // BLOCK):
        lanes = slice(part * BLOCK, (part + 1) * BLOCK)
        up_lanes = slice(GROUP + part * BLOCK, GROUP + (part + 1) * BLOCK)

        def activate(start):
            rows = pl.ds(start, TILE)
            value, slope = gelu_parts(pre[rows, lanes])
            up = pre[rows, up_lanes]
            grad = act[rows, lanes]
            hidden[rows, lanes] = (value * up).astype(bf16)
            pre_low[rows, lanes] = (grad * up * slope).astype(bf16)
            pre_low[rows, up_lanes] = (grad * value).astype(bf16)

        tiles(length, activate)
    total_ref[...] += nt(hidden[...], weights[:, 2 * GROUP :])
    grad_ref[...] += nt(pre_low[...], weights[:, : 2 * GROUP])
    low_grad_ref[:, : 2 * GROUP] = nn(normed_t_ref[:half], pre_low[...]).astype(bf16)
    high_grad_ref[:, : 2 * GROUP] = nn(normed_t_ref[half:], pre_low[...]).astype(bf16)
    low_grad_ref[:, 2 * GROUP :] = nn(cot_t_ref[:half], hidden[...]).astype(bf16)
    high_grad_ref[:, 2 * GROUP :] = nn(cot_t_ref[half:], hidden[...]).astype(bf16)


def lane_block(index):
    return pl.ds(pl.multiple_of(index * BLOCK, BLOCK), BLOCK)


def order_kernel(places_ref, hidden_ref, cot_ref, hidden_out_ref, cot_out_ref, cot_t_ref):
    for place in range(hidden_ref.shape[1] // BLOCK):
        lanes = slice(place * BLOCK, (place + 1) * BLOCK)
        hidden_out_ref[:, lanes] = hidden_ref[:, lane_block(places_ref[place])]
        cot_out_ref[:, lanes] = cot_ref[:, lane_block(places_ref[place])]
    cot_t_ref[...] = cot_out_ref[...].T


def row_loop(length, rows, body, start):
    def step(index, carry):
        return body(pl.ds(pl.multiple_of(index * rows, rows), rows), carry)

    return lax.fori_loop(0, length // rows, step, start)


def scale_of(values):
    return lax.rsqrt(jnp.mean(values * values, axis=1, keepdims=True) + epsilon)


def norm_kernel(places_ref, hidden_ref, first_ref, gains_ref, normed_ref, normed_t_ref, first_buf):
    length = hidden_ref.shape[0]
    for place in range(hidden_ref.shape[1] // BLOCK):
        lanes = slice(place * BLOCK, (place + 1) * BLOCK)
        first_buf[:, lanes] = first_ref[:, lane_block(places_ref[place])].astype(f32)
    first = first_buf[...]
    normed_ref[:HALO, :] = (first * scale_of(first) * gains_ref[0:1, :]).astype(bf16)

    def body(rows, carry):
        values = hidden_ref[rows, :].astype(f32)
        normed_ref[pl.ds(rows.start + HALO, rows.size), :] = (values * scale_of(values) * gains_ref[0:1, :]).astype(bf16)
        return carry

    row_loop(length, 16, body, 0)
    normed_t_ref[...] = normed_ref[HALO:, :].T


def second_norm_kernel(places_ref, middle_ref, gains_ref, normed_ref, normed_t_ref, buffer):
    length, model = middle_ref.shape

    def body(rows, carry):
        values = middle_ref[rows, :]
        buffer[rows, :] = (values * scale_of(values) * gains_ref[1:2, :]).astype(bf16)
        return carry

    row_loop(length, 16, body, 0)
    normed_t_ref[...] = buffer[...].T
    for place in range(model // BLOCK):
        normed_ref[:, lane_block(places_ref[place])] = buffer[:, place * BLOCK : (place + 1) * BLOCK]


def norm_back(values, grad, gain):
    scale = scale_of(values)
    unit = values * scale
    scaled = grad * gain
    return scale * (scaled - unit * jnp.mean(scaled * unit, axis=1, keepdims=True)), grad * unit


def fold_rows(value):
    rows, width = value.shape
    return jnp.sum(value.reshape(rows // 8, 8, width), axis=0)


def middle_kernel(
    places_ref, middle_ref, total_ref, grad_ref, cot_ref, gains_ref,
    out_ref, middle_grad_ref, low_ref, low_t_ref, gain_ref, buffer, own_total, own_grad,
):
    length, model = middle_ref.shape
    for place in range(model // BLOCK):
        lanes = slice(place * BLOCK, (place + 1) * BLOCK)
        own_total[:, lanes] = total_ref[:, lane_block(places_ref[place])]
        own_grad[:, lanes] = grad_ref[:, lane_block(places_ref[place])]

    def body(rows, carry):
        middle = middle_ref[rows, :]
        change, part = norm_back(middle, own_grad[rows, :], gains_ref[1:2, :])
        middle_grad = cot_ref[rows, :].astype(f32) + change
        middle_grad_ref[rows, :] = middle_grad
        low_ref[rows, :] = middle_grad.astype(bf16)
        buffer[rows, :] = (middle + own_total[rows, :]).astype(bf16)
        return carry + fold_rows(part)

    total = row_loop(length, 16, body, jnp.zeros((8, model), f32))
    gain_ref[...] = jnp.sum(total, axis=0, keepdims=True)
    low_t_ref[...] = low_ref[...].T
    for place in range(model // BLOCK):
        out_ref[:, lane_block(places_ref[place])] = buffer[:, place * BLOCK : (place + 1) * BLOCK]


def final_kernel(places_ref, hidden_ref, grad_ref, middle_grad_ref, gains_ref, out_ref, gain_ref, buffer):
    length, model = hidden_ref.shape

    def body(rows, carry):
        change, part = norm_back(hidden_ref[rows, :].astype(f32), grad_ref[rows, :], gains_ref[0:1, :])
        buffer[rows, :] = middle_grad_ref[rows, :] + change
        return carry + fold_rows(part)

    total = row_loop(length, 16, body, jnp.zeros((8, model), f32))
    gain_ref[...] = jnp.sum(total, axis=0, keepdims=True)
    for place in range(model // BLOCK):
        out_ref[:, lane_block(places_ref[place])] = buffer[:, place * BLOCK : (place + 1) * BLOCK]


def tables_kernel(places_ref, low_ref, high_ref, rgate_ref, igate_ref, table_ref, gains_ref, *, sub, local_blocks, chunks):
    rows_each = 2 * local_blocks * sub
    kinds = 2 * CONV
    count = places_ref.shape[0]
    size = low_ref.shape[0] * 2 // count
    sums = [jnp.zeros((kinds * local_blocks, BLOCK), f32)] * chunks
    for place in range(count):
        source = low_ref if place < count // 2 else high_ref
        top = (place % (count // 2)) * size
        natural = places_ref[place]
        for at in range(chunks):
            lanes = slice(at * BLOCK, (at + 1) * BLOCK)
            for which, gate_ref in enumerate((rgate_ref, igate_ref)):
                for block in range(local_blocks):
                    start = top + (which * local_blocks + block) * sub
                    gate_ref[at * local_blocks + block, pl.ds(pl.multiple_of(natural * sub, sub), sub), :] = source[start : start + sub, lanes]
            sums[at] = sums[at] + source[top + rows_each : top + rows_each + kinds * local_blocks, lanes].astype(f32)
        start = top + rows_each + kinds * local_blocks
        gains_ref[:, place * BLOCK : (place + 1) * BLOCK] = source[start : start + 2, :BLOCK].astype(f32)
    for at in range(chunks):
        for block in range(local_blocks):
            column = (at * local_blocks + block) * BLOCK
            for kind in range(kinds):
                row = kind * local_blocks + block
                table_ref[kind : kind + 1, column : column + BLOCK] = sums[at][row : row + 1]


def small_grads_kernel(places_ref, rgrad_ref, igrad_ref, sums_ref, low_ref, high_ref, *, sub, local_blocks, chunks):
    kinds = 2 * CONV
    rows_each = 2 * local_blocks * sub
    count = places_ref.shape[0]
    size = low_ref.shape[0] * 2 // count
    spare = size - rows_each - kinds * local_blocks
    vectors = []
    for at in range(chunks):
        rows = []
        for kind in range(kinds):
            for block in range(local_blocks):
                column = (at * local_blocks + block) * BLOCK
                rows.append(sums_ref[kind : kind + 1, column : column + BLOCK])
        vectors.append(jnp.concatenate(rows, axis=0))
    for place in range(count):
        target = low_ref if place < count // 2 else high_ref
        top = (place % (count // 2)) * size
        natural = places_ref[place]
        for at in range(chunks):
            lanes = slice(at * BLOCK, (at + 1) * BLOCK)
            for which, grad_ref in enumerate((rgrad_ref, igrad_ref)):
                for block in range(local_blocks):
                    start = top + (which * local_blocks + block) * sub
                    target[start : start + sub, lanes] = grad_ref[
                        at * local_blocks + block, pl.ds(pl.multiple_of(natural * sub, sub), sub), :
                    ].astype(bf16)
            rest = jnp.concatenate([vectors[at], jnp.zeros((spare, BLOCK), f32)], axis=0)
            target[top + rows_each : top + size, lanes] = rest.astype(bf16)


def mix_back_kernel(
    grad_low_ref, grad_t_ref, normed_t_ref, low_ref, high_ref, pre_ref, states_ref, mixed_ref, open_ref, table_ref, sum_ref,
    total_ref, local_ref, product_ref, edge_ref, low_grad_ref, high_grad_ref,
    mixed_grad, drive, pre_low, decay_buf,
):
    length = pre_ref.shape[0]
    half = low_ref.shape[0]

    @pl.when(pl.program_id(0) == 0)
    def _():
        total_ref[...] = sum_ref[...]

    mixed_grad[...] = nn(grad_low_ref[:, :half], low_ref[:, GROUP:]) + nn(grad_low_ref[:, half:], high_ref[:, GROUP:])
    decay_buf[pl.ds(length, 8), :] = jnp.ones((8, GROUP), f32)
    for part in range(GROUP // BLOCK):
        lanes = slice(part * BLOCK, (part + 1) * BLOCK)

        def back(start):
            rows = pl.ds(start, TILE)
            value, slope = gelu_parts(pre_ref[rows, lanes])
            grad = mixed_grad[rows, lanes]
            pre_low[rows, lanes] = (grad * states_ref[pl.ds(start + 8, TILE), lanes] * slope).astype(bf16)
            drive[rows, lanes] = grad * value
            decay_buf[rows, lanes] = jnp.exp(open_ref[rows, lanes] * table_ref[7:8, lanes])

        tiles(length, back)
    scan_rows(decay_buf, drive, 1, local_ref, 0, product_ref, length, True)
    edge_ref[0:1, :] = decay_buf[0:1, :] * local_ref[0:1, :]
    edge_ref[1:2, :] = decay_buf[0:1, :] * product_ref[0:1, :]
    total_ref[:, :half] += nt(pre_low[...], low_ref[:, :GROUP])
    total_ref[:, half:] += nt(pre_low[...], high_ref[:, :GROUP])
    low_grad_ref[:, :GROUP] = nn(normed_t_ref[:half], pre_low[...]).astype(bf16)
    high_grad_ref[:, :GROUP] = nn(normed_t_ref[half:], pre_low[...]).astype(bf16)
    low_grad_ref[:, GROUP:] = nn(grad_t_ref[:half], mixed_ref[...]).astype(bf16)
    high_grad_ref[:, GROUP:] = nn(grad_t_ref[half:], mixed_ref[...]).astype(bf16)


def gate_back_kernel(
    local_ref, product_ref, enter_ref, states_ref, open_ref, flow_ref, conv_ref, branch_ref, rgate_ref, igate_ref, table_ref,
    conv_grad_ref, rgrad_ref, igrad_ref, sums_ref,
    rec_low, inp_low, conv_low,
):
    length = local_ref.shape[0]
    for part in range(GROUP // BLOCK):
        lanes = slice(part * BLOCK, (part + 1) * BLOCK)

        def back(index, sums):
            start = pl.multiple_of(index * TILE, TILE)
            rows = pl.ds(start, TILE)
            carried = local_ref[rows, lanes] + product_ref[rows, lanes] * enter_ref[0:1, lanes]
            recur_open = open_ref[rows, lanes]
            inflow = flow_ref[rows, lanes]
            conv_out = conv_ref[rows, lanes]
            rate = table_ref[7:8, lanes]
            log_decay = recur_open * rate
            decay = jnp.exp(log_decay)
            multiplier = jnp.sqrt(one_minus_exp(2.0 * log_decay))
            before = states_ref[pl.ds(start, TILE + 8), lanes][7 : 7 + TILE]
            weighted = carried * inflow
            decay_grad = carried * before * decay - weighted * conv_out * decay * decay / multiplier
            scaled = decay_grad * recur_open
            rec_grad = rate * scaled * (1.0 - recur_open)
            direct = weighted * multiplier
            inp_grad = direct * conv_out * (1.0 - inflow)
            rec_low[rows, lanes] = rec_grad.astype(bf16)
            inp_low[rows, lanes] = inp_grad.astype(bf16)
            conv_low[rows, lanes] = conv_out.astype(bf16)
            conv_grad_ref[rows, lanes] = direct

            def fold(value):
                return jnp.sum(value.reshape(TILE // 8, 8, BLOCK), axis=0)

            return (sums[0] + fold(rec_grad), sums[1] + fold(inp_grad), sums[2] + fold(scaled))

        zero = jnp.zeros((8, BLOCK), f32)
        sums = lax.fori_loop(0, length // TILE, back, (zero, zero, zero))
        for row, value in zip((2, 1, 3), sums):
            sums_ref[row : row + 1, lanes] = jnp.sum(value, axis=0, keepdims=True)
        rgrad_ref[part] = tn(conv_low[:, lanes], rec_low[:, lanes])
        igrad_ref[part] = tn(conv_low[:, lanes], inp_low[:, lanes])
        conv_grad_ref[:, lanes] += nt(rec_low[:, lanes], rgate_ref[part]) + nt(inp_low[:, lanes], igate_ref[part])

        def taps(index, sums):
            start = pl.multiple_of(index * TILE, TILE)
            grad = conv_grad_ref[pl.ds(start, TILE), lanes]

            def fold(value):
                return jnp.sum(value.reshape(TILE // 8, 8, BLOCK), axis=0)

            window = branch_ref[pl.ds(start + HALO - 8, TILE + 8), lanes]
            new = [sums[0] + fold(grad)]
            for offset in range(CONV):
                new.append(sums[offset + 1] + fold(grad * window[8 - offset : 8 - offset + TILE]))
            return tuple(new)

        sums = lax.fori_loop(0, length // TILE, taps, (zero,) * (CONV + 1))
        for row, value in zip((0, 4, 5, 6, 7), sums):
            sums_ref[row : row + 1, lanes] = jnp.sum(value, axis=0, keepdims=True)


def branch_back_kernel(
    conv_grad_ref, after_ref, table_ref, normed_t_ref, low_ref, high_ref, sum_ref,
    total_ref, low_grad_ref, high_grad_ref,
    padded, branch_low,
):
    length = conv_grad_ref.shape[0]
    half = low_ref.shape[0]

    @pl.when(pl.program_id(0) == 0)
    def _():
        total_ref[...] = sum_ref[...]

    padded[pl.ds(0, length), :] = conv_grad_ref[...]
    padded[pl.ds(length, 8), :] = after_ref[...]
    for part in range(GROUP // BLOCK):
        lanes = slice(part * BLOCK, (part + 1) * BLOCK)

        def back(start):
            window = padded[pl.ds(start, TILE + 8), lanes]
            result = table_ref[0:1, lanes] * window[:TILE]
            for offset in range(1, CONV):
                result = result + table_ref[offset : offset + 1, lanes] * window[offset : offset + TILE]
            branch_low[pl.ds(start, TILE), lanes] = result.astype(bf16)

        tiles(length, back)
    total_ref[:, :half] += nt(branch_low[...], low_ref[...])
    total_ref[:, half:] += nt(branch_low[...], high_ref[...])
    low_grad_ref[...] = nn(normed_t_ref[:half], branch_low[...]).astype(bf16)
    high_grad_ref[...] = nn(normed_t_ref[half:], branch_low[...]).astype(bf16)


def join_kernel(*refs, columns):
    parts, outs = refs[: -len(columns)], refs[-len(columns) :]
    for out_ref, places in zip(outs, columns):
        to = 0
        for start, size in places:
            total = parts[0][:, start : start + size].astype(f32)
            for part in parts[1:]:
                total = total + part[:, start : start + size].astype(f32)
            out_ref[:, to : to + size] = total
            to += size


def fixed(shape):
    return pl.BlockSpec(shape, lambda g: (0,) * len(shape))


def lanes_of(rows, width=GROUP):
    return pl.BlockSpec((rows, width), lambda g: (0, g))


def blocks_of():
    return pl.BlockSpec((GROUP // BLOCK, BLOCK, BLOCK), lambda g: (g, 0, 0))


def shaped(*dims, kind=f32):
    return jax.ShapeDtypeStruct(dims, kind)


PARAMS = pltpu.CompilerParams(dimension_semantics=("arbitrary",), vmem_limit_bytes=56 * 1024 * 1024)


ANYWHERE = pl.BlockSpec(memory_space=pl.ANY)
SCALARS = pl.BlockSpec(memory_space=pltpu.SMEM)


SPANS = {
    "order_kernel": 4, "tables_of": 2, "norm_kernel": 6, "mix_in_kernel": 14, "mix_out_kernel": 10,
    "second_norm_kernel": 6, "mlp_kernel": 17, "middle_kernel": 12, "mix_back_kernel": 18, "gate_back_kernel": 11,
    "branch_back_kernel": 8, "final_kernel": 10, "small_grads": 3, "join": 2,
}


def call(kernel, steps, in_specs, out_specs, out_shape, scratch, hold=()):
    count = len(in_specs)
    name = getattr(kernel, "func", kernel).__name__

    def body(*refs):
        kernel(*refs[:count], *refs[count + len(hold) :])

    run = pl.pallas_call(
        body,
        grid=(steps,),
        in_specs=list(in_specs) + [ANYWHERE] * len(hold),
        out_specs=out_specs,
        out_shape=out_shape,
        scratch_shapes=scratch,
        compiler_params=PARAMS,
        name=name,
        cost_estimate=pl.CostEstimate(flops=SPANS[name] * 1150 * 10**6, bytes_accessed=0, transcendentals=0),
    )
    return lambda *args: run(*args, *hold)


def make_per_device(dp_size, tensor_size):
    pairs = tensor_size // 2
    dp_bits = [1 << bit for bit in range(dp_size.bit_length() - 1)]
    order_one = dp_bits[1:] + dp_bits[:1]
    order_two = dp_bits[2:3] + dp_bits[1:2] + dp_bits[3:] + dp_bits[:1]
    orders = (order_one, order_two)
    position_of = {bit: place for place, bit in enumerate(order_one)}

    def swap_dp(values, bit):
        return lax.ppermute(values, "dp", [(at, at ^ bit) for at in range(dp_size)])

    def swap_tensor(values, bit):
        return lax.ppermute(values, "tensor", [(at, at ^ bit) for at in range(tensor_size)])

    def relative(pieces, index):
        bit = 1
        while bit < len(pieces):
            flag = (index & bit) != 0
            pieces = [jnp.where(flag, pieces[at ^ bit], piece) for at, piece in enumerate(pieces)]
            bit *= 2
        return pieces

    place_index = [
        sum(bit for bit in dp_bits if place & (1 << position_of[bit])) for place in range(dp_size)
    ]

    def split_lanes(values, count):
        width = values.shape[1] // count
        return [values[:, at * width : (at + 1) * width] for at in range(count)]

    def gather_dp(values, order):
        rows = values.shape[0]
        done, marks = [], []
        for bit in order[:-1]:
            received = swap_dp(values, bit)
            marks.append(received)
            low_place = position_of[bit]
            if all(position_of[other] < low_place for other in done):
                values = jnp.concatenate([values, received], axis=0)
            else:
                pieces = []
                for at in range(values.shape[0] // rows):
                    pieces += [values[at * rows : (at + 1) * rows], received[at * rows : (at + 1) * rows]]
                values = jnp.concatenate(pieces, axis=0)
            done.append(bit)
        last = swap_dp(values, order[-1])
        return values, last, marks + [last]

    def add(one, two):
        return (one.astype(f32) + two.astype(f32)).astype(one.dtype)

    def scatter_dp(own, other, order, block_rows):
        values = add(own, swap_dp(other, order[-1]))
        marks = [values]
        left = list(order[:-1])
        while left:
            bit = left.pop()
            place = position_of[bit]
            rows = values.shape[0]
            if all(position_of[o] < place for o in left):
                keep, send = values[: rows // 2], values[rows // 2 :]
            else:
                count = rows // block_rows
                take = lambda start: jnp.concatenate(
                    [values[at * block_rows : (at + 1) * block_rows] for at in range(start, count, 2)], axis=0
                )
                keep, send = take(0), take(1)
            values = add(keep, swap_dp(send, bit))
            marks.append(values)
        return values, marks

    def spread_tensor(values):
        return [values] + [swap_tensor(values, other) for other in range(1, tensor_size)]

    def join_parts(own, others, columns, hold):
        received = {other: swap_tensor(part, other) for other, part in others.items()}
        parts = [own] + [received[other] for other in range(1, tensor_size)]

        def join(*refs):
            join_kernel(*refs, columns=columns)

        rows = own.shape[0]
        widths = [sum(size for _, size in places) for places in columns]
        return call(
            join, 1, [fixed(own.shape)] * tensor_size, [fixed((rows, width)) for width in widths],
            [shaped(rows, width) for width in widths], [], hold=hold,
        )(*parts)

    def join_tensor(parts):
        total = parts[0].astype(f32)
        received = []
        for other in range(1, tensor_size):
            received.append(swap_tensor(parts[other], other))
            total = total + received[-1].astype(f32)
        return total, received

    def per_device(
        hidden_in, cotangent, norm_gains, mixer_in, branch_gate, mixer_out, input_gate, recur_gate,
        conv_kernel, conv_bias, input_bias, recur_bias, decay_param, mlp_gate, mlp_up, mlp_down,
    ):
        dp_at = lax.axis_index("dp")
        tensor_at = lax.axis_index("tensor")
        length, model = hidden_in.shape
        block_rows, chunk = mixer_in.shape
        half = model // 2
        hidden_chunk = mlp_gate.shape[1]
        sub = block_rows * BLOCK // model
        local_blocks = chunk // BLOCK
        pair_width = 2 * chunk
        groups = pair_width // GROUP
        mlp_groups = hidden_chunk // GROUP
        fast = block_rows == BLOCK and sub % 16 == 0
        natural_at = jnp.array(place_index, jnp.int32) ^ dp_at
        places = natural_at if fast else jnp.arange(model // BLOCK, dtype=jnp.int32)

        def features(values, back=False):
            if fast:
                return values
            pieces = jnp.stack(split_lanes(values, dp_size), axis=0)
            order = natural_at
            if back:
                order = jnp.zeros_like(natural_at).at[natural_at].set(jnp.arange(dp_size, dtype=jnp.int32))
            return jnp.concatenate(list(jnp.take(pieces, order, axis=0)), axis=1)

        first_rows = lax.ppermute(
            hidden_in[length - HALO :], "tensor", [(at, at + 1) for at in range(tensor_size - 1)]
        )

        def rows_first(table):
            return table.transpose(1, 0, 2).reshape(-1, BLOCK)

        vectors = jnp.concatenate(
            [conv_kernel.transpose(1, 2, 0).reshape(-1, sub)]
            + [table.T for table in (conv_bias, input_bias, recur_bias, decay_param)],
            axis=0,
        )
        owner = lax.broadcasted_iota(jnp.int32, (1, BLOCK), 1) // sub
        vectors = jnp.where(owner == dp_at, jnp.tile(vectors, (1, BLOCK // sub)), jnp.zeros((), bf16))
        gate_rows = 2 * local_blocks * sub
        vector_rows = vectors.shape[0]
        small_rows = (gate_rows + vector_rows + 2 + 15) // 16 * 16
        small = jnp.concatenate(
            [
                rows_first(recur_gate),
                rows_first(input_gate),
                vectors,
                jnp.pad(norm_gains.T, ((0, 0), (0, BLOCK - block_rows))),
                jnp.zeros((small_rows - gate_rows - vector_rows - 2, BLOCK), bf16),
            ],
            axis=0,
        )
        small_low, small_high, _ = gather_dp(jnp.concatenate(spread_tensor(small), axis=1), order_one)

        def gather_pairs(values, arrange):
            found = spread_tensor(values)
            result = []
            for pair in range(pairs):
                packed = arrange(found[2 * pair], found[2 * pair + 1])
                result.append(gather_dp(packed, orders[pair % 2]))
            return result, found[1:]

        def interleave(one, two):
            gate = jnp.concatenate([one[:, :chunk], two[:, :chunk]], axis=1)
            out = jnp.concatenate([one[:, chunk:], two[:, chunk:]], axis=1)
            pieces = []
            for at in range(groups):
                pieces += [gate[:, at * GROUP : (at + 1) * GROUP], out[:, at * GROUP : (at + 1) * GROUP]]
            return jnp.concatenate(pieces, axis=1)

        in_pairs, in_far = gather_pairs(mixer_in, lambda one, two: jnp.concatenate([one, two], axis=1))
        out_pairs, out_far = gather_pairs(jnp.concatenate([branch_gate, mixer_out], axis=1), interleave)
        mlp_pieces = []
        for at in range(mlp_groups):
            mlp_pieces += [w[:, at * GROUP : (at + 1) * GROUP] for w in (mlp_gate, mlp_up, mlp_down)]
        mlp_weights = lax.all_gather(jnp.concatenate(mlp_pieces, axis=1), ("dp", "tensor"), axis=0, tiled=False)
        mlp_weights = mlp_weights.reshape(dp_size, tensor_size, block_rows, 3 * hidden_chunk)

        whole = fixed((length, model))
        turned = fixed((model, length))
        hidden_low, cot_low, cot_t = call(
            order_kernel, 1, [SCALARS, whole, whole], [whole, whole, turned],
            [shaped(length, model, kind=bf16), shaped(length, model, kind=bf16), shaped(model, length, kind=bf16)], [],
        )(places, features(hidden_in), features(cotangent))

        kinds = 2 * CONV
        channels = tensor_size * chunk
        blocks = tensor_size * local_blocks
        if fast:
            small_spec = fixed((model // 2 // block_rows * small_rows, tensor_size * BLOCK))
            gate_spec = fixed((blocks, BLOCK, BLOCK))
            def tables_of(*args, **sizes):
                tables_kernel(*args, sub=sub, local_blocks=local_blocks, chunks=tensor_size)
            rgates, igates, table, gains = call(
                tables_of, 1, [SCALARS, small_spec, small_spec], [gate_spec, gate_spec, fixed((kinds, channels)), fixed((2, model))],
                [shaped(blocks, BLOCK, BLOCK, kind=bf16), shaped(blocks, BLOCK, BLOCK, kind=bf16), shaped(kinds, channels), shaped(2, model)], [],
                hold=out_far,
            )(places, small_low, small_high)
        else:
            stacked = jnp.concatenate([small_low, small_high], axis=0).reshape(dp_size, small_rows, -1)
            order = jnp.zeros_like(natural_at).at[natural_at].set(jnp.arange(dp_size, dtype=jnp.int32))
            gates = jnp.take(stacked[:, :gate_rows], order, axis=0).reshape(dp_size, 2, local_blocks, sub, tensor_size, BLOCK)
            gates = gates.transpose(1, 4, 2, 0, 3, 5).reshape(2, blocks, BLOCK, BLOCK)
            rgates, igates = gates[0], gates[1]
            table = jnp.sum(stacked[:, gate_rows : gate_rows + vector_rows].astype(f32), axis=0)
            table = table.reshape(kinds, local_blocks, tensor_size, BLOCK).transpose(0, 2, 1, 3).reshape(kinds, channels)
            gains = stacked[:, gate_rows + vector_rows : gate_rows + vector_rows + 2, :block_rows]
            gains = gains.transpose(1, 0, 2).reshape(2, model).astype(f32)
        decay_rates = table[7:8]
        table = jnp.concatenate([table[:7], -8.0 * jax.nn.softplus(-decay_rates)], axis=0)

        full = length + HALO
        normed_one, normed_one_t = call(
            norm_kernel, 1, [SCALARS, whole, fixed((HALO, model)), fixed((2, model))], [fixed((full, model)), turned],
            [shaped(full, model, kind=bf16), shaped(model, length, kind=bf16)], [pltpu.VMEM((HALO, model), f32)],
        )(places, hidden_low, features(first_rows), gains)

        fed = []
        fed_holds = [
            [out_pairs[0][2][0], out_pairs[1][2][0]],
            [out_pairs[0][2][1], out_pairs[1][2][1]],
        ]
        for pair in range(pairs):
            low, high, _ = in_pairs[pair]
            part = slice(2 * pair * local_blocks, 2 * (pair + 1) * local_blocks)
            lanes = slice(pair * pair_width, (pair + 1) * pair_width)
            fed.append(
                call(
                    mix_in_kernel,
                    groups,
                    [fixed((full, model)), lanes_of(half), lanes_of(half), blocks_of(), blocks_of(), lanes_of(8)],
                    [lanes_of(full)] + [lanes_of(length)] * 5,
                    [shaped(full, pair_width)] + [shaped(length, pair_width)] * 5,
                    [pltpu.VMEM((length, GROUP), bf16)] + [pltpu.VMEM((length, GROUP), f32)] * 3,
                    hold=fed_holds[pair],
                )(normed_one, low, high, rgates[part], igates[part], table[:, lanes])
            )

        def exchange(products, ends, later):
            mine = jnp.concatenate([products, ends], axis=0)
            found = [mine]
            for other in range(1, tensor_size):
                pieces = split_lanes(swap_tensor(mine, other), tensor_size)
                found.append(jnp.concatenate([pieces[at ^ other] for at in range(tensor_size)], axis=1))
            found = relative(found, tensor_at)
            state = jnp.zeros_like(ends)
            turn = range(tensor_size - 1, 0, -1) if later else range(tensor_size - 1)
            for at in turn:
                use = (at > tensor_at) if later else (at < tensor_at)
                state = jnp.where(use, found[at][0:1] * state + found[at][1:2], state)
            return state

        enter = exchange(
            jnp.concatenate([one[5][length - 1 :] for one in fed], axis=1),
            jnp.concatenate([one[4][length - 1 :] for one in fed], axis=1),
            False,
        )
        middle = hidden_low.astype(f32)
        mixed = []
        for pair in range(pairs):
            low, high, _ = out_pairs[pair]
            lanes = slice(pair * pair_width, (pair + 1) * pair_width)
            gate_pre, states, mixed_low, middle = call(
                mix_out_kernel,
                groups,
                [fixed((full, model)), lanes_of(half, 2 * GROUP), lanes_of(half, 2 * GROUP), lanes_of(length), lanes_of(length), lanes_of(1), whole],
                [lanes_of(length), lanes_of(length + 8), lanes_of(length), whole],
                [shaped(length, pair_width), shaped(length + 8, pair_width), shaped(length, pair_width, kind=bf16), shaped(length, model)],
                [],
            )(normed_one, low, high, fed[pair][4], fed[pair][5], enter[:, lanes], middle)
            mixed.append((gate_pre, states, mixed_low))
        normed_two, normed_two_t = call(
            second_norm_kernel, 1, [SCALARS, whole, fixed((2, model))], [whole, turned],
            [shaped(length, model, kind=bf16), shaped(model, length, kind=bf16)], [pltpu.VMEM((length, model), bf16)],
        )(places, middle, gains)
        normed_two = features(normed_two, True)

        chunk_at = jnp.arange(tensor_size, dtype=jnp.int32) ^ tensor_at
        before = []
        moved = []
        width = 3 * GROUP
        whole_at = pl.BlockSpec((length, model), lambda g, chunks: (0, 0))
        turned_at = pl.BlockSpec((model, length), lambda g, chunks: (0, 0))
        half_at = pl.BlockSpec((half, width), lambda g, chunks: (0, g))
        for at in reversed(range(tensor_size)):
            hold = [moved[-2][1][0]] if len(moved) >= 2 else []

            def kernel(*refs, count=len(before), held=len(hold)):
                sums = refs[6 : 6 + count] if count else (None, None)
                mlp_kernel(*refs[:6], *sums, *refs[6 + count + held :])

            total, normed_grad, low_grad, high_grad = pl.pallas_call(
                kernel,
                grid_spec=pltpu.PrefetchScalarGridSpec(
                    num_scalar_prefetch=1,
                    grid=(mlp_groups,),
                    in_specs=[
                        whole_at, turned_at, whole_at, turned_at,
                        pl.BlockSpec((dp_size, 1, block_rows, width), lambda g, chunks, at=at: (0, chunks[at], 0, g)),
                    ] + [whole_at] * len(before) + [ANYWHERE] * len(hold),
                    out_specs=[whole_at, whole_at, half_at, half_at],
                    scratch_shapes=[
                        pltpu.VMEM((length, 2 * GROUP), f32), pltpu.VMEM((length, GROUP), bf16),
                        pltpu.VMEM((length, 2 * GROUP), bf16), pltpu.VMEM((length, GROUP), f32),
                    ],
                ),
                out_shape=[shaped(length, model), shaped(length, model)] + [shaped(half, 3 * hidden_chunk, kind=bf16)] * 2,
                compiler_params=PARAMS,
                name="mlp_kernel",
                cost_estimate=pl.CostEstimate(flops=SPANS["mlp_kernel"] * 1150 * 10**6, bytes_accessed=0, transcendentals=0),
            )(chunk_at, normed_two, normed_two_t, cotangent, cot_t, mlp_weights, *before, *hold)
            before = [total, normed_grad]
            moved.append(scatter_dp(low_grad, high_grad, orders[at % 2], block_rows))
        hidden_out, middle_grad, middle_low, middle_low_t, gain_two = call(
            middle_kernel, 1, [SCALARS, whole, whole, whole, whole, fixed((2, model))],
            [whole, whole, whole, turned, fixed((1, model))],
            [shaped(length, model, kind=bf16), shaped(length, model), shaped(length, model, kind=bf16), shaped(model, length, kind=bf16), shaped(1, model)],
            [pltpu.VMEM((length, model), bf16), pltpu.VMEM((length, model), f32), pltpu.VMEM((length, model), f32)],
            hold=[moved[2][1][0], moved[0][1][1]],
        )(places, middle, features(total), features(normed_grad), cot_low, gains)
        hidden_out = features(hidden_out, True)

        normed_grad = jnp.zeros((length, model), f32)
        backs = {}
        out_moved = {}
        back_holds = [
            [moved[3][1][0], moved[1][1][1]],
            [moved[2][1][1], moved[0][1][2]],
        ]
        backward = list(reversed(range(pairs)))
        for step, pair in enumerate(backward):
            low, high, _ = out_pairs[pair]
            gate_pre, states, mixed_low = mixed[pair]
            lanes = slice(pair * pair_width, (pair + 1) * pair_width)
            normed_grad, local, product, edge, low_grad, high_grad = call(
                mix_back_kernel,
                groups,
                [whole, turned, turned, lanes_of(half, 2 * GROUP), lanes_of(half, 2 * GROUP), lanes_of(length), lanes_of(length + 8), lanes_of(length), lanes_of(length), lanes_of(8), whole],
                [whole, lanes_of(length), lanes_of(length), lanes_of(8), lanes_of(half, 2 * GROUP), lanes_of(half, 2 * GROUP)],
                [shaped(length, model), shaped(length, pair_width), shaped(length, pair_width), shaped(8, pair_width), shaped(half, 2 * pair_width, kind=bf16), shaped(half, 2 * pair_width, kind=bf16)],
                [pltpu.VMEM((length, GROUP), f32), pltpu.VMEM((length, GROUP), f32), pltpu.VMEM((length, GROUP), bf16), pltpu.VMEM((length + 8, GROUP), f32)],
                hold=back_holds[step],
            )(middle_low, middle_low_t, normed_one_t, low, high, gate_pre, states, mixed_low, fed[pair][2], table[:, lanes], normed_grad)
            backs[pair] = (local, product, edge)
            out_moved[pair] = scatter_dp(low_grad, high_grad, orders[step % 2], block_rows)

        def separate(values):
            gate = [values[:, 2 * at * GROUP : (2 * at + 1) * GROUP] for at in range(groups)]
            out = [values[:, (2 * at + 1) * GROUP : (2 * at + 2) * GROUP] for at in range(groups)]
            gate, out = jnp.concatenate(gate, axis=1), jnp.concatenate(out, axis=1)
            return [jnp.concatenate([gate[:, :chunk], out[:, :chunk]], axis=1), jnp.concatenate([gate[:, chunk:], out[:, chunk:]], axis=1)]

        leave = exchange(
            jnp.concatenate([one[2][1:2] for _, one in sorted(backs.items())], axis=1),
            jnp.concatenate([one[2][0:1] for _, one in sorted(backs.items())], axis=1),
            True,
        )
        gate_backs = {}
        out_marks = [out_moved[pair][1] for pair in backward]
        gate_holds = [
            [moved[3][1][1], moved[1][1][2], out_marks[0][0]],
            [moved[2][1][2], out_marks[1][0]],
        ]
        for step, pair in enumerate(backward):
            part = slice(2 * pair * local_blocks, 2 * (pair + 1) * local_blocks)
            lanes = slice(pair * pair_width, (pair + 1) * pair_width)
            branch, conv_out, recur_open, inflow = fed[pair][:4]
            local, product, _ = backs[pair]
            gate_backs[pair] = (
                call(
                    gate_back_kernel,
                    groups,
                    [lanes_of(length), lanes_of(length), lanes_of(1), lanes_of(length + 8)] + [lanes_of(length)] * 3 + [lanes_of(full), blocks_of(), blocks_of(), lanes_of(8)],
                    [lanes_of(length), blocks_of(), blocks_of(), lanes_of(8)],
                    [shaped(length, pair_width), shaped(2 * local_blocks, BLOCK, BLOCK), shaped(2 * local_blocks, BLOCK, BLOCK), shaped(8, pair_width)],
                    [pltpu.VMEM((length, GROUP), bf16)] * 3,
                    hold=gate_holds[step],
                )(local, product, leave[:, lanes], mixed[pair][1], recur_open, inflow, conv_out, branch, rgates[part], igates[part], table[:, lanes])
            )
        gate_list = [gate_backs[pair] for pair in range(pairs)]
        heads = jnp.concatenate([one[0][:8] for one in gate_list], axis=1)
        heads = jnp.concatenate(relative(split_lanes(heads, tensor_size), tensor_at), axis=1)
        heads = lax.ppermute(heads, "tensor", [(at + 1, at) for at in range(tensor_size - 1)])
        after = jnp.concatenate(relative(split_lanes(heads, tensor_size), tensor_at), axis=1)
        rgrads = jnp.concatenate([one[1] for one in gate_list], axis=0)
        igrads = jnp.concatenate([one[2] for one in gate_list], axis=0)
        rows = jnp.concatenate([one[3] for one in gate_list], axis=1)
        decay_row = rows[3:4] * (8.0 * jax.nn.sigmoid(-decay_rates))
        rows = jnp.concatenate([rows[4:8], rows[0:3], decay_row], axis=0)
        if fast:
            def small_grads(*args, **sizes):
                small_grads_kernel(*args, sub=sub, local_blocks=local_blocks, chunks=tensor_size)
            small_own, small_other = call(
                small_grads, 1, [SCALARS, gate_spec, gate_spec, fixed((kinds, channels))], [small_spec, small_spec],
                [shaped(*small_spec.block_shape, kind=bf16)] * 2, [],
            )(places, rgrads, igrads, rows)
        else:
            gate_grads = jnp.stack([rgrads, igrads], axis=0).reshape(2, tensor_size, local_blocks, dp_size, sub, BLOCK)
            gate_grads = gate_grads.transpose(3, 0, 2, 4, 1, 5).reshape(dp_size, gate_rows, tensor_size * BLOCK)
            gate_grads = jnp.take(gate_grads, natural_at, axis=0)
            rows = rows.reshape(kinds, tensor_size, local_blocks, BLOCK).transpose(0, 2, 1, 3).reshape(1, vector_rows, -1)
            rest = small_rows - gate_rows - vector_rows
            pieces = [
                gate_grads,
                jnp.broadcast_to(rows, (dp_size,) + rows.shape[1:]),
                jnp.zeros((dp_size, rest, tensor_size * BLOCK), f32),
            ]
            small_grads = jnp.concatenate(pieces, axis=1).reshape(dp_size * small_rows, -1).astype(bf16)
            small_own, small_other = jnp.split(small_grads, 2, axis=0)
        small_sum, small_marks = scatter_dp(small_own, small_other, order_one, small_rows)

        in_parts = {}
        branch_holds = [
            [moved[3][1][2], out_marks[0][1], out_marks[1][1]],
            [out_marks[0][2], out_marks[1][2], small_marks[0]],
        ]
        for step, pair in enumerate(backward):
            low, high, _ = in_pairs[pair]
            lanes = slice(pair * pair_width, (pair + 1) * pair_width)
            normed_grad, low_grad, high_grad = call(
                branch_back_kernel,
                groups,
                [lanes_of(length), lanes_of(8), lanes_of(8), turned, lanes_of(half), lanes_of(half), whole],
                [whole, lanes_of(half), lanes_of(half)],
                [shaped(length, model), shaped(half, pair_width, kind=bf16), shaped(half, pair_width, kind=bf16)],
                [pltpu.VMEM((length + 8, GROUP), f32), pltpu.VMEM((length, GROUP), bf16)],
                hold=branch_holds[step],
            )(gate_backs[pair][0], after[:, lanes], table[:, lanes], normed_one_t, low, high, normed_grad)
            in_parts[pair] = scatter_dp(low_grad, high_grad, orders[step % 2], block_rows)
        final_holds = [small_marks[1], in_parts[backward[0]][1][0]]

        hidden_grad, gain_one = call(
            final_kernel, 1, [SCALARS, whole, whole, whole, fixed((2, model))], [whole, fixed((1, model))],
            [shaped(length, model), shaped(1, model)], [pltpu.VMEM((length, model), f32)],
            hold=final_holds,
        )(places, hidden_low, normed_grad, middle_grad, gains)
        in_sum, _ = join_tensor([part for pair in range(pairs) for part in split_lanes(in_parts[pair][0], 2)])

        late = [gain_one]
        mlp_columns = [[((3 * at + which) * GROUP, GROUP) for at in range(mlp_groups)] for which in range(3)]
        mlp_others = {tensor_size - 1 - step: one[0] for step, one in enumerate(moved[:-1])}
        mlp_grads = join_parts(moved[-1][0], mlp_others, mlp_columns, late)
        out_parts = [part for pair in range(pairs) for part in separate(out_moved[pair][0])]
        out_columns = [[(0, chunk)], [(chunk, chunk)]]
        gate_grad, out_grad = join_parts(out_parts[0], dict(enumerate(out_parts[1:], 1)), out_columns, late)

        gain_parts = jnp.concatenate([gain_one, gain_two], axis=0).reshape(2, dp_size, block_rows)
        if not fast:
            gain_parts = jnp.take(gain_parts, natural_at, axis=1)
        gain_parts = jnp.pad(gain_parts.transpose(1, 0, 2), ((0, 0), (0, 6), (0, BLOCK - block_rows)))
        gain_parts = gain_parts.reshape(8 * dp_size, BLOCK)
        gain_sum, _ = scatter_dp(gain_parts[: 4 * dp_size], gain_parts[4 * dp_size :], order_one, 8)
        gain_sum = sum(spread_tensor(gain_sum)[1:], gain_sum)
        gain_rows = block_rows // tensor_size
        gain_sum = lax.dynamic_slice(gain_sum, (0, tensor_at * gain_rows), (2, gain_rows)).T

        hidden_grad = features(hidden_grad, True)
        small_sum, _ = join_tensor(split_lanes(small_sum, tensor_size))

        gate_sum = small_sum[:gate_rows].reshape(2, local_blocks, sub, BLOCK).transpose(0, 2, 1, 3)
        vector_sum = lax.dynamic_slice(small_sum, (gate_rows, dp_at * sub), (vector_rows, sub))
        vector_sum = vector_sum.reshape(kinds, local_blocks, sub)

        return (
            hidden_out,
            hidden_grad,
            gain_sum,
            in_sum,
            gate_grad,
            out_grad,
            gate_sum[1],
            gate_sum[0],
            vector_sum[:CONV].transpose(2, 0, 1),
            vector_sum[4].T,
            vector_sum[5].T,
            vector_sum[6].T,
            vector_sum[7].T,
            mlp_grads[0],
            mlp_grads[1],
            mlp_grads[2],
        )

    return per_device


def solution(mesh):
    rows = P(("dp", "tensor"), None)
    matrix = P("dp", "tensor")
    gate = P("dp", "tensor", None)
    kernel = P("dp", None, "tensor")
    placed = (rows, rows, P("dp", None), matrix, matrix, matrix, gate, gate, kernel) + (matrix,) * 7
    made = (rows, rows, rows, matrix, matrix, matrix, gate, gate, kernel) + (matrix,) * 7
    return jax.shard_map(
        make_per_device(mesh.shape["dp"], mesh.shape["tensor"]),
        mesh=mesh,
        in_specs=placed,
        out_specs=made,
        check_vma=False,
    )
```

```python
import jax
import jax.numpy as jnp
from jax import lax
from jax.experimental import pallas as pl
from jax.experimental.pallas import tpu as pltpu
from jax.sharding import PartitionSpec as P

BLOCK = 128
CONV = 4
HALO = 16
TILE = 64
GROUP = 256
epsilon = 1e-06
f32 = jnp.float32
bf16 = jnp.bfloat16
ROOT = 0.7978845608028654
CUBIC = 0.044715


def nn(left, right):
    return lax.dot_general(left, right, (((1,), (0,)), ((), ())), preferred_element_type=f32)


def nt(left, right):
    return lax.dot_general(left, right, (((1,), (1,)), ((), ())), preferred_element_type=f32)


def tn(left, right):
    return lax.dot_general(left, right, (((0,), (0,)), ((), ())), preferred_element_type=f32)


def gelu_parts(value):
    square = value * value
    curve = jnp.tanh(ROOT * value * (1.0 + CUBIC * square))
    half = 0.5 * (1.0 + curve)
    slope = half + (0.5 * ROOT) * value * (1.0 - curve * curve) * (1.0 + 3.0 * CUBIC * square)
    return value * half, slope


def one_minus_exp(value):
    series = 1.0 + value * (1.0 / 7.0)
    for term in (6.0, 5.0, 4.0, 3.0, 2.0):
        series = 1.0 + value * (1.0 / term) * series
    return jnp.where(value > -0.25, -value * series, 1.0 - jnp.exp(value))


def scan_rows(decay_ref, drive_ref, offset, out_ref, out_offset, total_ref, length, reverse):
    width = drive_ref.shape[1]
    rows = lax.broadcasted_iota(jnp.int32, (8, width), 0)
    steps = length // 8

    def body(step, carry):
        state, product = carry
        at = (steps - 1 - step) if reverse else step
        start = pl.multiple_of(at * 8, 8)
        decay = decay_ref[pl.ds(start, 8 + 8 * (offset > 0)), :][offset : offset + 8]
        drive = drive_ref[pl.ds(start, 8), :]
        for shift in (1, 2, 4):
            if reverse:
                inside = rows < 8 - shift
                amount = 8 - shift
            else:
                inside = rows >= shift
                amount = shift
            drive = drive + decay * jnp.where(inside, pltpu.roll(drive, amount, 0), 0.0)
            decay = decay * jnp.where(inside, pltpu.roll(decay, amount, 0), 1.0)
        state = drive + decay * state
        product = decay * product
        out_ref[pl.ds(start + out_offset, 8), :] = state
        total_ref[pl.ds(start, 8), :] = product
        edge = 0 if reverse else 7
        return (
            jnp.broadcast_to(state[edge : edge + 1], (8, width)),
            jnp.broadcast_to(product[edge : edge + 1], (8, width)),
        )

    lax.fori_loop(0, steps, body, (jnp.zeros((8, width), f32), jnp.ones((8, width), f32)))


def tiles(length, body):
    def step(index, carry):
        body(pl.multiple_of(index * TILE, TILE))
        return carry

    lax.fori_loop(0, length // TILE, step, 0)


def mix_in_kernel(
    normed_ref, low_ref, high_ref, rgate_ref, igate_ref, table_ref,
    branch_ref, conv_ref, open_ref, flow_ref, local_ref, product_ref,
    conv_low, rec_buf, inp_buf, decay_buf,
):
    length = conv_ref.shape[0]
    half = low_ref.shape[0]
    branch_ref[...] = nn(normed_ref[:, :half], low_ref[...]) + nn(normed_ref[:, half:], high_ref[...])
    for part in range(GROUP // BLOCK):
        lanes = slice(part * BLOCK, (part + 1) * BLOCK)

        def convolve(start):
            window = branch_ref[pl.ds(start + HALO - 8, TILE + 8), lanes]
            result = table_ref[4:5, lanes] + table_ref[0:1, lanes] * window[8:]
            for offset in range(1, CONV):
                result = result + table_ref[offset : offset + 1, lanes] * window[8 - offset : 8 - offset + TILE]
            conv_ref[pl.ds(start, TILE), lanes] = result
            conv_low[pl.ds(start, TILE), lanes] = result.astype(bf16)

        tiles(length, convolve)
        rec_buf[:, lanes] = nn(conv_low[:, lanes], rgate_ref[part])
        inp_buf[:, lanes] = nn(conv_low[:, lanes], igate_ref[part])

        def gates(start):
            rows = pl.ds(start, TILE)
            recur_open = jax.nn.sigmoid(rec_buf[rows, lanes] + table_ref[6:7, lanes])
            inflow = jax.nn.sigmoid(inp_buf[rows, lanes] + table_ref[5:6, lanes])
            log_decay = recur_open * table_ref[7:8, lanes]
            multiplier = jnp.sqrt(one_minus_exp(2.0 * log_decay))
            open_ref[rows, lanes] = recur_open
            flow_ref[rows, lanes] = inflow
            decay_buf[rows, lanes] = jnp.exp(log_decay)
            rec_buf[rows, lanes] = multiplier * inflow * conv_ref[rows, lanes]

        tiles(length, gates)
    scan_rows(decay_buf, rec_buf, 0, local_ref, 0, product_ref, length, False)


def mix_out_kernel(
    normed_ref, low_ref, high_ref, local_ref, product_ref, enter_ref, sum_ref,
    pre_ref, states_ref, mixed_ref, total_ref,
):
    length = local_ref.shape[0]
    half = low_ref.shape[0]

    @pl.when(pl.program_id(0) == 0)
    def _():
        total_ref[...] = sum_ref[...]

    pre_ref[...] = nn(normed_ref[HALO:, :half], low_ref[:, :GROUP]) + nn(normed_ref[HALO:, half:], high_ref[:, :GROUP])
    states_ref[0:8, :] = jnp.broadcast_to(enter_ref[0:1, :], (8, GROUP))
    for part in range(GROUP // BLOCK):
        lanes = slice(part * BLOCK, (part + 1) * BLOCK)

        def mix(start):
            rows = pl.ds(start, TILE)
            states = local_ref[rows, lanes] + product_ref[rows, lanes] * enter_ref[0:1, lanes]
            states_ref[pl.ds(start + 8, TILE), lanes] = states
            gate = pre_ref[rows, lanes]
            curve = jnp.tanh(ROOT * gate * (1.0 + CUBIC * gate * gate))
            mixed_ref[rows, lanes] = (states * (gate * (0.5 * (1.0 + curve)))).astype(bf16)

        tiles(length, mix)
    total_ref[:, :half] += nt(mixed_ref[...], low_ref[:, GROUP:])
    total_ref[:, half:] += nt(mixed_ref[...], high_ref[:, GROUP:])


def mlp_kernel(
    chunks_ref, normed_ref, normed_t_ref, cot_ref, cot_t_ref, weights_ref, sum_ref, back_ref,
    total_ref, grad_ref, low_grad_ref, high_grad_ref,
    pre, hidden, pre_low, act,
):
    length, model = normed_ref.shape
    half = model // 2
    first = sum_ref is None

    @pl.when(pl.program_id(0) == 0)
    def _():
        if first:
            total_ref[...] = jnp.zeros_like(total_ref)
            grad_ref[...] = jnp.zeros_like(grad_ref)
        else:
            total_ref[...] = sum_ref[...]
            grad_ref[...] = back_ref[...]

    weights = weights_ref[...].reshape(model, 3 * GROUP)
    pre[...] = nn(normed_ref[...], weights[:, : 2 * GROUP])
    act[...] = nn(cot_ref[...], weights[:, 2 * GROUP :])
    for part in range(GROUP // BLOCK):
        lanes = slice(part * BLOCK, (part + 1) * BLOCK)
        up_lanes = slice(GROUP + part * BLOCK, GROUP + (part + 1) * BLOCK)

        def activate(start):
            rows = pl.ds(start, TILE)
            value, slope = gelu_parts(pre[rows, lanes])
            up = pre[rows, up_lanes]
            grad = act[rows, lanes]
            hidden[rows, lanes] = (value * up).astype(bf16)
            pre_low[rows, lanes] = (grad * up * slope).astype(bf16)
            pre_low[rows, up_lanes] = (grad * value).astype(bf16)

        tiles(length, activate)
    total_ref[...] += nt(hidden[...], weights[:, 2 * GROUP :])
    grad_ref[...] += nt(pre_low[...], weights[:, : 2 * GROUP])
    low_grad_ref[:, : 2 * GROUP] = nn(normed_t_ref[:half], pre_low[...]).astype(bf16)
    high_grad_ref[:, : 2 * GROUP] = nn(normed_t_ref[half:], pre_low[...]).astype(bf16)
    low_grad_ref[:, 2 * GROUP :] = nn(cot_t_ref[:half], hidden[...]).astype(bf16)
    high_grad_ref[:, 2 * GROUP :] = nn(cot_t_ref[half:], hidden[...]).astype(bf16)


def lane_block(index):
    return pl.ds(pl.multiple_of(index * BLOCK, BLOCK), BLOCK)


def order_kernel(places_ref, hidden_ref, cot_ref, hidden_out_ref, cot_out_ref, cot_t_ref):
    for place in range(hidden_ref.shape[1] // BLOCK):
        lanes = slice(place * BLOCK, (place + 1) * BLOCK)
        hidden_out_ref[:, lanes] = hidden_ref[:, lane_block(places_ref[place])]
        cot_out_ref[:, lanes] = cot_ref[:, lane_block(places_ref[place])]
    cot_t_ref[...] = cot_out_ref[...].T


def row_loop(length, rows, body, start):
    def step(index, carry):
        return body(pl.ds(pl.multiple_of(index * rows, rows), rows), carry)

    return lax.fori_loop(0, length // rows, step, start)


def scale_of(values):
    return lax.rsqrt(jnp.mean(values * values, axis=1, keepdims=True) + epsilon)


def norm_kernel(places_ref, hidden_ref, first_ref, gains_ref, normed_ref, normed_t_ref, first_buf):
    length = hidden_ref.shape[0]
    for place in range(hidden_ref.shape[1] // BLOCK):
        lanes = slice(place * BLOCK, (place + 1) * BLOCK)
        first_buf[:, lanes] = first_ref[:, lane_block(places_ref[place])].astype(f32)
    first = first_buf[...]
    normed_ref[:HALO, :] = (first * scale_of(first) * gains_ref[0:1, :]).astype(bf16)

    def body(rows, carry):
        values = hidden_ref[rows, :].astype(f32)
        normed_ref[pl.ds(rows.start + HALO, rows.size), :] = (values * scale_of(values) * gains_ref[0:1, :]).astype(bf16)
        return carry

    row_loop(length, 16, body, 0)
    normed_t_ref[...] = normed_ref[HALO:, :].T


def second_norm_kernel(places_ref, middle_ref, gains_ref, normed_ref, normed_t_ref, buffer):
    length, model = middle_ref.shape

    def body(rows, carry):
        values = middle_ref[rows, :]
        buffer[rows, :] = (values * scale_of(values) * gains_ref[1:2, :]).astype(bf16)
        return carry

    row_loop(length, 16, body, 0)
    normed_t_ref[...] = buffer[...].T
    for place in range(model // BLOCK):
        normed_ref[:, lane_block(places_ref[place])] = buffer[:, place * BLOCK : (place + 1) * BLOCK]


def norm_back(values, grad, gain):
    scale = scale_of(values)
    unit = values * scale
    scaled = grad * gain
    return scale * (scaled - unit * jnp.mean(scaled * unit, axis=1, keepdims=True)), grad * unit


def fold_rows(value):
    rows, width = value.shape
    return jnp.sum(value.reshape(rows // 8, 8, width), axis=0)


def middle_kernel(
    places_ref, middle_ref, total_ref, grad_ref, cot_ref, gains_ref,
    out_ref, middle_grad_ref, low_ref, low_t_ref, gain_ref, buffer, own_total, own_grad,
):
    length, model = middle_ref.shape
    for place in range(model // BLOCK):
        lanes = slice(place * BLOCK, (place + 1) * BLOCK)
        own_total[:, lanes] = total_ref[:, lane_block(places_ref[place])]
        own_grad[:, lanes] = grad_ref[:, lane_block(places_ref[place])]

    def body(rows, carry):
        middle = middle_ref[rows, :]
        change, part = norm_back(middle, own_grad[rows, :], gains_ref[1:2, :])
        middle_grad = cot_ref[rows, :].astype(f32) + change
        middle_grad_ref[rows, :] = middle_grad
        low_ref[rows, :] = middle_grad.astype(bf16)
        buffer[rows, :] = (middle + own_total[rows, :]).astype(bf16)
        return carry + fold_rows(part)

    total = row_loop(length, 16, body, jnp.zeros((8, model), f32))
    gain_ref[...] = jnp.sum(total, axis=0, keepdims=True)
    low_t_ref[...] = low_ref[...].T
    for place in range(model // BLOCK):
        out_ref[:, lane_block(places_ref[place])] = buffer[:, place * BLOCK : (place + 1) * BLOCK]


def final_kernel(places_ref, hidden_ref, grad_ref, middle_grad_ref, gains_ref, out_ref, gain_ref, buffer):
    length, model = hidden_ref.shape

    def body(rows, carry):
        change, part = norm_back(hidden_ref[rows, :].astype(f32), grad_ref[rows, :], gains_ref[0:1, :])
        buffer[rows, :] = middle_grad_ref[rows, :] + change
        return carry + fold_rows(part)

    total = row_loop(length, 16, body, jnp.zeros((8, model), f32))
    gain_ref[...] = jnp.sum(total, axis=0, keepdims=True)
    for place in range(model // BLOCK):
        out_ref[:, lane_block(places_ref[place])] = buffer[:, place * BLOCK : (place + 1) * BLOCK]


def tables_kernel(places_ref, *refs, sub, local_blocks, chunks):
    sources, (rgate_ref, igate_ref, table_ref, gains_ref) = refs[:-4], refs[-4:]
    rows_each = 2 * local_blocks * sub
    kinds = 2 * CONV
    count = places_ref.shape[0]
    size = sources[0].shape[0] * 2 // count
    sums = [jnp.zeros((kinds * local_blocks, BLOCK), f32)] * chunks
    for place in range(count):
        side = place // (count // 2)
        top = (place % (count // 2)) * size
        natural = places_ref[place]
        for at in range(chunks):
            source = sources[at // 2 * 2 + side]
            lanes = slice(at % 2 * BLOCK, (at % 2 + 1) * BLOCK)
            for which, gate_ref in enumerate((rgate_ref, igate_ref)):
                for block in range(local_blocks):
                    start = top + (which * local_blocks + block) * sub
                    gate_ref[at * local_blocks + block, pl.ds(pl.multiple_of(natural * sub, sub), sub), :] = source[start : start + sub, lanes]
            sums[at] = sums[at] + source[top + rows_each : top + rows_each + kinds * local_blocks, lanes].astype(f32)
        start = top + rows_each + kinds * local_blocks
        gains_ref[:, place * BLOCK : (place + 1) * BLOCK] = sources[side][start : start + 2, :BLOCK].astype(f32)
    for at in range(chunks):
        for block in range(local_blocks):
            column = (at * local_blocks + block) * BLOCK
            for kind in range(kinds):
                row = kind * local_blocks + block
                table_ref[kind : kind + 1, column : column + BLOCK] = sums[at][row : row + 1]


def small_grads_kernel(places_ref, rgrad_ref, igrad_ref, sums_ref, *targets, sub, local_blocks, chunks):
    kinds = 2 * CONV
    rows_each = 2 * local_blocks * sub
    count = places_ref.shape[0]
    size = targets[0].shape[0] * 2 // count
    spare = size - rows_each - kinds * local_blocks
    vectors = []
    for at in range(chunks):
        rows = []
        for kind in range(kinds):
            for block in range(local_blocks):
                column = (at * local_blocks + block) * BLOCK
                rows.append(sums_ref[kind : kind + 1, column : column + BLOCK])
        vectors.append(jnp.concatenate(rows, axis=0))
    for place in range(count):
        side = place // (count // 2)
        top = (place % (count // 2)) * size
        natural = places_ref[place]
        for at in range(chunks):
            target = targets[at // 2 * 2 + side]
            lanes = slice(at % 2 * BLOCK, (at % 2 + 1) * BLOCK)
            for which, grad_ref in enumerate((rgrad_ref, igrad_ref)):
                for block in range(local_blocks):
                    start = top + (which * local_blocks + block) * sub
                    target[start : start + sub, lanes] = grad_ref[
                        at * local_blocks + block, pl.ds(pl.multiple_of(natural * sub, sub), sub), :
                    ].astype(bf16)
            rest = jnp.concatenate([vectors[at], jnp.zeros((spare, BLOCK), f32)], axis=0)
            target[top + rows_each : top + size, lanes] = rest.astype(bf16)


def mix_back_kernel(
    grad_low_ref, grad_t_ref, normed_t_ref, low_ref, high_ref, pre_ref, states_ref, mixed_ref, open_ref, table_ref, sum_ref,
    total_ref, local_ref, product_ref, edge_ref, low_grad_ref, high_grad_ref,
    mixed_grad, drive, pre_low, decay_buf,
):
    length = pre_ref.shape[0]
    half = low_ref.shape[0]

    @pl.when(pl.program_id(0) == 0)
    def _():
        total_ref[...] = sum_ref[...]

    mixed_grad[...] = nn(grad_low_ref[:, :half], low_ref[:, GROUP:]) + nn(grad_low_ref[:, half:], high_ref[:, GROUP:])
    decay_buf[pl.ds(length, 8), :] = jnp.ones((8, GROUP), f32)
    for part in range(GROUP // BLOCK):
        lanes = slice(part * BLOCK, (part + 1) * BLOCK)

        def back(start):
            rows = pl.ds(start, TILE)
            value, slope = gelu_parts(pre_ref[rows, lanes])
            grad = mixed_grad[rows, lanes]
            pre_low[rows, lanes] = (grad * states_ref[pl.ds(start + 8, TILE), lanes] * slope).astype(bf16)
            drive[rows, lanes] = grad * value
            decay_buf[rows, lanes] = jnp.exp(open_ref[rows, lanes] * table_ref[7:8, lanes])

        tiles(length, back)
    scan_rows(decay_buf, drive, 1, local_ref, 0, product_ref, length, True)
    edge_ref[0:1, :] = decay_buf[0:1, :] * local_ref[0:1, :]
    edge_ref[1:2, :] = decay_buf[0:1, :] * product_ref[0:1, :]
    total_ref[:, :half] += nt(pre_low[...], low_ref[:, :GROUP])
    total_ref[:, half:] += nt(pre_low[...], high_ref[:, :GROUP])
    low_grad_ref[:, :GROUP] = nn(normed_t_ref[:half], pre_low[...]).astype(bf16)
    high_grad_ref[:, :GROUP] = nn(normed_t_ref[half:], pre_low[...]).astype(bf16)
    low_grad_ref[:, GROUP:] = nn(grad_t_ref[:half], mixed_ref[...]).astype(bf16)
    high_grad_ref[:, GROUP:] = nn(grad_t_ref[half:], mixed_ref[...]).astype(bf16)


def gate_back_kernel(
    local_ref, product_ref, enter_ref, states_ref, open_ref, flow_ref, conv_ref, branch_ref, rgate_ref, igate_ref, table_ref,
    conv_grad_ref, rgrad_ref, igrad_ref, sums_ref,
    rec_low, inp_low, conv_low,
):
    length = local_ref.shape[0]
    for part in range(GROUP // BLOCK):
        lanes = slice(part * BLOCK, (part + 1) * BLOCK)

        def back(index, sums):
            start = pl.multiple_of(index * TILE, TILE)
            rows = pl.ds(start, TILE)
            carried = local_ref[rows, lanes] + product_ref[rows, lanes] * enter_ref[0:1, lanes]
            recur_open = open_ref[rows, lanes]
            inflow = flow_ref[rows, lanes]
            conv_out = conv_ref[rows, lanes]
            rate = table_ref[7:8, lanes]
            log_decay = recur_open * rate
            decay = jnp.exp(log_decay)
            multiplier = jnp.sqrt(one_minus_exp(2.0 * log_decay))
            before = states_ref[pl.ds(start, TILE + 8), lanes][7 : 7 + TILE]
            weighted = carried * inflow
            decay_grad = carried * before * decay - weighted * conv_out * decay * decay / multiplier
            scaled = decay_grad * recur_open
            rec_grad = rate * scaled * (1.0 - recur_open)
            direct = weighted * multiplier
            inp_grad = direct * conv_out * (1.0 - inflow)
            rec_low[rows, lanes] = rec_grad.astype(bf16)
            inp_low[rows, lanes] = inp_grad.astype(bf16)
            conv_low[rows, lanes] = conv_out.astype(bf16)
            conv_grad_ref[rows, lanes] = direct

            def fold(value):
                return jnp.sum(value.reshape(TILE // 8, 8, BLOCK), axis=0)

            return (sums[0] + fold(rec_grad), sums[1] + fold(inp_grad), sums[2] + fold(scaled))

        zero = jnp.zeros((8, BLOCK), f32)
        sums = lax.fori_loop(0, length // TILE, back, (zero, zero, zero))
        for row, value in zip((2, 1, 3), sums):
            sums_ref[row : row + 1, lanes] = jnp.sum(value, axis=0, keepdims=True)
        rgrad_ref[part] = tn(conv_low[:, lanes], rec_low[:, lanes])
        igrad_ref[part] = tn(conv_low[:, lanes], inp_low[:, lanes])
        conv_grad_ref[:, lanes] += nt(rec_low[:, lanes], rgate_ref[part]) + nt(inp_low[:, lanes], igate_ref[part])

        def taps(index, sums):
            start = pl.multiple_of(index * TILE, TILE)
            grad = conv_grad_ref[pl.ds(start, TILE), lanes]

            def fold(value):
                return jnp.sum(value.reshape(TILE // 8, 8, BLOCK), axis=0)

            window = branch_ref[pl.ds(start + HALO - 8, TILE + 8), lanes]
            new = [sums[0] + fold(grad)]
            for offset in range(CONV):
                new.append(sums[offset + 1] + fold(grad * window[8 - offset : 8 - offset + TILE]))
            return tuple(new)

        sums = lax.fori_loop(0, length // TILE, taps, (zero,) * (CONV + 1))
        for row, value in zip((0, 4, 5, 6, 7), sums):
            sums_ref[row : row + 1, lanes] = jnp.sum(value, axis=0, keepdims=True)


def branch_back_kernel(
    conv_grad_ref, after_ref, table_ref, normed_t_ref, low_ref, high_ref, sum_ref, small_refs,
    total_ref, low_grad_ref, high_grad_ref,
    padded, branch_low, *, groups,
):
    length = conv_grad_ref.shape[0]
    half = low_ref.shape[0]

    @pl.when(pl.program_id(0) == 0)
    def _():
        total_ref[...] = sum_ref[...]

    @pl.when(pl.program_id(0) < groups)
    def _():
        padded[pl.ds(0, length), :] = conv_grad_ref[...]
        padded[pl.ds(length, 8), :] = after_ref[...]
        for part in range(GROUP // BLOCK):
            lanes = slice(part * BLOCK, (part + 1) * BLOCK)

            def back(start):
                window = padded[pl.ds(start, TILE + 8), lanes]
                result = table_ref[0:1, lanes] * window[:TILE]
                for offset in range(1, CONV):
                    result = result + table_ref[offset : offset + 1, lanes] * window[offset : offset + TILE]
                branch_low[pl.ds(start, TILE), lanes] = result.astype(bf16)

            tiles(length, back)
        total_ref[:, :half] += nt(branch_low[...], low_ref[...])
        total_ref[:, half:] += nt(branch_low[...], high_ref[...])
        low_grad_ref[...] = nn(normed_t_ref[:half], branch_low[...]).astype(bf16)
        high_grad_ref[...] = nn(normed_t_ref[half:], branch_low[...]).astype(bf16)

    if small_refs:

        @pl.when(pl.program_id(0) == groups)
        def _():
            low_grad_ref[...] = small_refs[0][...]
            high_grad_ref[...] = small_refs[1][...]


def join_kernel(*refs, columns):
    parts, outs = refs[: -len(columns)], refs[-len(columns) :]
    for out_ref, places in zip(outs, columns):
        to = 0
        for start, size in places:
            total = parts[0][:, start : start + size].astype(f32)
            for part in parts[1:]:
                total = total + part[:, start : start + size].astype(f32)
            out_ref[:, to : to + size] = total
            to += size


def fixed(shape):
    return pl.BlockSpec(shape, lambda g: (0,) * len(shape))


def lanes_until(rows, last):
    return pl.BlockSpec((rows, GROUP), lambda g: (0, jnp.minimum(g, last)))


def lanes_of(rows, width=GROUP):
    return pl.BlockSpec((rows, width), lambda g: (0, g))


def blocks_of():
    return pl.BlockSpec((GROUP // BLOCK, BLOCK, BLOCK), lambda g: (g, 0, 0))


def shaped(*dims, kind=f32):
    return jax.ShapeDtypeStruct(dims, kind)


PARAMS = pltpu.CompilerParams(dimension_semantics=("arbitrary",), vmem_limit_bytes=56 * 1024 * 1024)


ANYWHERE = pl.BlockSpec(memory_space=pl.ANY)
SCALARS = pl.BlockSpec(memory_space=pltpu.SMEM)


SPANS = {
    "order_kernel": 4, "tables_of": 2, "norm_kernel": 6, "mix_in_kernel": 14, "mix_out_kernel": 10,
    "second_norm_kernel": 6, "mlp_kernel": 17, "middle_kernel": 12, "mix_back_kernel": 18, "gate_back_kernel": 11,
    "branch_back": 8, "final_kernel": 10, "small_grads": 3, "join": 2,
}


def call(kernel, steps, in_specs, out_specs, out_shape, scratch, hold=()):
    count = len(in_specs)
    name = getattr(kernel, "func", kernel).__name__

    def body(*refs):
        kernel(*refs[:count], *refs[count + len(hold) :])

    run = pl.pallas_call(
        body,
        grid=(steps,),
        in_specs=list(in_specs) + [ANYWHERE] * len(hold),
        out_specs=out_specs,
        out_shape=out_shape,
        scratch_shapes=scratch,
        compiler_params=PARAMS,
        name=name,
        cost_estimate=pl.CostEstimate(flops=SPANS[name] * 1150 * 10**6, bytes_accessed=0, transcendentals=0),
    )
    return lambda *args: run(*args, *hold)


def make_per_device(dp_size, tensor_size):
    pairs = tensor_size // 2
    dp_bits = [1 << bit for bit in range(dp_size.bit_length() - 1)]
    order_one = dp_bits[1:] + dp_bits[:1]
    order_two = dp_bits[2:3] + dp_bits[1:2] + dp_bits[3:] + dp_bits[:1]
    orders = (order_one, order_two)
    position_of = {bit: place for place, bit in enumerate(order_one)}

    def swap_dp(values, bit):
        return lax.ppermute(values, "dp", [(at, at ^ bit) for at in range(dp_size)])

    def swap_tensor(values, bit):
        return lax.ppermute(values, "tensor", [(at, at ^ bit) for at in range(tensor_size)])

    def relative(pieces, index):
        bit = 1
        while bit < len(pieces):
            flag = (index & bit) != 0
            pieces = [jnp.where(flag, pieces[at ^ bit], piece) for at, piece in enumerate(pieces)]
            bit *= 2
        return pieces

    place_index = [
        sum(bit for bit in dp_bits if place & (1 << position_of[bit])) for place in range(dp_size)
    ]

    def split_lanes(values, count):
        width = values.shape[1] // count
        return [values[:, at * width : (at + 1) * width] for at in range(count)]

    class Gather:
        def __init__(self, values, order):
            self.rows, self.left, self.done = values.shape[0], list(order), []
            self.send(values)

        def send(self, values):
            self.values, self.bit = values, self.left.pop(0)
            self.received = swap_dp(values, self.bit)

        def take(self, received):
            if not self.left:
                self.received, self.last = None, received
                return
            values, rows = self.values, self.rows
            if all(position_of[other] < position_of[self.bit] for other in self.done):
                values = jnp.concatenate([values, received], axis=0)
            else:
                pieces = []
                for at in range(0, values.shape[0], rows):
                    pieces += [values[at : at + rows], received[at : at + rows]]
                values = jnp.concatenate(pieces, axis=0)
            self.done.append(self.bit)
            self.send(values)

        def finish(self):
            while self.received is not None:
                self.take(self.received)
            return self.values, self.last

    def round_of(travellers, *others):
        travellers = [one for one in travellers if one.received is not None]
        found = lax.optimization_barrier(tuple(one.received for one in travellers) + others)
        for one, received in zip(travellers, found):
            one.take(received)
        return list(found[len(travellers) :])

    def add(one, two):
        return (one.astype(f32) + two.astype(f32)).astype(one.dtype)

    class Scatter:
        def __init__(self, own, other, order, block_rows):
            self.left, self.block_rows = list(order[:-1]), block_rows
            self.values, self.received = own, swap_dp(other, order[-1])

        def halves(self, values, bit):
            rows = values.shape[0]
            if all(position_of[other] < position_of[bit] for other in self.left):
                return values[: rows // 2], values[rows // 2 :]
            starts = range(0, rows, self.block_rows)
            pieces = [values[at : at + self.block_rows] for at in starts]
            return jnp.concatenate(pieces[0::2], axis=0), jnp.concatenate(pieces[1::2], axis=0)

        def step(self, token=None):
            received = self.received
            if token is not None:
                received, token = lax.optimization_barrier((received, token))
            self.take(received)
            return token

        def take(self, received):
            if self.left:
                bit = self.left.pop()
                keep, send = self.halves(self.values, bit)
                keep_more, send_more = self.halves(received, bit)
                sent = add(send, send_more)
                self.values, self.received = add(keep, keep_more), swap_dp(sent, bit)
                self.mark = sent
            else:
                self.values, self.received = add(self.values, received), None
                self.mark = self.values

        def finish(self):
            while self.received is not None:
                self.step()
            return self.values

    def steps(scatters, token):
        for one in scatters:
            if one.received is not None:
                token = one.step(token)
        return token, [one.mark for one in scatters]

    def spread_tensor(values):
        return [values] + [swap_tensor(values, other) for other in range(1, tensor_size)]

    def join_parts(own, others, columns, hold):
        parts = [own] + [others[other] for other in range(1, tensor_size)]

        def join(*refs):
            join_kernel(*refs, columns=columns)

        rows = own.shape[0]
        widths = [sum(size for _, size in places) for places in columns]
        return call(
            join, 1, [fixed(own.shape)] * tensor_size, [fixed((rows, width)) for width in widths],
            [shaped(rows, width) for width in widths], [], hold=hold,
        )(*parts)

    def join_tensor(parts):
        total = parts[0].astype(f32)
        received = []
        for other in range(1, tensor_size):
            received.append(swap_tensor(parts[other], other))
            total = total + received[-1].astype(f32)
        return total, received

    def per_device(
        hidden_in, cotangent, norm_gains, mixer_in, branch_gate, mixer_out, input_gate, recur_gate,
        conv_kernel, conv_bias, input_bias, recur_bias, decay_param, mlp_gate, mlp_up, mlp_down,
    ):
        dp_at = lax.axis_index("dp")
        tensor_at = lax.axis_index("tensor")
        length, model = hidden_in.shape
        block_rows, chunk = mixer_in.shape
        half = model // 2
        hidden_chunk = mlp_gate.shape[1]
        sub = block_rows * BLOCK // model
        local_blocks = chunk // BLOCK
        pair_width = 2 * chunk
        groups = pair_width // GROUP
        mlp_groups = hidden_chunk // GROUP
        fast = block_rows == BLOCK and sub % 16 == 0
        natural_at = jnp.array(place_index, jnp.int32) ^ dp_at
        places = natural_at if fast else jnp.arange(model // BLOCK, dtype=jnp.int32)

        def features(values, back=False):
            if fast:
                return values
            pieces = jnp.stack(split_lanes(values, dp_size), axis=0)
            order = natural_at
            if back:
                order = jnp.zeros_like(natural_at).at[natural_at].set(jnp.arange(dp_size, dtype=jnp.int32))
            return jnp.concatenate(list(jnp.take(pieces, order, axis=0)), axis=1)

        first_rows = lax.ppermute(
            hidden_in[length - HALO :], "tensor", [(at, at + 1) for at in range(tensor_size - 1)]
        )

        def rows_first(table):
            return table.transpose(1, 0, 2).reshape(-1, BLOCK)

        vectors = jnp.concatenate(
            [conv_kernel.transpose(1, 2, 0).reshape(-1, sub)]
            + [table.T for table in (conv_bias, input_bias, recur_bias, decay_param)],
            axis=0,
        )
        owner = lax.broadcasted_iota(jnp.int32, (1, BLOCK), 1) // sub
        vectors = jnp.where(owner == dp_at, jnp.tile(vectors, (1, BLOCK // sub)), jnp.zeros((), bf16))
        gate_rows = 2 * local_blocks * sub
        vector_rows = vectors.shape[0]
        small_rows = (gate_rows + vector_rows + 2 + 15) // 16 * 16
        small = jnp.concatenate(
            [
                rows_first(recur_gate),
                rows_first(input_gate),
                vectors,
                jnp.pad(norm_gains.T, ((0, 0), (0, BLOCK - block_rows))),
                jnp.zeros((small_rows - gate_rows - vector_rows - 2, BLOCK), bf16),
            ],
            axis=0,
        )
        merged = fast and small_rows == block_rows

        def in_pairs_of(found):
            return [
                jnp.concatenate([one[:, :chunk], two[:, :chunk], one[:, chunk:], two[:, chunk:]], axis=1) if merged
                else jnp.concatenate([one, two], axis=1)
                for one, two in zip(found[0::2], found[1::2])
            ]

        def interleave(one, two):
            gate = jnp.concatenate([one[:, :chunk], two[:, :chunk]], axis=1)
            out = jnp.concatenate([one[:, chunk:], two[:, chunk:]], axis=1)
            pieces = []
            for at in range(groups):
                pieces += [gate[:, at * GROUP : (at + 1) * GROUP], out[:, at * GROUP : (at + 1) * GROUP]]
            return jnp.concatenate(pieces, axis=1)

        in_near = spread_tensor(jnp.concatenate([mixer_in, small], axis=1) if merged else mixer_in)
        found = lax.optimization_barrier(tuple(in_near[1:]) + (branch_gate, mixer_out))
        in_near[1:] = found[:-2]
        in_gathers = [Gather(values, orders[at % 2]) for at, values in enumerate(in_pairs_of(in_near))]
        out_near = spread_tensor(jnp.concatenate(found[-2:], axis=1))
        out_near[1:] = round_of(in_gathers, *out_near[1:])
        out_gathers = [
            Gather(interleave(one, two), orders[at % 2]) for at, (one, two) in enumerate(zip(out_near[0::2], out_near[1::2]))
        ]
        round_of(in_gathers + out_gathers)
        in_pairs = [one.finish() for one in in_gathers]
        if not merged:
            small_low, small_high = Gather(jnp.concatenate(spread_tensor(small), axis=1), order_one).finish()
        mlp_pieces = []
        for at in range(mlp_groups):
            mlp_pieces += [w[:, at * GROUP : (at + 1) * GROUP] for w in (mlp_gate, mlp_up, mlp_down)]
        mlp_weights = lax.all_gather(jnp.concatenate(mlp_pieces, axis=1), ("dp", "tensor"), axis=0, tiled=False)
        mlp_weights = mlp_weights.reshape(dp_size, tensor_size, block_rows, 3 * hidden_chunk)

        whole = fixed((length, model))
        turned = fixed((model, length))
        hidden_low, cot_low, cot_t = call(
            order_kernel, 1, [SCALARS, whole, whole], [whole, whole, turned],
            [shaped(length, model, kind=bf16), shaped(length, model, kind=bf16), shaped(model, length, kind=bf16)], [],
        )(places, features(hidden_in), features(cotangent))

        kinds = 2 * CONV
        channels = tensor_size * chunk
        blocks = tensor_size * local_blocks
        if merged:
            small_spec = pl.BlockSpec((half, 2 * BLOCK), lambda g: (0, pair_width // (2 * BLOCK)))
            gate_spec = fixed((blocks, BLOCK, BLOCK))
            def tables_of(*args, **sizes):
                tables_kernel(*args, sub=sub, local_blocks=local_blocks, chunks=tensor_size)
            rgates, igates, table, gains = call(
                tables_of, 1, [SCALARS] + [small_spec] * tensor_size, [gate_spec, gate_spec, fixed((kinds, channels)), fixed((2, model))],
                [shaped(blocks, BLOCK, BLOCK, kind=bf16), shaped(blocks, BLOCK, BLOCK, kind=bf16), shaped(kinds, channels), shaped(2, model)], [],
            )(places, *[values for pair in in_pairs for values in pair])
        else:
            stacked = jnp.concatenate([small_low, small_high], axis=0).reshape(dp_size, small_rows, -1)
            order = jnp.zeros_like(natural_at).at[natural_at].set(jnp.arange(dp_size, dtype=jnp.int32))
            gates = jnp.take(stacked[:, :gate_rows], order, axis=0).reshape(dp_size, 2, local_blocks, sub, tensor_size, BLOCK)
            gates = gates.transpose(1, 4, 2, 0, 3, 5).reshape(2, blocks, BLOCK, BLOCK)
            rgates, igates = gates[0], gates[1]
            table = jnp.sum(stacked[:, gate_rows : gate_rows + vector_rows].astype(f32), axis=0)
            table = table.reshape(kinds, local_blocks, tensor_size, BLOCK).transpose(0, 2, 1, 3).reshape(kinds, channels)
            gains = stacked[:, gate_rows + vector_rows : gate_rows + vector_rows + 2, :block_rows]
            gains = gains.transpose(1, 0, 2).reshape(2, model).astype(f32)
        decay_rates = table[7:8]
        table = jnp.concatenate([table[:7], -8.0 * jax.nn.softplus(-decay_rates)], axis=0)

        full = length + HALO
        normed_one, normed_one_t = call(
            norm_kernel, 1, [SCALARS, whole, fixed((HALO, model)), fixed((2, model))], [fixed((full, model)), turned],
            [shaped(full, model, kind=bf16), shaped(model, length, kind=bf16)], [pltpu.VMEM((HALO, model), f32)],
        )(places, hidden_low, features(first_rows), gains)

        fed = []
        hold = []
        for pair in range(pairs):
            low, high = in_pairs[pair]
            part = slice(2 * pair * local_blocks, 2 * (pair + 1) * local_blocks)
            lanes = slice(pair * pair_width, (pair + 1) * pair_width)
            fed.append(
                call(
                    mix_in_kernel,
                    groups,
                    [fixed((full, model)), lanes_of(half), lanes_of(half), blocks_of(), blocks_of(), lanes_of(8)],
                    [lanes_of(full)] + [lanes_of(length)] * 5,
                    [shaped(full, pair_width)] + [shaped(length, pair_width)] * 5,
                    [pltpu.VMEM((length, GROUP), bf16)] + [pltpu.VMEM((length, GROUP), f32)] * 3,
                    hold=hold,
                )(normed_one, low, high, rgates[part], igates[part], table[:, lanes])
            )
            fed[pair] = list(fed[pair])
            fed[pair][5:] = round_of(out_gathers, fed[pair][5])
            hold = [fed[pair][5]] + [one.values for one in out_gathers]
        out_pairs = [one.finish() for one in out_gathers]

        def exchange(products, ends, later):
            mine = jnp.concatenate([products, ends], axis=0)
            found = [mine]
            for other in range(1, tensor_size):
                pieces = split_lanes(swap_tensor(mine, other), tensor_size)
                found.append(jnp.concatenate([pieces[at ^ other] for at in range(tensor_size)], axis=1))
            found = relative(found, tensor_at)
            state = jnp.zeros_like(ends)
            turn = range(tensor_size - 1, 0, -1) if later else range(tensor_size - 1)
            for at in turn:
                use = (at > tensor_at) if later else (at < tensor_at)
                state = jnp.where(use, found[at][0:1] * state + found[at][1:2], state)
            return state

        enter = exchange(
            jnp.concatenate([one[5][length - 1 :] for one in fed], axis=1),
            jnp.concatenate([one[4][length - 1 :] for one in fed], axis=1),
            False,
        )
        middle = hidden_low.astype(f32)
        mixed = []
        for pair in range(pairs):
            low, high = out_pairs[pair]
            lanes = slice(pair * pair_width, (pair + 1) * pair_width)
            gate_pre, states, mixed_low, middle = call(
                mix_out_kernel,
                groups,
                [fixed((full, model)), lanes_of(half, 2 * GROUP), lanes_of(half, 2 * GROUP), lanes_of(length), lanes_of(length), lanes_of(1), whole],
                [lanes_of(length), lanes_of(length + 8), lanes_of(length), whole],
                [shaped(length, pair_width), shaped(length + 8, pair_width), shaped(length, pair_width, kind=bf16), shaped(length, model)],
                [],
            )(normed_one, low, high, fed[pair][4], fed[pair][5], enter[:, lanes], middle)
            mixed.append((gate_pre, states, mixed_low))
        normed_two, normed_two_t = call(
            second_norm_kernel, 1, [SCALARS, whole, fixed((2, model))], [whole, turned],
            [shaped(length, model, kind=bf16), shaped(model, length, kind=bf16)], [pltpu.VMEM((length, model), bf16)],
        )(places, middle, gains)
        normed_two = features(normed_two, True)

        chunk_at = jnp.arange(tensor_size, dtype=jnp.int32) ^ tensor_at
        before = []
        moved = []
        width = 3 * GROUP
        whole_at = pl.BlockSpec((length, model), lambda g, chunks: (0, 0))
        turned_at = pl.BlockSpec((model, length), lambda g, chunks: (0, 0))
        half_at = pl.BlockSpec((half, width), lambda g, chunks: (0, g))
        for at in reversed(range(tensor_size)):
            hold = []
            if len(moved) >= 2:
                before[0], hold = steps([moved[-2]], before[0])

            def kernel(*refs, count=len(before), held=len(hold)):
                sums = refs[6 : 6 + count] if count else (None, None)
                mlp_kernel(*refs[:6], *sums, *refs[6 + count + held :])

            total, normed_grad, low_grad, high_grad = pl.pallas_call(
                kernel,
                grid_spec=pltpu.PrefetchScalarGridSpec(
                    num_scalar_prefetch=1,
                    grid=(mlp_groups,),
                    in_specs=[
                        whole_at, turned_at, whole_at, turned_at,
                        pl.BlockSpec((dp_size, 1, block_rows, width), lambda g, chunks, at=at: (0, chunks[at], 0, g)),
                    ] + [whole_at] * len(before) + [ANYWHERE] * len(hold),
                    out_specs=[whole_at, whole_at, half_at, half_at],
                    scratch_shapes=[
                        pltpu.VMEM((length, 2 * GROUP), f32), pltpu.VMEM((length, GROUP), bf16),
                        pltpu.VMEM((length, 2 * GROUP), bf16), pltpu.VMEM((length, GROUP), f32),
                    ],
                ),
                out_shape=[shaped(length, model), shaped(length, model)] + [shaped(half, 3 * hidden_chunk, kind=bf16)] * 2,
                compiler_params=PARAMS,
                name="mlp_kernel",
                cost_estimate=pl.CostEstimate(flops=SPANS["mlp_kernel"] * 1150 * 10**6, bytes_accessed=0, transcendentals=0),
            )(chunk_at, normed_two, normed_two_t, cotangent, cot_t, mlp_weights, *before, *hold)
            before = [total, normed_grad]
            moved.append(Scatter(low_grad, high_grad, orders[at % 2], block_rows))
        total, hold = steps([moved[2]], total)
        hidden_out, middle_grad, middle_low, middle_low_t, gain_two = call(
            middle_kernel, 1, [SCALARS, whole, whole, whole, whole, fixed((2, model))],
            [whole, whole, whole, turned, fixed((1, model))],
            [shaped(length, model, kind=bf16), shaped(length, model), shaped(length, model, kind=bf16), shaped(model, length, kind=bf16), shaped(1, model)],
            [pltpu.VMEM((length, model), bf16), pltpu.VMEM((length, model), f32), pltpu.VMEM((length, model), f32)],
            hold=hold,
        )(places, middle, features(total), features(normed_grad), cot_low, gains)
        hidden_out = features(hidden_out, True)

        normed_grad = jnp.zeros((length, model), f32)
        backs = {}
        out_moved = {}
        gain_two, marks = steps([moved[3], moved[0]], gain_two)
        hold = [gain_two] + marks
        backward = list(reversed(range(pairs)))
        for step, pair in enumerate(backward):
            low, high = out_pairs[pair]
            gate_pre, states, mixed_low = mixed[pair]
            lanes = slice(pair * pair_width, (pair + 1) * pair_width)
            normed_grad, local, product, edge, low_grad, high_grad = call(
                mix_back_kernel,
                groups,
                [whole, turned, turned, lanes_of(half, 2 * GROUP), lanes_of(half, 2 * GROUP), lanes_of(length), lanes_of(length + 8), lanes_of(length), lanes_of(length), lanes_of(8), whole],
                [whole, lanes_of(length), lanes_of(length), lanes_of(8), lanes_of(half, 2 * GROUP), lanes_of(half, 2 * GROUP)],
                [shaped(length, model), shaped(length, pair_width), shaped(length, pair_width), shaped(8, pair_width), shaped(half, 2 * pair_width, kind=bf16), shaped(half, 2 * pair_width, kind=bf16)],
                [pltpu.VMEM((length, GROUP), f32), pltpu.VMEM((length, GROUP), f32), pltpu.VMEM((length, GROUP), bf16), pltpu.VMEM((length + 8, GROUP), f32)],
                hold=hold,
            )(middle_low, middle_low_t, normed_one_t, low, high, gate_pre, states, mixed_low, fed[pair][2], table[:, lanes], normed_grad)
            out_moved[pair] = Scatter(low_grad, high_grad, orders[step % 2], block_rows)
            if step == 0:
                edge, marks = steps([moved[1], moved[0]], edge)
                hold = [edge] + marks
            else:
                edge, _ = steps([moved[1]], edge)
            backs[pair] = (local, product, edge)

        def separate(values):
            gate = [values[:, 2 * at * GROUP : (2 * at + 1) * GROUP] for at in range(groups)]
            out = [values[:, (2 * at + 1) * GROUP : (2 * at + 2) * GROUP] for at in range(groups)]
            gate, out = jnp.concatenate(gate, axis=1), jnp.concatenate(out, axis=1)
            return [jnp.concatenate([gate[:, :chunk], out[:, :chunk]], axis=1), jnp.concatenate([gate[:, chunk:], out[:, chunk:]], axis=1)]

        leave = exchange(
            jnp.concatenate([one[2][1:2] for _, one in sorted(backs.items())], axis=1),
            jnp.concatenate([one[2][0:1] for _, one in sorted(backs.items())], axis=1),
            True,
        )
        gate_backs = {}
        mlp_others = {}

        def send_along(step, token):
            other = tensor_size - 1 - step
            values, token = lax.optimization_barrier((moved[step].finish(), token))
            mlp_others[other] = swap_tensor(values, other)
            return token

        leave, hold = steps([moved[2], out_moved[backward[0]]], leave)
        leave = send_along(0, leave)
        for step, pair in enumerate(backward):
            part = slice(2 * pair * local_blocks, 2 * (pair + 1) * local_blocks)
            lanes = slice(pair * pair_width, (pair + 1) * pair_width)
            branch, conv_out, recur_open, inflow = fed[pair][:4]
            local, product, _ = backs[pair]
            gate_backs[pair] = list(
                call(
                    gate_back_kernel,
                    groups,
                    [lanes_of(length), lanes_of(length), lanes_of(1), lanes_of(length + 8)] + [lanes_of(length)] * 3 + [lanes_of(full), blocks_of(), blocks_of(), lanes_of(8)],
                    [lanes_of(length), blocks_of(), blocks_of(), lanes_of(8)],
                    [shaped(length, pair_width), shaped(2 * local_blocks, BLOCK, BLOCK), shaped(2 * local_blocks, BLOCK, BLOCK), shaped(8, pair_width)],
                    [pltpu.VMEM((length, GROUP), bf16)] * 3,
                    hold=hold,
                )(local, product, leave[:, lanes], mixed[pair][1], recur_open, inflow, conv_out, branch, rgates[part], igates[part], table[:, lanes])
            )
            if step == 0:
                token, marks = steps([moved[3], out_moved[backward[1]]], gate_backs[pair][3])
                hold = [token] + marks
                gate_backs[pair][3] = token
            else:
                gate_backs[pair][3], hold = steps([moved[2]], gate_backs[pair][3])
        gate_list = [gate_backs[pair] for pair in range(pairs)]
        heads = jnp.concatenate([one[0][:8] for one in gate_list], axis=1)
        heads = jnp.concatenate(relative(split_lanes(heads, tensor_size), tensor_at), axis=1)
        heads = lax.ppermute(heads, "tensor", [(at + 1, at) for at in range(tensor_size - 1)])
        after = jnp.concatenate(relative(split_lanes(heads, tensor_size), tensor_at), axis=1)
        mlp_others[tensor_size - 1], after = lax.optimization_barrier((mlp_others[tensor_size - 1], after))
        after = send_along(2, send_along(1, after))
        after, marks = steps([out_moved[backward[0]]], after)
        hold = hold + marks
        rgrads = jnp.concatenate([one[1] for one in gate_list], axis=0)
        igrads = jnp.concatenate([one[2] for one in gate_list], axis=0)
        rows = jnp.concatenate([one[3] for one in gate_list], axis=1)
        decay_row = rows[3:4] * (8.0 * jax.nn.sigmoid(-decay_rates))
        rows = jnp.concatenate([rows[4:8], rows[0:3], decay_row], axis=0)
        small_low, small_high = [], []
        if merged:
            small_target = fixed((half, 2 * BLOCK))

            def small_grads(*args, **sizes):
                small_grads_kernel(*args, sub=sub, local_blocks=local_blocks, chunks=tensor_size)
            small_halves = call(
                small_grads, 1, [SCALARS, gate_spec, gate_spec, fixed((kinds, channels))], [small_target] * tensor_size,
                [shaped(half, 2 * BLOCK, kind=bf16)] * tensor_size, [], hold=hold,
            )(places, rgrads, igrads, rows)
            small_low, small_high = small_halves[0::2], small_halves[1::2]
        else:
            gate_grads = jnp.stack([rgrads, igrads], axis=0).reshape(2, tensor_size, local_blocks, dp_size, sub, BLOCK)
            gate_grads = gate_grads.transpose(3, 0, 2, 4, 1, 5).reshape(dp_size, gate_rows, tensor_size * BLOCK)
            gate_grads = jnp.take(gate_grads, natural_at, axis=0)
            rows = rows.reshape(kinds, tensor_size, local_blocks, BLOCK).transpose(0, 2, 1, 3).reshape(1, vector_rows, -1)
            rest = small_rows - gate_rows - vector_rows
            pieces = [
                gate_grads,
                jnp.broadcast_to(rows, (dp_size,) + rows.shape[1:]),
                jnp.zeros((dp_size, rest, tensor_size * BLOCK), f32),
            ]
            small_grads = jnp.concatenate(pieces, axis=1).reshape(dp_size * small_rows, -1).astype(bf16)
            small_own, small_other = jnp.split(small_grads, 2, axis=0)
        if not merged:
            small_moved = Scatter(small_own, small_other, order_one, small_rows)

        in_parts = {}
        for step, pair in enumerate(backward):
            low, high = in_pairs[pair]
            lanes = slice(pair * pair_width, (pair + 1) * pair_width)
            smalls = [small_low[pair], small_high[pair]] if merged else []
            moved_width = pair_width + 2 * BLOCK * merged

            def branch_back(*refs, count=len(smalls)):
                branch_back_kernel(*refs[:7], refs[7 : 7 + count], *refs[7 + count :], groups=groups)

            last = groups - 1
            normed_grad, low_grad, high_grad = call(
                branch_back,
                moved_width // GROUP,
                [lanes_until(length, last), lanes_until(8, last), lanes_until(8, last), turned, lanes_until(half, last), lanes_until(half, last), whole]
                + [fixed((half, GROUP))] * len(smalls),
                [whole, lanes_of(half), lanes_of(half)],
                [shaped(length, model), shaped(half, moved_width, kind=bf16), shaped(half, moved_width, kind=bf16)],
                [pltpu.VMEM((length + 8, GROUP), f32), pltpu.VMEM((length, GROUP), bf16)],
                hold=hold,
            )(gate_backs[pair][0], after[:, lanes], table[:, lanes], normed_one_t, low, high, normed_grad, *smalls)
            in_parts[pair] = Scatter(low_grad, high_grad, orders[step % 2], block_rows)
            if step == 0:
                normed_grad, hold = steps([moved[3], out_moved[backward[1]], out_moved[backward[0]]], normed_grad)
            else:
                normed_grad, hold = steps([out_moved[backward[1]], in_parts[backward[0]]], normed_grad)

        hidden_grad, gain_one = call(
            final_kernel, 1, [SCALARS, whole, whole, whole, fixed((2, model))], [whole, fixed((1, model))],
            [shaped(length, model), shaped(1, model)], [pltpu.VMEM((length, model), f32)],
            hold=hold,
        )(places, hidden_low, normed_grad, middle_grad, gains)
        in_list = [in_parts[pair] for pair in backward]
        gain_one, = round_of(in_list, gain_one)
        late = [gain_one]
        gain_parts = jnp.concatenate([gain_one, gain_two], axis=0).reshape(2, dp_size, block_rows)
        if not fast:
            gain_parts = jnp.take(gain_parts, natural_at, axis=1)
        gain_parts = jnp.pad(gain_parts.transpose(1, 0, 2), ((0, 0), (0, 6), (0, BLOCK - block_rows)))
        gain_parts = gain_parts.reshape(8 * dp_size, BLOCK)
        gains_moved = Scatter(gain_parts[: 4 * dp_size], gain_parts[4 * dp_size :], order_one, 8)
        out_parts = [part for pair in range(pairs) for part in separate(out_moved[pair].finish())]
        out_others = {other: swap_tensor(out_parts[other], other) for other in range(tensor_size - 1, 0, -1)}
        mlp_columns = [[((3 * at + which) * GROUP, GROUP) for at in range(mlp_groups)] for which in range(3)]
        mlp_grads = join_parts(moved[-1].finish(), mlp_others, mlp_columns, late)
        far, near = out_others[tensor_size - 1], out_others[tensor_size - 2]
        far, near = round_of(in_list + [gains_moved], far, near)
        out_others.update({tensor_size - 1: far, tensor_size - 2: near})
        round_of([one for one in in_list] + [gains_moved])
        out_columns = [[(0, chunk)], [(chunk, chunk)]]
        gate_grad, out_grad = join_parts(out_parts[0], out_others, out_columns, late)

        def in_chunks(values):
            if not merged:
                return split_lanes(values, 2)
            one, two = values[:, :chunk], values[:, chunk:pair_width]
            small_one, small_two = split_lanes(values[:, pair_width:], 2)
            return [jnp.concatenate([one, small_one], axis=1), jnp.concatenate([two, small_two], axis=1)]

        in_sum, in_far = join_tensor([part for pair in range(pairs) for part in in_chunks(in_parts[pair].finish())])
        gain_sum = gains_moved.finish()
        gain_sum = sum(spread_tensor(gain_sum)[1:], gain_sum)
        gain_rows = block_rows // tensor_size
        gain_sum = lax.dynamic_slice(gain_sum, (0, tensor_at * gain_rows), (2, gain_rows)).T

        hidden_grad = features(hidden_grad, True)
        if merged:
            in_sum, small_sum = in_sum[:, :chunk], in_sum[:, chunk:]
        else:
            small_sum, _ = join_tensor(split_lanes(small_moved.finish(), tensor_size))

        gate_sum = small_sum[:gate_rows].reshape(2, local_blocks, sub, BLOCK).transpose(0, 2, 1, 3)
        vector_sum = lax.dynamic_slice(small_sum, (gate_rows, dp_at * sub), (vector_rows, sub))
        vector_sum = vector_sum.reshape(kinds, local_blocks, sub)

        return (
            hidden_out,
            hidden_grad,
            gain_sum,
            in_sum,
            gate_grad,
            out_grad,
            gate_sum[1],
            gate_sum[0],
            vector_sum[:CONV].transpose(2, 0, 1),
            vector_sum[4].T,
            vector_sum[5].T,
            vector_sum[6].T,
            vector_sum[7].T,
            mlp_grads[0],
            mlp_grads[1],
            mlp_grads[2],
        )

    return per_device


def solution(mesh):
    rows = P(("dp", "tensor"), None)
    matrix = P("dp", "tensor")
    gate = P("dp", "tensor", None)
    kernel = P("dp", None, "tensor")
    placed = (rows, rows, P("dp", None), matrix, matrix, matrix, gate, gate, kernel) + (matrix,) * 7
    made = (rows, rows, rows, matrix, matrix, matrix, gate, gate, kernel) + (matrix,) * 7
    return jax.shard_map(
        make_per_device(mesh.shape["dp"], mesh.shape["tensor"]),
        mesh=mesh,
        in_specs=placed,
        out_specs=made,
        check_vma=False,
    )
```

```python
import jax
import jax.numpy as jnp
from jax import lax
from jax.experimental import pallas as pl
from jax.experimental.pallas import tpu as pltpu
from jax.sharding import PartitionSpec as P

BLOCK = 128
CONV = 4
HALO = 16
TILE = 64
GROUP = 256
ROWS = 32
epsilon = 1e-06
f32 = jnp.float32
bf16 = jnp.bfloat16
ROOT = 0.7978845608028654
CUBIC = 0.044715


def nn(left, right):
    return lax.dot_general(left, right, (((1,), (0,)), ((), ())), preferred_element_type=f32)


def nt(left, right):
    return lax.dot_general(left, right, (((1,), (1,)), ((), ())), preferred_element_type=f32)


def tn(left, right):
    return lax.dot_general(left, right, (((0,), (0,)), ((), ())), preferred_element_type=f32)


def gelu_parts(value):
    square = value * value
    curve = jnp.tanh(ROOT * value * (1.0 + CUBIC * square))
    half = 0.5 * (1.0 + curve)
    slope = half + (0.5 * ROOT) * value * (1.0 - curve * curve) * (1.0 + 3.0 * CUBIC * square)
    return value * half, slope


def one_minus_exp(value):
    series = 1.0 + value * (1.0 / 7.0)
    for term in (6.0, 5.0, 4.0, 3.0, 2.0):
        series = 1.0 + value * (1.0 / term) * series
    return jnp.where(value > -0.25, -value * series, 1.0 - jnp.exp(value))


def scan_rows(decay_ref, drive_ref, offset, out_ref, out_offset, total_ref, length, reverse):
    width = drive_ref.shape[1]
    rows = lax.broadcasted_iota(jnp.int32, (8, width), 0)
    steps = length // 8

    def body(step, carry):
        state, product = carry
        at = (steps - 1 - step) if reverse else step
        start = pl.multiple_of(at * 8, 8)
        decay = decay_ref[pl.ds(start, 8 + 8 * (offset > 0)), :][offset : offset + 8]
        drive = drive_ref[pl.ds(start, 8), :]
        for shift in (1, 2, 4):
            if reverse:
                inside = rows < 8 - shift
                amount = 8 - shift
            else:
                inside = rows >= shift
                amount = shift
            drive = drive + decay * jnp.where(inside, pltpu.roll(drive, amount, 0), 0.0)
            decay = decay * jnp.where(inside, pltpu.roll(decay, amount, 0), 1.0)
        state = drive + decay * state
        product = decay * product
        out_ref[pl.ds(start + out_offset, 8), :] = state
        total_ref[pl.ds(start, 8), :] = product
        edge = 0 if reverse else 7
        return (
            jnp.broadcast_to(state[edge : edge + 1], (8, width)),
            jnp.broadcast_to(product[edge : edge + 1], (8, width)),
        )

    lax.fori_loop(0, steps, body, (jnp.zeros((8, width), f32), jnp.ones((8, width), f32)))


def tiles(length, body):
    def step(index, carry):
        body(pl.multiple_of(index * TILE, TILE))
        return carry

    lax.fori_loop(0, length // TILE, step, 0)


def mix_in_kernel(
    normed_ref, low_ref, high_ref, rgate_ref, igate_ref, table_ref,
    branch_ref, conv_ref, open_ref, flow_ref, local_ref, product_ref,
    conv_low, rec_buf, inp_buf, decay_buf,
):
    length = conv_ref.shape[0]
    half = low_ref.shape[0]
    branch_ref[...] = nn(normed_ref[:, :half], low_ref[...]) + nn(normed_ref[:, half:], high_ref[...])
    for part in range(GROUP // BLOCK):
        lanes = slice(part * BLOCK, (part + 1) * BLOCK)

        def convolve(start):
            window = branch_ref[pl.ds(start + HALO - 8, TILE + 8), lanes]
            result = table_ref[4:5, lanes] + table_ref[0:1, lanes] * window[8:]
            for offset in range(1, CONV):
                result = result + table_ref[offset : offset + 1, lanes] * window[8 - offset : 8 - offset + TILE]
            conv_ref[pl.ds(start, TILE), lanes] = result
            conv_low[pl.ds(start, TILE), lanes] = result.astype(bf16)

        tiles(length, convolve)
        rec_buf[:, lanes] = nn(conv_low[:, lanes], rgate_ref[part])
        inp_buf[:, lanes] = nn(conv_low[:, lanes], igate_ref[part])

        def gates(start):
            rows = pl.ds(start, TILE)
            recur_open = jax.nn.sigmoid(rec_buf[rows, lanes] + table_ref[6:7, lanes])
            inflow = jax.nn.sigmoid(inp_buf[rows, lanes] + table_ref[5:6, lanes])
            log_decay = recur_open * table_ref[7:8, lanes]
            multiplier = jnp.sqrt(one_minus_exp(2.0 * log_decay))
            open_ref[rows, lanes] = recur_open
            flow_ref[rows, lanes] = inflow
            decay_buf[rows, lanes] = jnp.exp(log_decay)
            rec_buf[rows, lanes] = multiplier * inflow * conv_ref[rows, lanes]

        tiles(length, gates)
    scan_rows(decay_buf, rec_buf, 0, local_ref, 0, product_ref, length, False)


def mix_out_kernel(
    normed_ref, low_ref, high_ref, local_ref, product_ref, enter_ref, sum_ref,
    pre_ref, states_ref, mixed_ref, total_ref,
):
    length = local_ref.shape[0]
    half = low_ref.shape[0]

    @pl.when(pl.program_id(0) == 0)
    def _():
        total_ref[...] = sum_ref[...].astype(f32)

    pre_ref[...] = nn(normed_ref[HALO:, :half], low_ref[:, :GROUP]) + nn(normed_ref[HALO:, half:], high_ref[:, :GROUP])
    states_ref[0:8, :] = jnp.broadcast_to(enter_ref[0:1, :], (8, GROUP))
    for part in range(GROUP // BLOCK):
        lanes = slice(part * BLOCK, (part + 1) * BLOCK)

        def mix(start):
            rows = pl.ds(start, TILE)
            states = local_ref[rows, lanes] + product_ref[rows, lanes] * enter_ref[0:1, lanes]
            states_ref[pl.ds(start + 8, TILE), lanes] = states
            gate = pre_ref[rows, lanes]
            curve = jnp.tanh(ROOT * gate * (1.0 + CUBIC * gate * gate))
            mixed_ref[rows, lanes] = (states * (gate * (0.5 * (1.0 + curve)))).astype(bf16)

        tiles(length, mix)
    total_ref[:, :half] += nt(mixed_ref[...], low_ref[:, GROUP:])
    total_ref[:, half:] += nt(mixed_ref[...], high_ref[:, GROUP:])


def mlp_kernel(
    chunks_ref, normed_ref, normed_t_ref, cot_ref, cot_t_ref, gate_ref, up_ref, down_ref, sum_ref, back_ref,
    total_ref, grad_ref, low_grad_ref, high_grad_ref,
    pre, hidden, pre_low, act,
):
    length, model = normed_ref.shape
    half = model // 2
    first = sum_ref is None

    @pl.when(pl.program_id(0) == 0)
    def _():
        if first:
            total_ref[...] = jnp.zeros_like(total_ref)
            grad_ref[...] = jnp.zeros_like(grad_ref)
        else:
            total_ref[...] = sum_ref[...]
            grad_ref[...] = back_ref[...]

    gate = gate_ref[...].reshape(model, GROUP)
    up_weights = up_ref[...].reshape(model, GROUP)
    down = down_ref[...].reshape(model, GROUP)
    pre[:, :GROUP] = nn(normed_ref[...], gate)
    pre[:, GROUP:] = nn(normed_ref[...], up_weights)
    act[...] = nn(cot_ref[...], down)
    for part in range(GROUP // BLOCK):
        lanes = slice(part * BLOCK, (part + 1) * BLOCK)
        up_lanes = slice(GROUP + part * BLOCK, GROUP + (part + 1) * BLOCK)

        def activate(start):
            rows = pl.ds(start, TILE)
            value, slope = gelu_parts(pre[rows, lanes])
            up = pre[rows, up_lanes]
            grad = act[rows, lanes]
            hidden[rows, lanes] = (value * up).astype(bf16)
            pre_low[rows, lanes] = (grad * up * slope).astype(bf16)
            pre_low[rows, up_lanes] = (grad * value).astype(bf16)

        tiles(length, activate)
    total_ref[...] += nt(hidden[...], down)
    grad_ref[...] += nt(pre_low[:, :GROUP], gate) + nt(pre_low[:, GROUP:], up_weights)
    low_grad_ref[:, : 2 * GROUP] = nn(normed_t_ref[:half], pre_low[...]).astype(bf16)
    high_grad_ref[:, : 2 * GROUP] = nn(normed_t_ref[half:], pre_low[...]).astype(bf16)
    low_grad_ref[:, 2 * GROUP :] = nn(cot_t_ref[:half], hidden[...]).astype(bf16)
    high_grad_ref[:, 2 * GROUP :] = nn(cot_t_ref[half:], hidden[...]).astype(bf16)


def lane_block(index):
    return pl.ds(pl.multiple_of(index * BLOCK, BLOCK), BLOCK)


def order_kernel(places_ref, hidden_ref, cot_ref, hidden_out_ref, cot_out_ref, cot_t_ref):
    for place in range(hidden_ref.shape[1] // BLOCK):
        lanes = slice(place * BLOCK, (place + 1) * BLOCK)
        hidden_out_ref[:, lanes] = hidden_ref[:, lane_block(places_ref[place])]
        cot_out_ref[:, lanes] = cot_ref[:, lane_block(places_ref[place])]
    cot_t_ref[...] = cot_out_ref[...].T


def row_loop(length, rows, body, start):
    def step(index, carry):
        return body(pl.ds(pl.multiple_of(index * rows, rows), rows), carry)

    return lax.fori_loop(0, length // rows, step, start)


def scale_of(values):
    return lax.rsqrt(jnp.mean(values * values, axis=1, keepdims=True) + epsilon)


def norm_kernel(places_ref, hidden_ref, first_ref, gains_ref, normed_ref, normed_t_ref, first_buf):
    length = hidden_ref.shape[0]
    for place in range(hidden_ref.shape[1] // BLOCK):
        lanes = slice(place * BLOCK, (place + 1) * BLOCK)
        first_buf[:, lanes] = first_ref[:, lane_block(places_ref[place])].astype(f32)
    first = first_buf[...]
    normed_ref[:HALO, :] = (first * scale_of(first) * gains_ref[0:1, :]).astype(bf16)

    def body(rows, carry):
        values = hidden_ref[rows, :].astype(f32)
        normed_ref[pl.ds(rows.start + HALO, rows.size), :] = (values * scale_of(values) * gains_ref[0:1, :]).astype(bf16)
        return carry

    row_loop(length, ROWS, body, 0)
    normed_t_ref[...] = normed_ref[HALO:, :].T


def second_norm_kernel(places_ref, middle_ref, gains_ref, normed_ref, normed_t_ref, buffer):
    length, model = middle_ref.shape

    def body(rows, carry):
        values = middle_ref[rows, :]
        buffer[rows, :] = (values * scale_of(values) * gains_ref[1:2, :]).astype(bf16)
        return carry

    row_loop(length, ROWS, body, 0)
    normed_t_ref[...] = buffer[...].T
    for place in range(model // BLOCK):
        normed_ref[:, lane_block(places_ref[place])] = buffer[:, place * BLOCK : (place + 1) * BLOCK]


def norm_back(values, grad, gain):
    scale = scale_of(values)
    unit = values * scale
    scaled = grad * gain
    return scale * (scaled - unit * jnp.mean(scaled * unit, axis=1, keepdims=True)), grad * unit


def fold_rows(value):
    rows, width = value.shape
    return jnp.sum(value.reshape(rows // 8, 8, width), axis=0)


def middle_kernel(
    places_ref, middle_ref, total_ref, grad_ref, cot_ref, gains_ref,
    out_ref, middle_grad_ref, low_ref, low_t_ref, gain_ref, buffer, own_total, own_grad,
):
    length, model = middle_ref.shape
    for place in range(model // BLOCK):
        lanes = slice(place * BLOCK, (place + 1) * BLOCK)
        own_total[:, lanes] = total_ref[:, lane_block(places_ref[place])]
        own_grad[:, lanes] = grad_ref[:, lane_block(places_ref[place])]

    def body(rows, carry):
        middle = middle_ref[rows, :]
        change, part = norm_back(middle, own_grad[rows, :], gains_ref[1:2, :])
        middle_grad = cot_ref[rows, :].astype(f32) + change
        middle_grad_ref[rows, :] = middle_grad
        low_ref[rows, :] = middle_grad.astype(bf16)
        buffer[rows, :] = (middle + own_total[rows, :]).astype(bf16)
        return carry + fold_rows(part)

    total = row_loop(length, ROWS, body, jnp.zeros((8, model), f32))
    gain_ref[...] = jnp.sum(total, axis=0, keepdims=True)
    low_t_ref[...] = low_ref[...].T
    for place in range(model // BLOCK):
        out_ref[:, lane_block(places_ref[place])] = buffer[:, place * BLOCK : (place + 1) * BLOCK]


def final_kernel(places_ref, hidden_ref, grad_ref, middle_grad_ref, gains_ref, out_ref, gain_ref, buffer):
    length, model = hidden_ref.shape

    def body(rows, carry):
        change, part = norm_back(hidden_ref[rows, :].astype(f32), grad_ref[rows, :], gains_ref[0:1, :])
        buffer[rows, :] = middle_grad_ref[rows, :] + change
        return carry + fold_rows(part)

    total = row_loop(length, ROWS, body, jnp.zeros((8, model), f32))
    gain_ref[...] = jnp.sum(total, axis=0, keepdims=True)
    for place in range(model // BLOCK):
        out_ref[:, lane_block(places_ref[place])] = buffer[:, place * BLOCK : (place + 1) * BLOCK]


def tables_kernel(places_ref, *refs, sub, local_blocks, chunks):
    sources, (rgate_ref, igate_ref, table_ref, gains_ref) = refs[:-4], refs[-4:]
    rows_each = 2 * local_blocks * sub
    kinds = 2 * CONV
    count = places_ref.shape[0]
    size = sources[0].shape[0] * 2 // count
    sums = [jnp.zeros((kinds * local_blocks, BLOCK), f32)] * chunks
    for place in range(count):
        side = place // (count // 2)
        top = (place % (count // 2)) * size
        natural = places_ref[place]
        for at in range(chunks):
            source = sources[at // 2 * 2 + side]
            lanes = slice(at % 2 * BLOCK, (at % 2 + 1) * BLOCK)
            for which, gate_ref in enumerate((rgate_ref, igate_ref)):
                for block in range(local_blocks):
                    start = top + (which * local_blocks + block) * sub
                    gate_ref[at * local_blocks + block, pl.ds(pl.multiple_of(natural * sub, sub), sub), :] = source[start : start + sub, lanes]
            sums[at] = sums[at] + source[top + rows_each : top + rows_each + kinds * local_blocks, lanes].astype(f32)
        start = top + rows_each + kinds * local_blocks
        gains_ref[:, place * BLOCK : (place + 1) * BLOCK] = sources[side][start : start + 2, :BLOCK].astype(f32)
    for at in range(chunks):
        for block in range(local_blocks):
            column = (at * local_blocks + block) * BLOCK
            for kind in range(kinds):
                row = kind * local_blocks + block
                table_ref[kind : kind + 1, column : column + BLOCK] = sums[at][row : row + 1]


def small_grads_kernel(places_ref, rgrad_ref, igrad_ref, sums_ref, *targets, sub, local_blocks, chunks):
    kinds = 2 * CONV
    rows_each = 2 * local_blocks * sub
    count = places_ref.shape[0]
    size = targets[0].shape[0] * 2 // count
    spare = size - rows_each - kinds * local_blocks
    vectors = []
    for at in range(chunks):
        rows = []
        for kind in range(kinds):
            for block in range(local_blocks):
                column = (at * local_blocks + block) * BLOCK
                rows.append(sums_ref[kind : kind + 1, column : column + BLOCK])
        vectors.append(jnp.concatenate(rows, axis=0))
    for place in range(count):
        side = place // (count // 2)
        top = (place % (count // 2)) * size
        natural = places_ref[place]
        for at in range(chunks):
            target = targets[at // 2 * 2 + side]
            lanes = slice(at % 2 * BLOCK, (at % 2 + 1) * BLOCK)
            for which, grad_ref in enumerate((rgrad_ref, igrad_ref)):
                for block in range(local_blocks):
                    start = top + (which * local_blocks + block) * sub
                    target[start : start + sub, lanes] = grad_ref[
                        at * local_blocks + block, pl.ds(pl.multiple_of(natural * sub, sub), sub), :
                    ].astype(bf16)
            rest = jnp.concatenate([vectors[at], jnp.zeros((spare, BLOCK), f32)], axis=0)
            target[top + rows_each : top + size, lanes] = rest.astype(bf16)


def mix_back_kernel(
    grad_low_ref, grad_t_ref, normed_t_ref, low_ref, high_ref, pre_ref, states_ref, mixed_ref, open_ref, table_ref, sum_ref,
    total_ref, local_ref, product_ref, edge_ref, low_grad_ref, high_grad_ref,
    mixed_grad, drive, pre_low, decay_buf, *, first,
):
    length = pre_ref.shape[0]
    half = low_ref.shape[0]

    @pl.when(pl.program_id(0) == 0)
    def _():
        total_ref[...] = jnp.zeros_like(total_ref) if first else sum_ref[...]

    mixed_grad[...] = nn(grad_low_ref[:, :half], low_ref[:, GROUP:]) + nn(grad_low_ref[:, half:], high_ref[:, GROUP:])
    decay_buf[pl.ds(length, 8), :] = jnp.ones((8, GROUP), f32)
    for part in range(GROUP // BLOCK):
        lanes = slice(part * BLOCK, (part + 1) * BLOCK)

        def back(start):
            rows = pl.ds(start, TILE)
            value, slope = gelu_parts(pre_ref[rows, lanes])
            grad = mixed_grad[rows, lanes]
            pre_low[rows, lanes] = (grad * states_ref[pl.ds(start + 8, TILE), lanes] * slope).astype(bf16)
            drive[rows, lanes] = grad * value
            decay_buf[rows, lanes] = jnp.exp(open_ref[rows, lanes] * table_ref[7:8, lanes])

        tiles(length, back)
    scan_rows(decay_buf, drive, 1, local_ref, 0, product_ref, length, True)
    edge_ref[0:1, :] = decay_buf[0:1, :] * local_ref[0:1, :]
    edge_ref[1:2, :] = decay_buf[0:1, :] * product_ref[0:1, :]
    total_ref[:, :half] += nt(pre_low[...], low_ref[:, :GROUP])
    total_ref[:, half:] += nt(pre_low[...], high_ref[:, :GROUP])
    low_grad_ref[:, :GROUP] = nn(normed_t_ref[:half], pre_low[...]).astype(bf16)
    high_grad_ref[:, :GROUP] = nn(normed_t_ref[half:], pre_low[...]).astype(bf16)
    low_grad_ref[:, GROUP:] = nn(grad_t_ref[:half], mixed_ref[...]).astype(bf16)
    high_grad_ref[:, GROUP:] = nn(grad_t_ref[half:], mixed_ref[...]).astype(bf16)


def gate_back_kernel(
    local_ref, product_ref, enter_ref, states_ref, open_ref, flow_ref, conv_ref, branch_ref, rgate_ref, igate_ref, table_ref,
    conv_grad_ref, rgrad_ref, igrad_ref, sums_ref,
    rec_low, inp_low, conv_low,
):
    length = local_ref.shape[0]
    for part in range(GROUP // BLOCK):
        lanes = slice(part * BLOCK, (part + 1) * BLOCK)

        def back(index, sums):
            start = pl.multiple_of(index * TILE, TILE)
            rows = pl.ds(start, TILE)
            carried = local_ref[rows, lanes] + product_ref[rows, lanes] * enter_ref[0:1, lanes]
            recur_open = open_ref[rows, lanes]
            inflow = flow_ref[rows, lanes]
            conv_out = conv_ref[rows, lanes]
            rate = table_ref[7:8, lanes]
            log_decay = recur_open * rate
            decay = jnp.exp(log_decay)
            multiplier = jnp.sqrt(one_minus_exp(2.0 * log_decay))
            before = states_ref[pl.ds(start, TILE + 8), lanes][7 : 7 + TILE]
            weighted = carried * inflow
            decay_grad = carried * before * decay - weighted * conv_out * decay * decay / multiplier
            scaled = decay_grad * recur_open
            rec_grad = rate * scaled * (1.0 - recur_open)
            direct = weighted * multiplier
            inp_grad = direct * conv_out * (1.0 - inflow)
            rec_low[rows, lanes] = rec_grad.astype(bf16)
            inp_low[rows, lanes] = inp_grad.astype(bf16)
            conv_low[rows, lanes] = conv_out.astype(bf16)
            conv_grad_ref[rows, lanes] = direct

            def fold(value):
                return jnp.sum(value.reshape(TILE // 8, 8, BLOCK), axis=0)

            return (sums[0] + fold(rec_grad), sums[1] + fold(inp_grad), sums[2] + fold(scaled))

        zero = jnp.zeros((8, BLOCK), f32)
        sums = lax.fori_loop(0, length // TILE, back, (zero, zero, zero))
        for row, value in zip((2, 1, 3), sums):
            sums_ref[row : row + 1, lanes] = jnp.sum(value, axis=0, keepdims=True)
        rgrad_ref[part] = tn(conv_low[:, lanes], rec_low[:, lanes])
        igrad_ref[part] = tn(conv_low[:, lanes], inp_low[:, lanes])
        conv_grad_ref[:, lanes] += nt(rec_low[:, lanes], rgate_ref[part]) + nt(inp_low[:, lanes], igate_ref[part])

        def taps(index, sums):
            start = pl.multiple_of(index * TILE, TILE)
            grad = conv_grad_ref[pl.ds(start, TILE), lanes]

            def fold(value):
                return jnp.sum(value.reshape(TILE // 8, 8, BLOCK), axis=0)

            window = branch_ref[pl.ds(start + HALO - 8, TILE + 8), lanes]
            new = [sums[0] + fold(grad)]
            for offset in range(CONV):
                new.append(sums[offset + 1] + fold(grad * window[8 - offset : 8 - offset + TILE]))
            return tuple(new)

        sums = lax.fori_loop(0, length // TILE, taps, (zero,) * (CONV + 1))
        for row, value in zip((0, 4, 5, 6, 7), sums):
            sums_ref[row : row + 1, lanes] = jnp.sum(value, axis=0, keepdims=True)


def branch_back_kernel(
    conv_grad_ref, after_ref, table_ref, normed_t_ref, low_ref, high_ref, sum_ref, small_refs,
    total_ref, low_grad_ref, high_grad_ref,
    padded, branch_low, *, groups,
):
    length = conv_grad_ref.shape[0]
    half = low_ref.shape[0]

    @pl.when(pl.program_id(0) == 0)
    def _():
        total_ref[...] = sum_ref[...]

    @pl.when(pl.program_id(0) < groups)
    def _():
        padded[pl.ds(0, length), :] = conv_grad_ref[...]
        padded[pl.ds(length, 8), :] = after_ref[...]
        for part in range(GROUP // BLOCK):
            lanes = slice(part * BLOCK, (part + 1) * BLOCK)

            def back(start):
                window = padded[pl.ds(start, TILE + 8), lanes]
                result = table_ref[0:1, lanes] * window[:TILE]
                for offset in range(1, CONV):
                    result = result + table_ref[offset : offset + 1, lanes] * window[offset : offset + TILE]
                branch_low[pl.ds(start, TILE), lanes] = result.astype(bf16)

            tiles(length, back)
        total_ref[:, :half] += nt(branch_low[...], low_ref[...])
        total_ref[:, half:] += nt(branch_low[...], high_ref[...])
        low_grad_ref[...] = nn(normed_t_ref[:half], branch_low[...]).astype(bf16)
        high_grad_ref[...] = nn(normed_t_ref[half:], branch_low[...]).astype(bf16)

    if small_refs:

        @pl.when(pl.program_id(0) == groups)
        def _():
            low_grad_ref[...] = small_refs[0][...]
            high_grad_ref[...] = small_refs[1][...]


def join_kernel(*refs, columns):
    parts, outs = refs[: -len(columns)], refs[-len(columns) :]
    for out_ref, places in zip(outs, columns):
        to = 0
        for start, size in places:
            total = parts[0][:, start : start + size].astype(f32)
            for part in parts[1:]:
                total = total + part[:, start : start + size].astype(f32)
            out_ref[:, to : to + size] = total
            to += size


def fixed(shape):
    return pl.BlockSpec(shape, lambda g: (0,) * len(shape))


def lanes_until(rows, last):
    return pl.BlockSpec((rows, GROUP), lambda g: (0, jnp.minimum(g, last)))


def lanes_of(rows, width=GROUP):
    return pl.BlockSpec((rows, width), lambda g: (0, g))


def blocks_of():
    return pl.BlockSpec((GROUP // BLOCK, BLOCK, BLOCK), lambda g: (g, 0, 0))


def shaped(*dims, kind=f32):
    return jax.ShapeDtypeStruct(dims, kind)


VMEM_LIMIT = 28 * 1024 * 1024
PARAMS = pltpu.CompilerParams(dimension_semantics=("arbitrary",), vmem_limit_bytes=VMEM_LIMIT)


ANYWHERE = pl.BlockSpec(memory_space=pl.ANY)
SCALARS = pl.BlockSpec(memory_space=pltpu.SMEM)


SPANS = {
    "order_kernel": 4, "tables_of": 2, "norm_kernel": 6, "mix_in_kernel": 14, "mix_out_kernel": 10,
    "second_norm_kernel": 6, "mlp_kernel": 17, "middle_kernel": 12, "mix_back": 18, "gate_back_kernel": 11,
    "branch_back": 8, "final_kernel": 10, "small_grads": 3, "join": 2,
}


def call(kernel, steps, in_specs, out_specs, out_shape, scratch, hold=()):
    count = len(in_specs)
    name = getattr(kernel, "func", kernel).__name__

    def body(*refs):
        kernel(*refs[:count], *refs[count + len(hold) :])

    run = pl.pallas_call(
        body,
        grid=(steps,),
        in_specs=list(in_specs) + [ANYWHERE] * len(hold),
        out_specs=out_specs,
        out_shape=out_shape,
        scratch_shapes=scratch,
        compiler_params=PARAMS,
        name=name,
        cost_estimate=pl.CostEstimate(flops=SPANS[name] * 1150 * 10**6, bytes_accessed=0, transcendentals=0),
    )
    return lambda *args: run(*args, *hold)


def make_per_device(dp_size, tensor_size):
    pairs = tensor_size // 2
    dp_bits = [1 << bit for bit in range(dp_size.bit_length() - 1)]
    order_one = dp_bits[1:] + dp_bits[:1]
    order_two = dp_bits[2:3] + dp_bits[1:2] + dp_bits[3:] + dp_bits[:1]
    orders = (order_one, order_two)
    position_of = {bit: place for place, bit in enumerate(order_one)}

    def swap_dp(values, bit):
        return lax.ppermute(values, "dp", [(at, at ^ bit) for at in range(dp_size)])

    def swap_tensor(values, bit):
        return lax.ppermute(values, "tensor", [(at, at ^ bit) for at in range(tensor_size)])

    def relative(pieces, index):
        bit = 1
        while bit < len(pieces):
            flag = (index & bit) != 0
            pieces = [jnp.where(flag, pieces[at ^ bit], piece) for at, piece in enumerate(pieces)]
            bit *= 2
        return pieces

    place_index = [
        sum(bit for bit in dp_bits if place & (1 << position_of[bit])) for place in range(dp_size)
    ]

    def split_lanes(values, count):
        width = values.shape[1] // count
        return [values[:, at * width : (at + 1) * width] for at in range(count)]

    class Gather:
        def __init__(self, values, order):
            self.rows, self.left, self.done = values.shape[0], list(order), []
            self.send(values)

        def send(self, values):
            self.values, self.bit = values, self.left.pop(0)
            self.received = swap_dp(values, self.bit)

        def take(self, received):
            if not self.left:
                self.received, self.last = None, received
                return
            values, rows = self.values, self.rows
            if all(position_of[other] < position_of[self.bit] for other in self.done):
                values = jnp.concatenate([values, received], axis=0)
            else:
                pieces = []
                for at in range(0, values.shape[0], rows):
                    pieces += [values[at : at + rows], received[at : at + rows]]
                values = jnp.concatenate(pieces, axis=0)
            self.done.append(self.bit)
            self.send(values)

        def finish(self):
            while self.received is not None:
                self.take(self.received)
            return self.values, self.last

    def round_of(travellers, *others):
        travellers = [one for one in travellers if one.received is not None]
        found = lax.optimization_barrier(tuple(one.received for one in travellers) + others)
        for one, received in zip(travellers, found):
            one.take(received)
        return list(found[len(travellers) :])

    def add(one, two):
        return (one.astype(f32) + two.astype(f32)).astype(one.dtype)

    class Scatter:
        def __init__(self, own, other, order, block_rows):
            self.left, self.block_rows = list(order[:-1]), block_rows
            self.values, self.received = own, swap_dp(other, order[-1])

        def halves(self, values, bit):
            rows = values.shape[0]
            if all(position_of[other] < position_of[bit] for other in self.left):
                return values[: rows // 2], values[rows // 2 :]
            starts = range(0, rows, self.block_rows)
            pieces = [values[at : at + self.block_rows] for at in starts]
            return jnp.concatenate(pieces[0::2], axis=0), jnp.concatenate(pieces[1::2], axis=0)

        def step(self, token=None):
            received = self.received
            if token is not None:
                received, token = lax.optimization_barrier((received, token))
            self.take(received)
            return token

        def take(self, received):
            if self.left:
                bit = self.left.pop()
                keep, send = self.halves(self.values, bit)
                keep_more, send_more = self.halves(received, bit)
                sent = add(send, send_more)
                self.values, self.received = add(keep, keep_more), swap_dp(sent, bit)
                self.mark = sent
            else:
                self.values, self.received = add(self.values, received), None
                self.mark = self.values

        def finish(self):
            while self.received is not None:
                self.step()
            return self.values

    def steps(scatters, token):
        for one in scatters:
            if one.received is not None:
                token = one.step(token)
        return token, [one.mark for one in scatters]

    def spread_tensor(values):
        return [values] + [swap_tensor(values, other) for other in range(1, tensor_size)]

    def join_parts(own, others, columns, hold):
        parts = [own] + [others[other] for other in range(1, tensor_size)]

        def join(*refs):
            join_kernel(*refs, columns=columns)

        rows = own.shape[0]
        widths = [sum(size for _, size in places) for places in columns]
        return call(
            join, 1, [fixed(own.shape)] * tensor_size, [fixed((rows, width)) for width in widths],
            [shaped(rows, width) for width in widths], [], hold=hold,
        )(*parts)

    def join_tensor(parts):
        total = parts[0].astype(f32)
        received = []
        for other in range(1, tensor_size):
            received.append(swap_tensor(parts[other], other))
            total = total + received[-1].astype(f32)
        return total, received

    def per_device(
        hidden_in, cotangent, norm_gains, mixer_in, branch_gate, mixer_out, input_gate, recur_gate,
        conv_kernel, conv_bias, input_bias, recur_bias, decay_param, mlp_gate, mlp_up, mlp_down,
    ):
        dp_at = lax.axis_index("dp")
        tensor_at = lax.axis_index("tensor")
        length, model = hidden_in.shape
        block_rows, chunk = mixer_in.shape
        half = model // 2
        hidden_chunk = mlp_gate.shape[1]
        sub = block_rows * BLOCK // model
        local_blocks = chunk // BLOCK
        pair_width = 2 * chunk
        groups = pair_width // GROUP
        mlp_groups = hidden_chunk // GROUP
        fast = block_rows == BLOCK and sub % 16 == 0
        natural_at = jnp.array(place_index, jnp.int32) ^ dp_at
        places = natural_at if fast else jnp.arange(model // BLOCK, dtype=jnp.int32)

        def features(values, back=False):
            if fast:
                return values
            pieces = jnp.stack(split_lanes(values, dp_size), axis=0)
            order = natural_at
            if back:
                order = jnp.zeros_like(natural_at).at[natural_at].set(jnp.arange(dp_size, dtype=jnp.int32))
            return jnp.concatenate(list(jnp.take(pieces, order, axis=0)), axis=1)

        first_rows = lax.ppermute(
            hidden_in[length - HALO :], "tensor", [(at, at + 1) for at in range(tensor_size - 1)]
        )

        def rows_first(table):
            return table.transpose(1, 0, 2).reshape(-1, BLOCK)

        vectors = jnp.concatenate(
            [conv_kernel.transpose(1, 2, 0).reshape(-1, sub)]
            + [table.T for table in (conv_bias, input_bias, recur_bias, decay_param)],
            axis=0,
        )
        owner = lax.broadcasted_iota(jnp.int32, (1, BLOCK), 1) // sub
        vectors = jnp.where(owner == dp_at, jnp.tile(vectors, (1, BLOCK // sub)), jnp.zeros((), bf16))
        gate_rows = 2 * local_blocks * sub
        vector_rows = vectors.shape[0]
        small_rows = (gate_rows + vector_rows + 2 + 15) // 16 * 16
        small = jnp.concatenate(
            [
                rows_first(recur_gate),
                rows_first(input_gate),
                vectors,
                jnp.pad(norm_gains.T, ((0, 0), (0, BLOCK - block_rows))),
                jnp.zeros((small_rows - gate_rows - vector_rows - 2, BLOCK), bf16),
            ],
            axis=0,
        )
        whole = fixed((length, model))
        turned = fixed((model, length))
        hidden_low, cot_low, cot_t = call(
            order_kernel, 1, [SCALARS, whole, whole], [whole, whole, turned],
            [shaped(length, model, kind=bf16), shaped(length, model, kind=bf16), shaped(model, length, kind=bf16)], [],
        )(places, features(hidden_in), features(cotangent))

        merged = fast and small_rows == block_rows

        def in_pairs_of(found):
            return [
                jnp.concatenate([one[:, :chunk], two[:, :chunk], one[:, chunk:], two[:, chunk:]], axis=1) if merged
                else jnp.concatenate([one, two], axis=1)
                for one, two in zip(found[0::2], found[1::2])
            ]

        def interleave(one, two):
            gate = jnp.concatenate([one[:, :chunk], two[:, :chunk]], axis=1)
            out = jnp.concatenate([one[:, chunk:], two[:, chunk:]], axis=1)
            pieces = []
            for at in range(groups):
                pieces += [gate[:, at * GROUP : (at + 1) * GROUP], out[:, at * GROUP : (at + 1) * GROUP]]
            return jnp.concatenate(pieces, axis=1)

        in_near = spread_tensor(jnp.concatenate([mixer_in, small], axis=1) if merged else mixer_in)
        *in_near[1:], first_rows, gate_weights, out_weights = lax.optimization_barrier(
            tuple(in_near[1:]) + (first_rows, branch_gate, mixer_out)
        )
        in_gathers = [Gather(values, orders[at % 2]) for at, values in enumerate(in_pairs_of(in_near))]
        out_near = spread_tensor(jnp.concatenate([gate_weights, out_weights], axis=1))
        *out_near[1:], hidden_low = round_of(in_gathers, *out_near[1:], hidden_low)
        out_gathers = [
            Gather(interleave(one, two), orders[at % 2]) for at, (one, two) in enumerate(zip(out_near[0::2], out_near[1::2]))
        ]
        round_of(in_gathers + out_gathers)
        in_pairs = [one.finish() for one in in_gathers]
        if not merged:
            small_low, small_high = Gather(jnp.concatenate(spread_tensor(small), axis=1), order_one).finish()
        mlp_weights = lax.all_gather(jnp.concatenate([mlp_gate, mlp_up, mlp_down], axis=1), ("dp", "tensor"), axis=0, tiled=False)
        mlp_weights = mlp_weights.reshape(dp_size, tensor_size, block_rows, 3 * hidden_chunk)

        kinds = 2 * CONV
        channels = tensor_size * chunk
        blocks = tensor_size * local_blocks
        if merged:
            small_spec = pl.BlockSpec((half, 2 * BLOCK), lambda g: (0, pair_width // (2 * BLOCK)))
            gate_spec = fixed((blocks, BLOCK, BLOCK))
            def tables_of(*args, **sizes):
                tables_kernel(*args, sub=sub, local_blocks=local_blocks, chunks=tensor_size)
            rgates, igates, table, gains = call(
                tables_of, 1, [SCALARS] + [small_spec] * tensor_size, [gate_spec, gate_spec, fixed((kinds, channels)), fixed((2, model))],
                [shaped(blocks, BLOCK, BLOCK, kind=bf16), shaped(blocks, BLOCK, BLOCK, kind=bf16), shaped(kinds, channels), shaped(2, model)], [],
            )(places, *[values for pair in in_pairs for values in pair])
        else:
            stacked = jnp.concatenate([small_low, small_high], axis=0).reshape(dp_size, small_rows, -1)
            order = jnp.zeros_like(natural_at).at[natural_at].set(jnp.arange(dp_size, dtype=jnp.int32))
            gates = jnp.take(stacked[:, :gate_rows], order, axis=0).reshape(dp_size, 2, local_blocks, sub, tensor_size, BLOCK)
            gates = gates.transpose(1, 4, 2, 0, 3, 5).reshape(2, blocks, BLOCK, BLOCK)
            rgates, igates = gates[0], gates[1]
            table = jnp.sum(stacked[:, gate_rows : gate_rows + vector_rows].astype(f32), axis=0)
            table = table.reshape(kinds, local_blocks, tensor_size, BLOCK).transpose(0, 2, 1, 3).reshape(kinds, channels)
            gains = stacked[:, gate_rows + vector_rows : gate_rows + vector_rows + 2, :block_rows]
            gains = gains.transpose(1, 0, 2).reshape(2, model).astype(f32)
        decay_rates = table[7:8]
        last_row = lax.broadcasted_iota(jnp.int32, table.shape, 0) == kinds - 1
        table = jnp.where(last_row, -8.0 * jax.nn.softplus(-table), table)

        full = length + HALO
        normed_one, normed_one_t = call(
            norm_kernel, 1, [SCALARS, whole, fixed((HALO, model)), fixed((2, model))], [fixed((full, model)), turned],
            [shaped(full, model, kind=bf16), shaped(model, length, kind=bf16)], [pltpu.VMEM((HALO, model), f32)],
        )(places, hidden_low, features(first_rows), gains)

        fed = []
        for pair in range(pairs):
            low, high = in_pairs[pair]
            part = slice(2 * pair * local_blocks, 2 * (pair + 1) * local_blocks)
            lanes = slice(pair * pair_width, (pair + 1) * pair_width)
            fed.append(
                call(
                    mix_in_kernel,
                    groups,
                    [fixed((full, model)), lanes_of(half), lanes_of(half), blocks_of(), blocks_of(), lanes_of(8)],
                    [lanes_of(full)] + [lanes_of(length)] * 5,
                    [shaped(full, pair_width)] + [shaped(length, pair_width)] * 5,
                    [pltpu.VMEM((length, GROUP), bf16)] + [pltpu.VMEM((length, GROUP), f32)] * 3,
                )(normed_one, low, high, rgates[part], igates[part], table[:, lanes])
            )
            fed[pair] = list(fed[pair])
        fed[-1][5:] = round_of(out_gathers, fed[-1][5])
        out_pairs = [one.finish() for one in out_gathers]

        def exchange(products, ends, later):
            mine = jnp.concatenate([products, ends], axis=0)
            found = [mine]
            for other in range(1, tensor_size):
                pieces = split_lanes(swap_tensor(mine, other), tensor_size)
                found.append(jnp.concatenate([pieces[at ^ other] for at in range(tensor_size)], axis=1))
            found = relative(found, tensor_at)
            state = jnp.zeros_like(ends)
            turn = range(tensor_size - 1, 0, -1) if later else range(tensor_size - 1)
            for at in turn:
                use = (at > tensor_at) if later else (at < tensor_at)
                state = jnp.where(use, found[at][0:1] * state + found[at][1:2], state)
            return state

        enter = exchange(
            jnp.concatenate([one[5][length - 1 :] for one in fed], axis=1),
            jnp.concatenate([one[4][length - 1 :] for one in fed], axis=1),
            False,
        )
        middle = hidden_low
        mixed = []
        for pair in range(pairs):
            low, high = out_pairs[pair]
            lanes = slice(pair * pair_width, (pair + 1) * pair_width)
            gate_pre, states, mixed_low, middle = call(
                mix_out_kernel,
                groups,
                [fixed((full, model)), lanes_of(half, 2 * GROUP), lanes_of(half, 2 * GROUP), lanes_of(length), lanes_of(length), lanes_of(1), whole],
                [lanes_of(length), lanes_of(length + 8), lanes_of(length), whole],
                [shaped(length, pair_width), shaped(length + 8, pair_width), shaped(length, pair_width, kind=bf16), shaped(length, model)],
                [],
            )(normed_one, low, high, fed[pair][4], fed[pair][5], enter[:, lanes], middle)
            mixed.append((gate_pre, states, mixed_low))
        normed_two, normed_two_t = call(
            second_norm_kernel, 1, [SCALARS, whole, fixed((2, model))], [whole, turned],
            [shaped(length, model, kind=bf16), shaped(model, length, kind=bf16)], [pltpu.VMEM((length, model), bf16)],
        )(places, middle, gains)
        normed_two = features(normed_two, True)

        chunk_at = jnp.arange(tensor_size, dtype=jnp.int32) ^ tensor_at
        before = []
        moved = []
        width = 3 * GROUP
        whole_at = pl.BlockSpec((length, model), lambda g, chunks: (0, 0))
        turned_at = pl.BlockSpec((model, length), lambda g, chunks: (0, 0))
        half_at = pl.BlockSpec((half, width), lambda g, chunks: (0, g))
        for at in reversed(range(tensor_size)):
            hold = []
            if len(moved) >= 2:
                before[0], hold = steps([moved[-2]], before[0])

            def kernel(*refs, count=len(before), held=len(hold)):
                sums = refs[8 : 8 + count] if count else (None, None)
                mlp_kernel(*refs[:8], *sums, *refs[8 + count + held :])

            total, normed_grad, low_grad, high_grad = pl.pallas_call(
                kernel,
                grid_spec=pltpu.PrefetchScalarGridSpec(
                    num_scalar_prefetch=1,
                    grid=(mlp_groups,),
                    in_specs=[
                        whole_at, turned_at, whole_at, turned_at,
                    ] + [
                        pl.BlockSpec(
                            (dp_size, 1, block_rows, GROUP),
                            lambda g, chunks, at=at, which=which: (0, chunks[at], 0, which * mlp_groups + g),
                        )
                        for which in range(3)
                    ] + [whole_at] * len(before) + [ANYWHERE] * len(hold),
                    out_specs=[whole_at, whole_at, half_at, half_at],
                    scratch_shapes=[
                        pltpu.VMEM((length, 2 * GROUP), f32), pltpu.VMEM((length, GROUP), bf16),
                        pltpu.VMEM((length, 2 * GROUP), bf16), pltpu.VMEM((length, GROUP), f32),
                    ],
                ),
                out_shape=[shaped(length, model), shaped(length, model)] + [shaped(half, 3 * hidden_chunk, kind=bf16)] * 2,
                compiler_params=PARAMS,
                name="mlp_kernel",
                cost_estimate=pl.CostEstimate(flops=SPANS["mlp_kernel"] * 1150 * 10**6, bytes_accessed=0, transcendentals=0),
            )(chunk_at, normed_two, normed_two_t, cotangent, cot_t, *[mlp_weights] * 3, *before, *hold)
            before = [total, normed_grad]
            moved.append(Scatter(low_grad, high_grad, orders[at % 2], block_rows))
        total, hold = steps([moved[2]], total)
        hidden_out, middle_grad, middle_low, middle_low_t, gain_two = call(
            middle_kernel, 1, [SCALARS, whole, whole, whole, whole, fixed((2, model))],
            [whole, whole, whole, turned, fixed((1, model))],
            [shaped(length, model, kind=bf16), shaped(length, model), shaped(length, model, kind=bf16), shaped(model, length, kind=bf16), shaped(1, model)],
            [pltpu.VMEM((length, model), bf16), pltpu.VMEM((length, model), f32), pltpu.VMEM((length, model), f32)],
            hold=hold,
        )(places, middle, features(total), features(normed_grad), cot_low, gains)
        hidden_out = features(hidden_out, True)

        backs = {}
        out_moved = {}
        gain_two, marks = steps([moved[3], moved[0]], gain_two)
        hold = [gain_two] + marks
        backward = list(reversed(range(pairs)))
        for step, pair in enumerate(backward):
            low, high = out_pairs[pair]
            gate_pre, states, mixed_low = mixed[pair]
            lanes = slice(pair * pair_width, (pair + 1) * pair_width)
            def mix_back(*refs, first=step == 0):
                if first:
                    refs = refs[:10] + (None,) + refs[10:]
                mix_back_kernel(*refs, first=first)

            sums = [normed_grad] if step else []
            normed_grad, local, product, edge, low_grad, high_grad = call(
                mix_back,
                groups,
                [whole, turned, turned, lanes_of(half, 2 * GROUP), lanes_of(half, 2 * GROUP), lanes_of(length), lanes_of(length + 8), lanes_of(length), lanes_of(length), lanes_of(8)] + [whole] * len(sums),
                [whole, lanes_of(length), lanes_of(length), lanes_of(8), lanes_of(half, 2 * GROUP), lanes_of(half, 2 * GROUP)],
                [shaped(length, model), shaped(length, pair_width), shaped(length, pair_width), shaped(8, pair_width), shaped(half, 2 * pair_width, kind=bf16), shaped(half, 2 * pair_width, kind=bf16)],
                [pltpu.VMEM((length, GROUP), f32), pltpu.VMEM((length, GROUP), f32), pltpu.VMEM((length, GROUP), bf16), pltpu.VMEM((length + 8, GROUP), f32)],
                hold=hold,
            )(middle_low, middle_low_t, normed_one_t, low, high, gate_pre, states, mixed_low, fed[pair][2], table[:, lanes], *sums)
            out_moved[pair] = Scatter(low_grad, high_grad, orders[step % 2], block_rows)
            if step == 0:
                edge, marks = steps([moved[1], moved[0]], edge)
                hold = [edge] + marks
            else:
                edge, _ = steps([moved[1]], edge)
            backs[pair] = (local, product, edge)

        def separate(values):
            gate = [values[:, 2 * at * GROUP : (2 * at + 1) * GROUP] for at in range(groups)]
            out = [values[:, (2 * at + 1) * GROUP : (2 * at + 2) * GROUP] for at in range(groups)]
            gate, out = jnp.concatenate(gate, axis=1), jnp.concatenate(out, axis=1)
            return [jnp.concatenate([gate[:, :chunk], out[:, :chunk]], axis=1), jnp.concatenate([gate[:, chunk:], out[:, chunk:]], axis=1)]

        leave = exchange(
            jnp.concatenate([one[2][1:2] for _, one in sorted(backs.items())], axis=1),
            jnp.concatenate([one[2][0:1] for _, one in sorted(backs.items())], axis=1),
            True,
        )
        gate_backs = {}
        mlp_others = {}

        def send_along(step, token):
            other = tensor_size - 1 - step
            values, token = lax.optimization_barrier((moved[step].finish(), token))
            mlp_others[other] = swap_tensor(values, other)
            return token

        leave, hold = steps([moved[2], out_moved[backward[0]]], leave)
        leave = send_along(0, leave)
        for step, pair in enumerate(backward):
            part = slice(2 * pair * local_blocks, 2 * (pair + 1) * local_blocks)
            lanes = slice(pair * pair_width, (pair + 1) * pair_width)
            branch, conv_out, recur_open, inflow = fed[pair][:4]
            local, product, _ = backs[pair]
            gate_backs[pair] = list(
                call(
                    gate_back_kernel,
                    groups,
                    [lanes_of(length), lanes_of(length), lanes_of(1), lanes_of(length + 8)] + [lanes_of(length)] * 3 + [lanes_of(full), blocks_of(), blocks_of(), lanes_of(8)],
                    [lanes_of(length), blocks_of(), blocks_of(), lanes_of(8)],
                    [shaped(length, pair_width), shaped(2 * local_blocks, BLOCK, BLOCK), shaped(2 * local_blocks, BLOCK, BLOCK), shaped(8, pair_width)],
                    [pltpu.VMEM((length, GROUP), bf16)] * 3,
                    hold=hold,
                )(local, product, leave[:, lanes], mixed[pair][1], recur_open, inflow, conv_out, branch, rgates[part], igates[part], table[:, lanes])
            )
            if step == 0:
                token, marks = steps([moved[3], out_moved[backward[1]]], gate_backs[pair][3])
                hold = [token] + marks
                gate_backs[pair][3] = token
            else:
                gate_backs[pair][3], hold = steps([moved[2]], gate_backs[pair][3])
        gate_list = [gate_backs[pair] for pair in range(pairs)]
        heads = jnp.concatenate([one[0][:8] for one in gate_list], axis=1)
        heads = jnp.concatenate(relative(split_lanes(heads, tensor_size), tensor_at), axis=1)
        heads = lax.ppermute(heads, "tensor", [(at + 1, at) for at in range(tensor_size - 1)])
        after = jnp.concatenate(relative(split_lanes(heads, tensor_size), tensor_at), axis=1)
        mlp_others[tensor_size - 1], after = lax.optimization_barrier((mlp_others[tensor_size - 1], after))
        after = send_along(2, send_along(1, after))
        after, marks = steps([out_moved[backward[0]]], after)
        hold = hold + marks
        rgrads = jnp.concatenate([one[1] for one in gate_list], axis=0)
        igrads = jnp.concatenate([one[2] for one in gate_list], axis=0)
        rows = jnp.concatenate([one[3] for one in gate_list], axis=1)
        decay_row = rows[3:4] * (8.0 * jax.nn.sigmoid(-decay_rates))
        rows = jnp.concatenate([rows[4:8], rows[0:3], decay_row], axis=0)
        small_low, small_high = [], []
        if merged:
            small_target = fixed((half, 2 * BLOCK))

            def small_grads(*args, **sizes):
                small_grads_kernel(*args, sub=sub, local_blocks=local_blocks, chunks=tensor_size)
            small_halves = call(
                small_grads, 1, [SCALARS, gate_spec, gate_spec, fixed((kinds, channels))], [small_target] * tensor_size,
                [shaped(half, 2 * BLOCK, kind=bf16)] * tensor_size, [], hold=hold,
            )(places, rgrads, igrads, rows)
            small_low, small_high = small_halves[0::2], small_halves[1::2]
        else:
            gate_grads = jnp.stack([rgrads, igrads], axis=0).reshape(2, tensor_size, local_blocks, dp_size, sub, BLOCK)
            gate_grads = gate_grads.transpose(3, 0, 2, 4, 1, 5).reshape(dp_size, gate_rows, tensor_size * BLOCK)
            gate_grads = jnp.take(gate_grads, natural_at, axis=0)
            rows = rows.reshape(kinds, tensor_size, local_blocks, BLOCK).transpose(0, 2, 1, 3).reshape(1, vector_rows, -1)
            rest = small_rows - gate_rows - vector_rows
            pieces = [
                gate_grads,
                jnp.broadcast_to(rows, (dp_size,) + rows.shape[1:]),
                jnp.zeros((dp_size, rest, tensor_size * BLOCK), f32),
            ]
            small_grads = jnp.concatenate(pieces, axis=1).reshape(dp_size * small_rows, -1).astype(bf16)
            small_own, small_other = jnp.split(small_grads, 2, axis=0)
        if not merged:
            small_moved = Scatter(small_own, small_other, order_one, small_rows)

        in_parts = {}
        for step, pair in enumerate(backward):
            low, high = in_pairs[pair]
            lanes = slice(pair * pair_width, (pair + 1) * pair_width)
            smalls = [small_low[pair], small_high[pair]] if merged else []
            moved_width = pair_width + 2 * BLOCK * merged

            def branch_back(*refs, count=len(smalls)):
                branch_back_kernel(*refs[:7], refs[7 : 7 + count], *refs[7 + count :], groups=groups)

            last = groups - 1
            normed_grad, low_grad, high_grad = call(
                branch_back,
                moved_width // GROUP,
                [lanes_until(length, last), lanes_until(8, last), lanes_until(8, last), turned, lanes_until(half, last), lanes_until(half, last), whole]
                + [fixed((half, GROUP))] * len(smalls),
                [whole, lanes_of(half), lanes_of(half)],
                [shaped(length, model), shaped(half, moved_width, kind=bf16), shaped(half, moved_width, kind=bf16)],
                [pltpu.VMEM((length + 8, GROUP), f32), pltpu.VMEM((length, GROUP), bf16)],
                hold=hold,
            )(gate_backs[pair][0], after[:, lanes], table[:, lanes], normed_one_t, low, high, normed_grad, *smalls)
            in_parts[pair] = Scatter(low_grad, high_grad, orders[step % 2], block_rows)
            if step == 0:
                normed_grad, hold = steps([moved[3], out_moved[backward[1]], out_moved[backward[0]]], normed_grad)
            else:
                normed_grad, hold = steps([out_moved[backward[1]], in_parts[backward[0]], in_parts[backward[1]]], normed_grad)

        hidden_grad, gain_one = call(
            final_kernel, 1, [SCALARS, whole, whole, whole, fixed((2, model))], [whole, fixed((1, model))],
            [shaped(length, model), shaped(1, model)], [pltpu.VMEM((length, model), f32)],
            hold=hold,
        )(places, hidden_low, normed_grad, middle_grad, gains)
        in_list = [in_parts[pair] for pair in backward]
        gain_one, = round_of(in_list, gain_one)
        late = [gain_one]
        gain_parts = jnp.concatenate([gain_one, gain_two], axis=0).reshape(2, dp_size, block_rows)
        if not fast:
            gain_parts = jnp.take(gain_parts, natural_at, axis=1)
        gain_parts = jnp.pad(gain_parts.transpose(1, 0, 2), ((0, 0), (0, 6), (0, BLOCK - block_rows)))
        gain_parts = gain_parts.reshape(8 * dp_size, BLOCK)
        gains_moved = Scatter(gain_parts[: 4 * dp_size], gain_parts[4 * dp_size :], order_one, 8)
        out_parts = [part for pair in range(pairs) for part in separate(out_moved[pair].finish())]
        out_others = {other: swap_tensor(out_parts[other], other) for other in range(tensor_size - 1, 0, -1)}
        mlp_columns = [[((3 * at + which) * GROUP, GROUP) for at in range(mlp_groups)] for which in range(3)]
        mlp_grads = join_parts(moved[-1].finish(), mlp_others, mlp_columns, late)
        far, near = out_others[tensor_size - 1], out_others[tensor_size - 2]
        far, near = round_of(in_list + [gains_moved], far, near)
        out_others.update({tensor_size - 1: far, tensor_size - 2: near})
        round_of([one for one in in_list] + [gains_moved])
        out_columns = [[(0, chunk)], [(chunk, chunk)]]
        gate_grad, out_grad = join_parts(out_parts[0], out_others, out_columns, late)

        def in_chunks(values):
            if not merged:
                return split_lanes(values, 2)
            one, two = values[:, :chunk], values[:, chunk:pair_width]
            small_one, small_two = split_lanes(values[:, pair_width:], 2)
            return [jnp.concatenate([one, small_one], axis=1), jnp.concatenate([two, small_two], axis=1)]

        in_sum, in_far = join_tensor([part for pair in range(pairs) for part in in_chunks(in_parts[pair].finish())])
        gain_sum = gains_moved.finish()
        gain_sum = sum(spread_tensor(gain_sum)[1:], gain_sum)
        gain_rows = block_rows // tensor_size
        gain_sum = lax.dynamic_slice(gain_sum, (0, tensor_at * gain_rows), (2, gain_rows)).T

        hidden_grad = features(hidden_grad, True)
        if merged:
            in_sum, small_sum = in_sum[:, :chunk], in_sum[:, chunk:]
        else:
            small_sum, _ = join_tensor(split_lanes(small_moved.finish(), tensor_size))

        gate_sum = small_sum[:gate_rows].reshape(2, local_blocks, sub, BLOCK).transpose(0, 2, 1, 3)
        vector_sum = lax.dynamic_slice(small_sum, (gate_rows, dp_at * sub), (vector_rows, sub))
        vector_sum = vector_sum.reshape(kinds, local_blocks, sub)

        return (
            hidden_out,
            hidden_grad,
            gain_sum,
            in_sum,
            gate_grad,
            out_grad,
            gate_sum[1],
            gate_sum[0],
            vector_sum[:CONV].transpose(2, 0, 1),
            vector_sum[4].T,
            vector_sum[5].T,
            vector_sum[6].T,
            vector_sum[7].T,
            mlp_grads[0],
            mlp_grads[1],
            mlp_grads[2],
        )

    return per_device


def solution(mesh):
    rows = P(("dp", "tensor"), None)
    matrix = P("dp", "tensor")
    gate = P("dp", "tensor", None)
    kernel = P("dp", None, "tensor")
    placed = (rows, rows, P("dp", None), matrix, matrix, matrix, gate, gate, kernel) + (matrix,) * 7
    made = (rows, rows, rows, matrix, matrix, matrix, gate, gate, kernel) + (matrix,) * 7
    return jax.shard_map(
        make_per_device(mesh.shape["dp"], mesh.shape["tensor"]),
        mesh=mesh,
        in_specs=placed,
        out_specs=made,
        check_vma=False,
    )
```

```python
import jax
import jax.numpy as jnp
from jax import lax
from jax.experimental import pallas as pl
from jax.experimental.pallas import tpu as pltpu
from jax.sharding import PartitionSpec as P

BLOCK = 128
CONV = 4
HALO = 16
TILE = 64
GROUP = 256
ROWS = 32
epsilon = 1e-06
f32 = jnp.float32
bf16 = jnp.bfloat16
ROOT = 0.7978845608028654
CUBIC = 0.044715


def nn(left, right):
    return lax.dot_general(left, right, (((1,), (0,)), ((), ())), preferred_element_type=f32)


def nt(left, right):
    return lax.dot_general(left, right, (((1,), (1,)), ((), ())), preferred_element_type=f32)


def tn(left, right):
    return lax.dot_general(left, right, (((0,), (0,)), ((), ())), preferred_element_type=f32)


def gelu_parts(value):
    square = value * value
    curve = jnp.tanh(ROOT * value * (1.0 + CUBIC * square))
    half = 0.5 * (1.0 + curve)
    slope = half + (0.5 * ROOT) * value * (1.0 - curve * curve) * (1.0 + 3.0 * CUBIC * square)
    return value * half, slope


def one_minus_exp(value):
    series = 1.0 + value * (1.0 / 7.0)
    for term in (6.0, 5.0, 4.0, 3.0, 2.0):
        series = 1.0 + value * (1.0 / term) * series
    return jnp.where(value > -0.25, -value * series, 1.0 - jnp.exp(value))


def scan_rows(decay_ref, drive_ref, offset, out_ref, out_offset, total_ref, length, reverse):
    width = drive_ref.shape[1]
    rows = lax.broadcasted_iota(jnp.int32, (8, width), 0)
    steps = length // 8

    def body(step, carry):
        state, product = carry
        at = (steps - 1 - step) if reverse else step
        start = pl.multiple_of(at * 8, 8)
        decay = decay_ref[pl.ds(start, 8 + 8 * (offset > 0)), :][offset : offset + 8]
        drive = drive_ref[pl.ds(start, 8), :]
        for shift in (1, 2, 4):
            if reverse:
                inside = rows < 8 - shift
                amount = 8 - shift
            else:
                inside = rows >= shift
                amount = shift
            drive = drive + decay * jnp.where(inside, pltpu.roll(drive, amount, 0), 0.0)
            decay = decay * jnp.where(inside, pltpu.roll(decay, amount, 0), 1.0)
        state = drive + decay * state
        product = decay * product
        out_ref[pl.ds(start + out_offset, 8), :] = state
        total_ref[pl.ds(start, 8), :] = product
        edge = 0 if reverse else 7
        return (
            jnp.broadcast_to(state[edge : edge + 1], (8, width)),
            jnp.broadcast_to(product[edge : edge + 1], (8, width)),
        )

    lax.fori_loop(0, steps, body, (jnp.zeros((8, width), f32), jnp.ones((8, width), f32)))


def tiles(length, body):
    def step(index, carry):
        body(pl.multiple_of(index * TILE, TILE))
        return carry

    lax.fori_loop(0, length // TILE, step, 0)


def mix_in_kernel(
    normed_ref, low_ref, high_ref, rgate_ref, igate_ref, table_ref,
    branch_ref, conv_ref, open_ref, flow_ref, local_ref, product_ref,
    conv_low, rec_buf, inp_buf, decay_buf,
):
    length = conv_ref.shape[0]
    half = low_ref.shape[0]
    branch_ref[...] = nn(normed_ref[:, :half], low_ref[...]) + nn(normed_ref[:, half:], high_ref[...])
    for part in range(GROUP // BLOCK):
        lanes = slice(part * BLOCK, (part + 1) * BLOCK)

        def convolve(start):
            window = branch_ref[pl.ds(start + HALO - 8, TILE + 8), lanes]
            result = table_ref[4:5, lanes] + table_ref[0:1, lanes] * window[8:]
            for offset in range(1, CONV):
                result = result + table_ref[offset : offset + 1, lanes] * window[8 - offset : 8 - offset + TILE]
            conv_ref[pl.ds(start, TILE), lanes] = result
            conv_low[pl.ds(start, TILE), lanes] = result.astype(bf16)

        tiles(length, convolve)
        rec_buf[:, lanes] = nn(conv_low[:, lanes], rgate_ref[part])
        inp_buf[:, lanes] = nn(conv_low[:, lanes], igate_ref[part])

        def gates(start):
            rows = pl.ds(start, TILE)
            recur_open = jax.nn.sigmoid(rec_buf[rows, lanes] + table_ref[6:7, lanes])
            inflow = jax.nn.sigmoid(inp_buf[rows, lanes] + table_ref[5:6, lanes])
            log_decay = recur_open * table_ref[7:8, lanes]
            multiplier = jnp.sqrt(one_minus_exp(2.0 * log_decay))
            open_ref[rows, lanes] = recur_open
            flow_ref[rows, lanes] = inflow
            decay_buf[rows, lanes] = jnp.exp(log_decay)
            rec_buf[rows, lanes] = multiplier * inflow * conv_ref[rows, lanes]

        tiles(length, gates)
    scan_rows(decay_buf, rec_buf, 0, local_ref, 0, product_ref, length, False)


def mix_out_kernel(
    normed_ref, low_ref, high_ref, local_ref, product_ref, enter_ref, sum_ref,
    pre_ref, states_ref, mixed_ref, total_ref,
):
    length = local_ref.shape[0]
    half = low_ref.shape[0]

    @pl.when(pl.program_id(0) == 0)
    def _():
        total_ref[...] = sum_ref[...].astype(f32)

    pre_ref[...] = nn(normed_ref[HALO:, :half], low_ref[:, :GROUP]) + nn(normed_ref[HALO:, half:], high_ref[:, :GROUP])
    states_ref[0:8, :] = jnp.broadcast_to(enter_ref[0:1, :], (8, GROUP))
    for part in range(GROUP // BLOCK):
        lanes = slice(part * BLOCK, (part + 1) * BLOCK)

        def mix(start):
            rows = pl.ds(start, TILE)
            states = local_ref[rows, lanes] + product_ref[rows, lanes] * enter_ref[0:1, lanes]
            states_ref[pl.ds(start + 8, TILE), lanes] = states
            gate = pre_ref[rows, lanes]
            curve = jnp.tanh(ROOT * gate * (1.0 + CUBIC * gate * gate))
            mixed_ref[rows, lanes] = (states * (gate * (0.5 * (1.0 + curve)))).astype(bf16)

        tiles(length, mix)
    total_ref[:, :half] += nt(mixed_ref[...], low_ref[:, GROUP:])
    total_ref[:, half:] += nt(mixed_ref[...], high_ref[:, GROUP:])


def mlp_kernel(
    chunks_ref, normed_ref, normed_t_ref, cot_ref, cot_t_ref, gate_ref, up_ref, down_ref, sum_ref, back_ref,
    total_ref, grad_ref, low_grad_ref, high_grad_ref,
    pre, hidden, pre_low, act,
):
    length, model = normed_ref.shape
    half = model // 2
    first = sum_ref is None

    @pl.when(pl.program_id(0) == 0)
    def _():
        if first:
            total_ref[...] = jnp.zeros_like(total_ref)
            grad_ref[...] = jnp.zeros_like(grad_ref)
        else:
            total_ref[...] = sum_ref[...]
            grad_ref[...] = back_ref[...]

    gate = gate_ref[...].reshape(model, GROUP)
    up_weights = up_ref[...].reshape(model, GROUP)
    down = down_ref[...].reshape(model, GROUP)
    pre[:, :GROUP] = nn(normed_ref[...], gate)
    pre[:, GROUP:] = nn(normed_ref[...], up_weights)
    act[...] = nn(cot_ref[...], down)
    for part in range(GROUP // BLOCK):
        lanes = slice(part * BLOCK, (part + 1) * BLOCK)
        up_lanes = slice(GROUP + part * BLOCK, GROUP + (part + 1) * BLOCK)

        def activate(start):
            rows = pl.ds(start, TILE)
            value, slope = gelu_parts(pre[rows, lanes])
            up = pre[rows, up_lanes]
            grad = act[rows, lanes]
            hidden[rows, lanes] = (value * up).astype(bf16)
            pre_low[rows, lanes] = (grad * up * slope).astype(bf16)
            pre_low[rows, up_lanes] = (grad * value).astype(bf16)

        tiles(length, activate)
    total_ref[...] += nt(hidden[...], down)
    grad_ref[...] += nt(pre_low[:, :GROUP], gate) + nt(pre_low[:, GROUP:], up_weights)
    low_grad_ref[:, : 2 * GROUP] = nn(normed_t_ref[:half], pre_low[...]).astype(bf16)
    high_grad_ref[:, : 2 * GROUP] = nn(normed_t_ref[half:], pre_low[...]).astype(bf16)
    low_grad_ref[:, 2 * GROUP :] = nn(cot_t_ref[:half], hidden[...]).astype(bf16)
    high_grad_ref[:, 2 * GROUP :] = nn(cot_t_ref[half:], hidden[...]).astype(bf16)


def lane_block(index):
    return pl.ds(pl.multiple_of(index * BLOCK, BLOCK), BLOCK)


def order_kernel(places_ref, hidden_ref, cot_ref, hidden_out_ref, cot_out_ref, cot_t_ref):
    for place in range(hidden_ref.shape[1] // BLOCK):
        lanes = slice(place * BLOCK, (place + 1) * BLOCK)
        hidden_out_ref[:, lanes] = hidden_ref[:, lane_block(places_ref[place])]
        cot_out_ref[:, lanes] = cot_ref[:, lane_block(places_ref[place])]
    cot_t_ref[...] = cot_out_ref[...].T


def row_loop(length, rows, body, start):
    def step(index, carry):
        return body(pl.ds(pl.multiple_of(index * rows, rows), rows), carry)

    return lax.fori_loop(0, length // rows, step, start)


def scale_of(values):
    return lax.rsqrt(jnp.mean(values * values, axis=1, keepdims=True) + epsilon)


def norm_kernel(places_ref, hidden_ref, first_ref, gains_ref, normed_ref, normed_t_ref, first_buf):
    length = hidden_ref.shape[0]
    for place in range(hidden_ref.shape[1] // BLOCK):
        lanes = slice(place * BLOCK, (place + 1) * BLOCK)
        first_buf[:, lanes] = first_ref[:, lane_block(places_ref[place])].astype(f32)
    first = first_buf[...]
    normed_ref[:HALO, :] = (first * scale_of(first) * gains_ref[0:1, :]).astype(bf16)

    def body(rows, carry):
        values = hidden_ref[rows, :].astype(f32)
        normed_ref[pl.ds(rows.start + HALO, rows.size), :] = (values * scale_of(values) * gains_ref[0:1, :]).astype(bf16)
        return carry

    row_loop(length, ROWS, body, 0)
    normed_t_ref[...] = normed_ref[HALO:, :].T


def second_norm_kernel(places_ref, middle_ref, gains_ref, normed_ref, normed_t_ref, buffer):
    length, model = middle_ref.shape

    def body(rows, carry):
        values = middle_ref[rows, :]
        buffer[rows, :] = (values * scale_of(values) * gains_ref[1:2, :]).astype(bf16)
        return carry

    row_loop(length, ROWS, body, 0)
    normed_t_ref[...] = buffer[...].T
    for place in range(model // BLOCK):
        normed_ref[:, lane_block(places_ref[place])] = buffer[:, place * BLOCK : (place + 1) * BLOCK]


def norm_back(values, grad, gain):
    scale = scale_of(values)
    unit = values * scale
    scaled = grad * gain
    return scale * (scaled - unit * jnp.mean(scaled * unit, axis=1, keepdims=True)), grad * unit


def fold_rows(value):
    rows, width = value.shape
    return jnp.sum(value.reshape(rows // 8, 8, width), axis=0)


def middle_kernel(
    places_ref, middle_ref, total_ref, grad_ref, cot_ref, gains_ref,
    out_ref, middle_grad_ref, low_ref, low_t_ref, gain_ref, buffer, own_total, own_grad,
):
    length, model = middle_ref.shape
    for place in range(model // BLOCK):
        lanes = slice(place * BLOCK, (place + 1) * BLOCK)
        own_total[:, lanes] = total_ref[:, lane_block(places_ref[place])]
        own_grad[:, lanes] = grad_ref[:, lane_block(places_ref[place])]

    def body(rows, carry):
        middle = middle_ref[rows, :]
        change, part = norm_back(middle, own_grad[rows, :], gains_ref[1:2, :])
        middle_grad = cot_ref[rows, :].astype(f32) + change
        middle_grad_ref[rows, :] = middle_grad
        low_ref[rows, :] = middle_grad.astype(bf16)
        buffer[rows, :] = (middle + own_total[rows, :]).astype(bf16)
        return carry + fold_rows(part)

    total = row_loop(length, ROWS, body, jnp.zeros((8, model), f32))
    gain_ref[...] = jnp.sum(total, axis=0, keepdims=True)
    low_t_ref[...] = low_ref[...].T
    for place in range(model // BLOCK):
        out_ref[:, lane_block(places_ref[place])] = buffer[:, place * BLOCK : (place + 1) * BLOCK]


def final_kernel(places_ref, hidden_ref, grad_ref, middle_grad_ref, gains_ref, out_ref, gain_ref, buffer):
    length, model = hidden_ref.shape

    def body(rows, carry):
        change, part = norm_back(hidden_ref[rows, :].astype(f32), grad_ref[rows, :], gains_ref[0:1, :])
        buffer[rows, :] = middle_grad_ref[rows, :] + change
        return carry + fold_rows(part)

    total = row_loop(length, ROWS, body, jnp.zeros((8, model), f32))
    gain_ref[...] = jnp.sum(total, axis=0, keepdims=True)
    for place in range(model // BLOCK):
        out_ref[:, lane_block(places_ref[place])] = buffer[:, place * BLOCK : (place + 1) * BLOCK]


def tables_kernel(places_ref, *refs, sub, local_blocks, chunks):
    sources, (rgate_ref, igate_ref, table_ref, gains_ref) = refs[:-4], refs[-4:]
    rows_each = 2 * local_blocks * sub
    kinds = 2 * CONV
    count = places_ref.shape[0]
    size = sources[0].shape[0] * 2 // count
    sums = [jnp.zeros((kinds * local_blocks, BLOCK), f32)] * chunks
    for place in range(count):
        side = place // (count // 2)
        top = (place % (count // 2)) * size
        natural = places_ref[place]
        for at in range(chunks):
            source = sources[at // 2 * 2 + side]
            lanes = slice(at % 2 * BLOCK, (at % 2 + 1) * BLOCK)
            for which, gate_ref in enumerate((rgate_ref, igate_ref)):
                for block in range(local_blocks):
                    start = top + (which * local_blocks + block) * sub
                    gate_ref[at * local_blocks + block, pl.ds(pl.multiple_of(natural * sub, sub), sub), :] = source[start : start + sub, lanes]
            sums[at] = sums[at] + source[top + rows_each : top + rows_each + kinds * local_blocks, lanes].astype(f32)
        start = top + rows_each + kinds * local_blocks
        gains_ref[:, place * BLOCK : (place + 1) * BLOCK] = sources[side][start : start + 2, :BLOCK].astype(f32)
    for at in range(chunks):
        for block in range(local_blocks):
            column = (at * local_blocks + block) * BLOCK
            for kind in range(kinds):
                row = kind * local_blocks + block
                table_ref[kind : kind + 1, column : column + BLOCK] = sums[at][row : row + 1]


def small_grads_kernel(places_ref, rgrad_ref, igrad_ref, sums_ref, *targets, sub, local_blocks, chunks):
    kinds = 2 * CONV
    rows_each = 2 * local_blocks * sub
    count = places_ref.shape[0]
    size = targets[0].shape[0] * 2 // count
    spare = size - rows_each - kinds * local_blocks
    vectors = []
    for at in range(chunks):
        rows = []
        for kind in range(kinds):
            for block in range(local_blocks):
                column = (at * local_blocks + block) * BLOCK
                rows.append(sums_ref[kind : kind + 1, column : column + BLOCK])
        vectors.append(jnp.concatenate(rows, axis=0))
    for place in range(count):
        side = place // (count // 2)
        top = (place % (count // 2)) * size
        natural = places_ref[place]
        for at in range(chunks):
            target = targets[at // 2 * 2 + side]
            lanes = slice(at % 2 * BLOCK, (at % 2 + 1) * BLOCK)
            for which, grad_ref in enumerate((rgrad_ref, igrad_ref)):
                for block in range(local_blocks):
                    start = top + (which * local_blocks + block) * sub
                    target[start : start + sub, lanes] = grad_ref[
                        at * local_blocks + block, pl.ds(pl.multiple_of(natural * sub, sub), sub), :
                    ].astype(bf16)
            rest = jnp.concatenate([vectors[at], jnp.zeros((spare, BLOCK), f32)], axis=0)
            target[top + rows_each : top + size, lanes] = rest.astype(bf16)


def mix_back_kernel(
    grad_low_ref, grad_t_ref, normed_t_ref, low_ref, high_ref, pre_ref, states_ref, mixed_ref, open_ref, table_ref, sum_ref,
    total_ref, local_ref, product_ref, edge_ref, low_grad_ref, high_grad_ref,
    mixed_grad, drive, pre_low, decay_buf, *, first,
):
    length = pre_ref.shape[0]
    half = low_ref.shape[0]

    @pl.when(pl.program_id(0) == 0)
    def _():
        total_ref[...] = jnp.zeros_like(total_ref) if first else sum_ref[...]

    mixed_grad[...] = nn(grad_low_ref[:, :half], low_ref[:, GROUP:]) + nn(grad_low_ref[:, half:], high_ref[:, GROUP:])
    decay_buf[pl.ds(length, 8), :] = jnp.ones((8, GROUP), f32)
    for part in range(GROUP // BLOCK):
        lanes = slice(part * BLOCK, (part + 1) * BLOCK)

        def back(start):
            rows = pl.ds(start, TILE)
            value, slope = gelu_parts(pre_ref[rows, lanes])
            grad = mixed_grad[rows, lanes]
            pre_low[rows, lanes] = (grad * states_ref[pl.ds(start + 8, TILE), lanes] * slope).astype(bf16)
            drive[rows, lanes] = grad * value
            decay_buf[rows, lanes] = jnp.exp(open_ref[rows, lanes] * table_ref[7:8, lanes])

        tiles(length, back)
    scan_rows(decay_buf, drive, 1, local_ref, 0, product_ref, length, True)
    edge_ref[0:1, :] = decay_buf[0:1, :] * local_ref[0:1, :]
    edge_ref[1:2, :] = decay_buf[0:1, :] * product_ref[0:1, :]
    total_ref[:, :half] += nt(pre_low[...], low_ref[:, :GROUP])
    total_ref[:, half:] += nt(pre_low[...], high_ref[:, :GROUP])
    low_grad_ref[:, :GROUP] = nn(normed_t_ref[:half], pre_low[...]).astype(bf16)
    high_grad_ref[:, :GROUP] = nn(normed_t_ref[half:], pre_low[...]).astype(bf16)
    low_grad_ref[:, GROUP:] = nn(grad_t_ref[:half], mixed_ref[...]).astype(bf16)
    high_grad_ref[:, GROUP:] = nn(grad_t_ref[half:], mixed_ref[...]).astype(bf16)


def gate_back_kernel(
    local_ref, product_ref, enter_ref, states_ref, open_ref, flow_ref, conv_ref, branch_ref, rgate_ref, igate_ref, table_ref,
    conv_grad_ref, rgrad_ref, igrad_ref, sums_ref,
    rec_low, inp_low, conv_low,
):
    length = local_ref.shape[0]
    for part in range(GROUP // BLOCK):
        lanes = slice(part * BLOCK, (part + 1) * BLOCK)

        def back(index, sums):
            start = pl.multiple_of(index * TILE, TILE)
            rows = pl.ds(start, TILE)
            carried = local_ref[rows, lanes] + product_ref[rows, lanes] * enter_ref[0:1, lanes]
            recur_open = open_ref[rows, lanes]
            inflow = flow_ref[rows, lanes]
            conv_out = conv_ref[rows, lanes]
            rate = table_ref[7:8, lanes]
            log_decay = recur_open * rate
            decay = jnp.exp(log_decay)
            multiplier = jnp.sqrt(one_minus_exp(2.0 * log_decay))
            before = states_ref[pl.ds(start, TILE + 8), lanes][7 : 7 + TILE]
            weighted = carried * inflow
            decay_grad = carried * before * decay - weighted * conv_out * decay * decay / multiplier
            scaled = decay_grad * recur_open
            rec_grad = rate * scaled * (1.0 - recur_open)
            direct = weighted * multiplier
            inp_grad = direct * conv_out * (1.0 - inflow)
            rec_low[rows, lanes] = rec_grad.astype(bf16)
            inp_low[rows, lanes] = inp_grad.astype(bf16)
            conv_low[rows, lanes] = conv_out.astype(bf16)
            conv_grad_ref[rows, lanes] = direct

            def fold(value):
                return jnp.sum(value.reshape(TILE // 8, 8, BLOCK), axis=0)

            return (sums[0] + fold(rec_grad), sums[1] + fold(inp_grad), sums[2] + fold(scaled))

        zero = jnp.zeros((8, BLOCK), f32)
        sums = lax.fori_loop(0, length // TILE, back, (zero, zero, zero))
        for row, value in zip((2, 1, 3), sums):
            sums_ref[row : row + 1, lanes] = jnp.sum(value, axis=0, keepdims=True)
        rgrad_ref[part] = tn(conv_low[:, lanes], rec_low[:, lanes])
        igrad_ref[part] = tn(conv_low[:, lanes], inp_low[:, lanes])
        conv_grad_ref[:, lanes] += nt(rec_low[:, lanes], rgate_ref[part]) + nt(inp_low[:, lanes], igate_ref[part])

        def taps(index, sums):
            start = pl.multiple_of(index * TILE, TILE)
            grad = conv_grad_ref[pl.ds(start, TILE), lanes]

            def fold(value):
                return jnp.sum(value.reshape(TILE // 8, 8, BLOCK), axis=0)

            window = branch_ref[pl.ds(start + HALO - 8, TILE + 8), lanes]
            new = [sums[0] + fold(grad)]
            for offset in range(CONV):
                new.append(sums[offset + 1] + fold(grad * window[8 - offset : 8 - offset + TILE]))
            return tuple(new)

        sums = lax.fori_loop(0, length // TILE, taps, (zero,) * (CONV + 1))
        for row, value in zip((0, 4, 5, 6, 7), sums):
            sums_ref[row : row + 1, lanes] = jnp.sum(value, axis=0, keepdims=True)


def branch_back_kernel(
    conv_grad_ref, after_ref, table_ref, normed_t_ref, low_ref, high_ref, sum_ref, small_refs,
    total_ref, low_grad_ref, high_grad_ref,
    padded, branch_low, *, groups,
):
    length = conv_grad_ref.shape[0]
    half = low_ref.shape[0]

    @pl.when(pl.program_id(0) == 0)
    def _():
        total_ref[...] = sum_ref[...]

    @pl.when(pl.program_id(0) < groups)
    def _():
        padded[pl.ds(0, length), :] = conv_grad_ref[...]
        padded[pl.ds(length, 8), :] = after_ref[...]
        for part in range(GROUP // BLOCK):
            lanes = slice(part * BLOCK, (part + 1) * BLOCK)

            def back(start):
                window = padded[pl.ds(start, TILE + 8), lanes]
                result = table_ref[0:1, lanes] * window[:TILE]
                for offset in range(1, CONV):
                    result = result + table_ref[offset : offset + 1, lanes] * window[offset : offset + TILE]
                branch_low[pl.ds(start, TILE), lanes] = result.astype(bf16)

            tiles(length, back)
        total_ref[:, :half] += nt(branch_low[...], low_ref[...])
        total_ref[:, half:] += nt(branch_low[...], high_ref[...])
        low_grad_ref[...] = nn(normed_t_ref[:half], branch_low[...]).astype(bf16)
        high_grad_ref[...] = nn(normed_t_ref[half:], branch_low[...]).astype(bf16)

    if small_refs:

        @pl.when(pl.program_id(0) == groups)
        def _():
            low_grad_ref[...] = small_refs[0][...]
            high_grad_ref[...] = small_refs[1][...]


def join_kernel(*refs, columns):
    parts, outs = refs[: -len(columns)], refs[-len(columns) :]
    for out_ref, places in zip(outs, columns):
        to = 0
        for start, size in places:
            total = parts[0][:, start : start + size].astype(f32)
            for part in parts[1:]:
                total = total + part[:, start : start + size].astype(f32)
            out_ref[:, to : to + size] = total
            to += size


def fixed(shape):
    return pl.BlockSpec(shape, lambda g: (0,) * len(shape))


def lanes_until(rows, last):
    return pl.BlockSpec((rows, GROUP), lambda g: (0, jnp.minimum(g, last)))


def lanes_of(rows, width=GROUP):
    return pl.BlockSpec((rows, width), lambda g: (0, g))


def blocks_of():
    return pl.BlockSpec((GROUP // BLOCK, BLOCK, BLOCK), lambda g: (g, 0, 0))


def shaped(*dims, kind=f32):
    return jax.ShapeDtypeStruct(dims, kind)


VMEM_LIMIT = 28 * 1024 * 1024
PARAMS = pltpu.CompilerParams(dimension_semantics=("arbitrary",), vmem_limit_bytes=VMEM_LIMIT)


ANYWHERE = pl.BlockSpec(memory_space=pl.ANY)
SCALARS = pl.BlockSpec(memory_space=pltpu.SMEM)


SPANS = {
    "order_kernel": 4, "tables_of": 2, "norm_kernel": 6, "mix_in_kernel": 14, "mix_out_kernel": 10,
    "second_norm_kernel": 6, "mlp_kernel": 17, "middle_kernel": 12, "mix_back": 18, "gate_back_kernel": 11,
    "branch_back": 8, "final_kernel": 10, "small_grads": 3, "join": 2,
}


def call(kernel, steps, in_specs, out_specs, out_shape, scratch, hold=()):
    count = len(in_specs)
    name = getattr(kernel, "func", kernel).__name__

    def body(*refs):
        kernel(*refs[:count], *refs[count + len(hold) :])

    run = pl.pallas_call(
        body,
        grid=(steps,),
        in_specs=list(in_specs) + [ANYWHERE] * len(hold),
        out_specs=out_specs,
        out_shape=out_shape,
        scratch_shapes=scratch,
        compiler_params=PARAMS,
        name=name,
        cost_estimate=pl.CostEstimate(flops=SPANS[name] * 1150 * 10**6, bytes_accessed=0, transcendentals=0),
    )
    return lambda *args: run(*args, *hold)


def make_per_device(dp_size, tensor_size):
    pairs = tensor_size // 2
    dp_bits = [1 << bit for bit in range(dp_size.bit_length() - 1)]
    order_one = dp_bits[1:] + dp_bits[:1]
    order_two = dp_bits[2:3] + dp_bits[1:2] + dp_bits[3:] + dp_bits[:1]
    orders = (order_one, order_two)
    position_of = {bit: place for place, bit in enumerate(order_one)}

    def swap_dp(values, bit):
        return lax.ppermute(values, "dp", [(at, at ^ bit) for at in range(dp_size)])

    def swap_tensor(values, bit):
        return lax.ppermute(values, "tensor", [(at, at ^ bit) for at in range(tensor_size)])

    def relative(pieces, index):
        bit = 1
        while bit < len(pieces):
            flag = (index & bit) != 0
            pieces = [jnp.where(flag, pieces[at ^ bit], piece) for at, piece in enumerate(pieces)]
            bit *= 2
        return pieces

    place_index = [
        sum(bit for bit in dp_bits if place & (1 << position_of[bit])) for place in range(dp_size)
    ]

    def split_lanes(values, count):
        width = values.shape[1] // count
        return [values[:, at * width : (at + 1) * width] for at in range(count)]

    class Gather:
        def __init__(self, values, order):
            self.rows, self.left, self.done = values.shape[0], list(order), []
            self.send(values)

        def send(self, values):
            self.values, self.bit = values, self.left.pop(0)
            self.received = swap_dp(values, self.bit)

        def take(self, received):
            if not self.left:
                self.received, self.last = None, received
                return
            values, rows = self.values, self.rows
            if all(position_of[other] < position_of[self.bit] for other in self.done):
                values = jnp.concatenate([values, received], axis=0)
            else:
                pieces = []
                for at in range(0, values.shape[0], rows):
                    pieces += [values[at : at + rows], received[at : at + rows]]
                values = jnp.concatenate(pieces, axis=0)
            self.done.append(self.bit)
            self.send(values)

        def finish(self):
            while self.received is not None:
                self.take(self.received)
            return self.values, self.last

    def round_of(travellers, *others):
        travellers = [one for one in travellers if one.received is not None]
        found = lax.optimization_barrier(tuple(one.received for one in travellers) + others)
        for one, received in zip(travellers, found):
            one.take(received)
        return list(found[len(travellers) :])

    def add(one, two):
        return (one.astype(f32) + two.astype(f32)).astype(one.dtype)

    class Scatter:
        def __init__(self, own, other, order, block_rows):
            self.left, self.block_rows = list(order[:-1]), block_rows
            self.values, self.received = own, swap_dp(other, order[-1])

        def halves(self, values, bit):
            rows = values.shape[0]
            if all(position_of[other] < position_of[bit] for other in self.left):
                return values[: rows // 2], values[rows // 2 :]
            starts = range(0, rows, self.block_rows)
            pieces = [values[at : at + self.block_rows] for at in starts]
            return jnp.concatenate(pieces[0::2], axis=0), jnp.concatenate(pieces[1::2], axis=0)

        def step(self, token=None):
            received = self.received
            if token is not None:
                received, token = lax.optimization_barrier((received, token))
            self.take(received)
            return token

        def take(self, received):
            if self.left:
                bit = self.left.pop()
                keep, send = self.halves(self.values, bit)
                keep_more, send_more = self.halves(received, bit)
                sent = add(send, send_more)
                self.values, self.received = add(keep, keep_more), swap_dp(sent, bit)
                self.mark = sent
            else:
                self.values, self.received = add(self.values, received), None
                self.mark = self.values

        def finish(self):
            while self.received is not None:
                self.step()
            return self.values

    def steps(scatters, token):
        for one in scatters:
            if one.received is not None:
                token = one.step(token)
        return token, [one.mark for one in scatters]

    def spread_tensor(values):
        return [values] + [swap_tensor(values, other) for other in range(1, tensor_size)]

    def join_parts(own, others, columns, hold):
        parts = [own] + [others[other] for other in range(1, tensor_size)]

        def join(*refs):
            join_kernel(*refs, columns=columns)

        rows = own.shape[0]
        widths = [sum(size for _, size in places) for places in columns]
        return call(
            join, 1, [fixed(own.shape)] * tensor_size, [fixed((rows, width)) for width in widths],
            [shaped(rows, width) for width in widths], [], hold=hold,
        )(*parts)

    def join_tensor(parts):
        total = parts[0].astype(f32)
        received = []
        for other in range(1, tensor_size):
            received.append(swap_tensor(parts[other], other))
            total = total + received[-1].astype(f32)
        return total, received

    def per_device(
        hidden_in, cotangent, norm_gains, mixer_in, branch_gate, mixer_out, input_gate, recur_gate,
        conv_kernel, conv_bias, input_bias, recur_bias, decay_param, mlp_gate, mlp_up, mlp_down,
    ):
        dp_at = lax.axis_index("dp")
        tensor_at = lax.axis_index("tensor")
        length, model = hidden_in.shape
        block_rows, chunk = mixer_in.shape
        half = model // 2
        hidden_chunk = mlp_gate.shape[1]
        sub = block_rows * BLOCK // model
        local_blocks = chunk // BLOCK
        pair_width = 2 * chunk
        groups = pair_width // GROUP
        mlp_groups = hidden_chunk // GROUP
        fast = block_rows == BLOCK and sub % 16 == 0
        natural_at = jnp.array(place_index, jnp.int32) ^ dp_at
        places = natural_at if fast else jnp.arange(model // BLOCK, dtype=jnp.int32)

        def features(values, back=False):
            if fast:
                return values
            pieces = jnp.stack(split_lanes(values, dp_size), axis=0)
            order = natural_at
            if back:
                order = jnp.zeros_like(natural_at).at[natural_at].set(jnp.arange(dp_size, dtype=jnp.int32))
            return jnp.concatenate(list(jnp.take(pieces, order, axis=0)), axis=1)

        first_rows = lax.ppermute(
            hidden_in[length - HALO :], "tensor", [(at, at + 1) for at in range(tensor_size - 1)]
        )

        def rows_first(table):
            return table.transpose(1, 0, 2).reshape(-1, BLOCK)

        vectors = jnp.concatenate(
            [conv_kernel.transpose(1, 2, 0).reshape(-1, sub)]
            + [table.T for table in (conv_bias, input_bias, recur_bias, decay_param)],
            axis=0,
        )
        owner = lax.broadcasted_iota(jnp.int32, (1, BLOCK), 1) // sub
        vectors = jnp.where(owner == dp_at, jnp.tile(vectors, (1, BLOCK // sub)), jnp.zeros((), bf16))
        gate_rows = 2 * local_blocks * sub
        vector_rows = vectors.shape[0]
        small_rows = (gate_rows + vector_rows + 2 + 15) // 16 * 16
        small = jnp.concatenate(
            [
                rows_first(recur_gate),
                rows_first(input_gate),
                vectors,
                jnp.pad(norm_gains.T, ((0, 0), (0, BLOCK - block_rows))),
                jnp.zeros((small_rows - gate_rows - vector_rows - 2, BLOCK), bf16),
            ],
            axis=0,
        )
        whole = fixed((length, model))
        turned = fixed((model, length))
        hidden_low, cot_low, cot_t = call(
            order_kernel, 1, [SCALARS, whole, whole], [whole, whole, turned],
            [shaped(length, model, kind=bf16), shaped(length, model, kind=bf16), shaped(model, length, kind=bf16)], [],
        )(places, features(hidden_in), features(cotangent))

        merged = fast and small_rows == block_rows

        def in_pairs_of(found):
            return [
                jnp.concatenate([one[:, :chunk], two[:, :chunk], one[:, chunk:], two[:, chunk:]], axis=1) if merged
                else jnp.concatenate([one, two], axis=1)
                for one, two in zip(found[0::2], found[1::2])
            ]

        def interleave(one, two):
            gate = jnp.concatenate([one[:, :chunk], two[:, :chunk]], axis=1)
            out = jnp.concatenate([one[:, chunk:], two[:, chunk:]], axis=1)
            pieces = []
            for at in range(groups):
                pieces += [gate[:, at * GROUP : (at + 1) * GROUP], out[:, at * GROUP : (at + 1) * GROUP]]
            return jnp.concatenate(pieces, axis=1)

        in_near = spread_tensor(jnp.concatenate([mixer_in, small], axis=1) if merged else mixer_in)
        *in_near[1:], first_rows, gate_weights, out_weights = lax.optimization_barrier(
            tuple(in_near[1:]) + (first_rows, branch_gate, mixer_out)
        )
        in_gathers = [Gather(values, orders[at % 2]) for at, values in enumerate(in_pairs_of(in_near))]
        gate_weights, out_weights, hidden_low = round_of(in_gathers, gate_weights, out_weights, hidden_low)
        out_near = spread_tensor(jnp.concatenate([gate_weights, out_weights], axis=1))
        out_near[1:] = round_of(in_gathers, *out_near[1:])
        out_gathers = [
            Gather(interleave(one, two), orders[at % 2]) for at, (one, two) in enumerate(zip(out_near[0::2], out_near[1::2]))
        ]
        in_pairs = [one.finish() for one in in_gathers]
        if not merged:
            small_low, small_high = Gather(jnp.concatenate(spread_tensor(small), axis=1), order_one).finish()
        mlp_weights = lax.all_gather(jnp.concatenate([mlp_gate, mlp_up, mlp_down], axis=1), ("dp", "tensor"), axis=0, tiled=False)
        mlp_weights = mlp_weights.reshape(dp_size, tensor_size, block_rows, 3 * hidden_chunk)

        kinds = 2 * CONV
        channels = tensor_size * chunk
        blocks = tensor_size * local_blocks
        if merged:
            small_spec = pl.BlockSpec((half, 2 * BLOCK), lambda g: (0, pair_width // (2 * BLOCK)))
            gate_spec = fixed((blocks, BLOCK, BLOCK))
            def tables_of(*args, **sizes):
                tables_kernel(*args, sub=sub, local_blocks=local_blocks, chunks=tensor_size)
            rgates, igates, table, gains = call(
                tables_of, 1, [SCALARS] + [small_spec] * tensor_size, [gate_spec, gate_spec, fixed((kinds, channels)), fixed((2, model))],
                [shaped(blocks, BLOCK, BLOCK, kind=bf16), shaped(blocks, BLOCK, BLOCK, kind=bf16), shaped(kinds, channels), shaped(2, model)], [],
            )(places, *[values for pair in in_pairs for values in pair])
        else:
            stacked = jnp.concatenate([small_low, small_high], axis=0).reshape(dp_size, small_rows, -1)
            order = jnp.zeros_like(natural_at).at[natural_at].set(jnp.arange(dp_size, dtype=jnp.int32))
            gates = jnp.take(stacked[:, :gate_rows], order, axis=0).reshape(dp_size, 2, local_blocks, sub, tensor_size, BLOCK)
            gates = gates.transpose(1, 4, 2, 0, 3, 5).reshape(2, blocks, BLOCK, BLOCK)
            rgates, igates = gates[0], gates[1]
            table = jnp.sum(stacked[:, gate_rows : gate_rows + vector_rows].astype(f32), axis=0)
            table = table.reshape(kinds, local_blocks, tensor_size, BLOCK).transpose(0, 2, 1, 3).reshape(kinds, channels)
            gains = stacked[:, gate_rows + vector_rows : gate_rows + vector_rows + 2, :block_rows]
            gains = gains.transpose(1, 0, 2).reshape(2, model).astype(f32)
        decay_rates = table[7:8]
        last_row = lax.broadcasted_iota(jnp.int32, table.shape, 0) == kinds - 1
        table = jnp.where(last_row, -8.0 * jax.nn.softplus(-table), table)

        full = length + HALO
        normed_one, normed_one_t = call(
            norm_kernel, 1, [SCALARS, whole, fixed((HALO, model)), fixed((2, model))], [fixed((full, model)), turned],
            [shaped(full, model, kind=bf16), shaped(model, length, kind=bf16)], [pltpu.VMEM((HALO, model), f32)],
        )(places, hidden_low, features(first_rows), gains)

        fed = []
        for pair in range(pairs):
            low, high = in_pairs[pair]
            part = slice(2 * pair * local_blocks, 2 * (pair + 1) * local_blocks)
            lanes = slice(pair * pair_width, (pair + 1) * pair_width)
            fed.append(
                call(
                    mix_in_kernel,
                    groups,
                    [fixed((full, model)), lanes_of(half), lanes_of(half), blocks_of(), blocks_of(), lanes_of(8)],
                    [lanes_of(full)] + [lanes_of(length)] * 5,
                    [shaped(full, pair_width)] + [shaped(length, pair_width)] * 5,
                    [pltpu.VMEM((length, GROUP), bf16)] + [pltpu.VMEM((length, GROUP), f32)] * 3,
                )(normed_one, low, high, rgates[part], igates[part], table[:, lanes])
            )
            fed[pair] = list(fed[pair])
            if pair == 0:
                fed[pair][5:] = round_of(out_gathers, fed[pair][5])
        fed[-1][5:] = round_of(out_gathers, fed[-1][5])
        out_pairs = [one.finish() for one in out_gathers]

        def exchange(products, ends, later):
            mine = jnp.concatenate([products, ends], axis=0)
            found = [mine]
            for other in range(1, tensor_size):
                pieces = split_lanes(swap_tensor(mine, other), tensor_size)
                found.append(jnp.concatenate([pieces[at ^ other] for at in range(tensor_size)], axis=1))
            found = relative(found, tensor_at)
            state = jnp.zeros_like(ends)
            turn = range(tensor_size - 1, 0, -1) if later else range(tensor_size - 1)
            for at in turn:
                use = (at > tensor_at) if later else (at < tensor_at)
                state = jnp.where(use, found[at][0:1] * state + found[at][1:2], state)
            return state

        enter = exchange(
            jnp.concatenate([one[5][length - 1 :] for one in fed], axis=1),
            jnp.concatenate([one[4][length - 1 :] for one in fed], axis=1),
            False,
        )
        middle = hidden_low
        mixed = []
        for pair in range(pairs):
            low, high = out_pairs[pair]
            lanes = slice(pair * pair_width, (pair + 1) * pair_width)
            gate_pre, states, mixed_low, middle = call(
                mix_out_kernel,
                groups,
                [fixed((full, model)), lanes_of(half, 2 * GROUP), lanes_of(half, 2 * GROUP), lanes_of(length), lanes_of(length), lanes_of(1), whole],
                [lanes_of(length), lanes_of(length + 8), lanes_of(length), whole],
                [shaped(length, pair_width), shaped(length + 8, pair_width), shaped(length, pair_width, kind=bf16), shaped(length, model)],
                [],
            )(normed_one, low, high, fed[pair][4], fed[pair][5], enter[:, lanes], middle)
            mixed.append((gate_pre, states, mixed_low))
        normed_two, normed_two_t = call(
            second_norm_kernel, 1, [SCALARS, whole, fixed((2, model))], [whole, turned],
            [shaped(length, model, kind=bf16), shaped(model, length, kind=bf16)], [pltpu.VMEM((length, model), bf16)],
        )(places, middle, gains)
        normed_two = features(normed_two, True)

        chunk_at = jnp.arange(tensor_size, dtype=jnp.int32) ^ tensor_at
        before = []
        moved = []
        width = 3 * GROUP
        whole_at = pl.BlockSpec((length, model), lambda g, chunks: (0, 0))
        turned_at = pl.BlockSpec((model, length), lambda g, chunks: (0, 0))
        half_at = pl.BlockSpec((half, width), lambda g, chunks: (0, g))
        for at in reversed(range(tensor_size)):
            hold = []
            if len(moved) >= 2:
                before[0], hold = steps([moved[-2]], before[0])

            def kernel(*refs, count=len(before), held=len(hold)):
                sums = refs[8 : 8 + count] if count else (None, None)
                mlp_kernel(*refs[:8], *sums, *refs[8 + count + held :])

            total, normed_grad, low_grad, high_grad = pl.pallas_call(
                kernel,
                grid_spec=pltpu.PrefetchScalarGridSpec(
                    num_scalar_prefetch=1,
                    grid=(mlp_groups,),
                    in_specs=[
                        whole_at, turned_at, whole_at, turned_at,
                    ] + [
                        pl.BlockSpec(
                            (dp_size, 1, block_rows, GROUP),
                            lambda g, chunks, at=at, which=which: (0, chunks[at], 0, which * mlp_groups + g),
                        )
                        for which in range(3)
                    ] + [whole_at] * len(before) + [ANYWHERE] * len(hold),
                    out_specs=[whole_at, whole_at, half_at, half_at],
                    scratch_shapes=[
                        pltpu.VMEM((length, 2 * GROUP), f32), pltpu.VMEM((length, GROUP), bf16),
                        pltpu.VMEM((length, 2 * GROUP), bf16), pltpu.VMEM((length, GROUP), f32),
                    ],
                ),
                out_shape=[shaped(length, model), shaped(length, model)] + [shaped(half, 3 * hidden_chunk, kind=bf16)] * 2,
                compiler_params=PARAMS,
                name="mlp_kernel",
                cost_estimate=pl.CostEstimate(flops=SPANS["mlp_kernel"] * 1150 * 10**6, bytes_accessed=0, transcendentals=0),
            )(chunk_at, normed_two, normed_two_t, cotangent, cot_t, *[mlp_weights] * 3, *before, *hold)
            before = [total, normed_grad]
            moved.append(Scatter(low_grad, high_grad, orders[at % 2], block_rows))
        total, hold = steps([moved[2]], total)
        hidden_out, middle_grad, middle_low, middle_low_t, gain_two = call(
            middle_kernel, 1, [SCALARS, whole, whole, whole, whole, fixed((2, model))],
            [whole, whole, whole, turned, fixed((1, model))],
            [shaped(length, model, kind=bf16), shaped(length, model), shaped(length, model, kind=bf16), shaped(model, length, kind=bf16), shaped(1, model)],
            [pltpu.VMEM((length, model), bf16), pltpu.VMEM((length, model), f32), pltpu.VMEM((length, model), f32)],
            hold=hold,
        )(places, middle, features(total), features(normed_grad), cot_low, gains)
        hidden_out = features(hidden_out, True)

        backs = {}
        out_moved = {}
        gain_two, marks = steps([moved[3], moved[0]], gain_two)
        hold = [gain_two] + marks
        backward = list(reversed(range(pairs)))
        for step, pair in enumerate(backward):
            low, high = out_pairs[pair]
            gate_pre, states, mixed_low = mixed[pair]
            lanes = slice(pair * pair_width, (pair + 1) * pair_width)
            def mix_back(*refs, first=step == 0):
                if first:
                    refs = refs[:10] + (None,) + refs[10:]
                mix_back_kernel(*refs, first=first)

            sums = [normed_grad] if step else []
            normed_grad, local, product, edge, low_grad, high_grad = call(
                mix_back,
                groups,
                [whole, turned, turned, lanes_of(half, 2 * GROUP), lanes_of(half, 2 * GROUP), lanes_of(length), lanes_of(length + 8), lanes_of(length), lanes_of(length), lanes_of(8)] + [whole] * len(sums),
                [whole, lanes_of(length), lanes_of(length), lanes_of(8), lanes_of(half, 2 * GROUP), lanes_of(half, 2 * GROUP)],
                [shaped(length, model), shaped(length, pair_width), shaped(length, pair_width), shaped(8, pair_width), shaped(half, 2 * pair_width, kind=bf16), shaped(half, 2 * pair_width, kind=bf16)],
                [pltpu.VMEM((length, GROUP), f32), pltpu.VMEM((length, GROUP), f32), pltpu.VMEM((length, GROUP), bf16), pltpu.VMEM((length + 8, GROUP), f32)],
                hold=hold,
            )(middle_low, middle_low_t, normed_one_t, low, high, gate_pre, states, mixed_low, fed[pair][2], table[:, lanes], *sums)
            out_moved[pair] = Scatter(low_grad, high_grad, orders[step % 2], block_rows)
            if step == 0:
                edge, marks = steps([moved[1], moved[0]], edge)
                hold = [edge] + marks
            else:
                edge, _ = steps([moved[1]], edge)
            backs[pair] = (local, product, edge)

        def separate(values):
            gate = [values[:, 2 * at * GROUP : (2 * at + 1) * GROUP] for at in range(groups)]
            out = [values[:, (2 * at + 1) * GROUP : (2 * at + 2) * GROUP] for at in range(groups)]
            gate, out = jnp.concatenate(gate, axis=1), jnp.concatenate(out, axis=1)
            return [jnp.concatenate([gate[:, :chunk], out[:, :chunk]], axis=1), jnp.concatenate([gate[:, chunk:], out[:, chunk:]], axis=1)]

        leave = exchange(
            jnp.concatenate([one[2][1:2] for _, one in sorted(backs.items())], axis=1),
            jnp.concatenate([one[2][0:1] for _, one in sorted(backs.items())], axis=1),
            True,
        )
        gate_backs = {}
        mlp_others = {}

        def send_along(step, token):
            other = tensor_size - 1 - step
            values, token = lax.optimization_barrier((moved[step].finish(), token))
            mlp_others[other] = swap_tensor(values, other)
            return token

        leave, hold = steps([moved[2], out_moved[backward[0]]], leave)
        leave = send_along(0, leave)
        for step, pair in enumerate(backward):
            part = slice(2 * pair * local_blocks, 2 * (pair + 1) * local_blocks)
            lanes = slice(pair * pair_width, (pair + 1) * pair_width)
            branch, conv_out, recur_open, inflow = fed[pair][:4]
            local, product, _ = backs[pair]
            gate_backs[pair] = list(
                call(
                    gate_back_kernel,
                    groups,
                    [lanes_of(length), lanes_of(length), lanes_of(1), lanes_of(length + 8)] + [lanes_of(length)] * 3 + [lanes_of(full), blocks_of(), blocks_of(), lanes_of(8)],
                    [lanes_of(length), blocks_of(), blocks_of(), lanes_of(8)],
                    [shaped(length, pair_width), shaped(2 * local_blocks, BLOCK, BLOCK), shaped(2 * local_blocks, BLOCK, BLOCK), shaped(8, pair_width)],
                    [pltpu.VMEM((length, GROUP), bf16)] * 3,
                    hold=hold,
                )(local, product, leave[:, lanes], mixed[pair][1], recur_open, inflow, conv_out, branch, rgates[part], igates[part], table[:, lanes])
            )
            if step == 0:
                token, marks = steps([moved[3], out_moved[backward[1]]], gate_backs[pair][3])
                hold = [token] + marks
                gate_backs[pair][3] = token
            else:
                gate_backs[pair][3], hold = steps([moved[2]], gate_backs[pair][3])
        gate_list = [gate_backs[pair] for pair in range(pairs)]
        heads = jnp.concatenate([one[0][:8] for one in gate_list], axis=1)
        heads = jnp.concatenate(relative(split_lanes(heads, tensor_size), tensor_at), axis=1)
        heads = lax.ppermute(heads, "tensor", [(at + 1, at) for at in range(tensor_size - 1)])
        after = jnp.concatenate(relative(split_lanes(heads, tensor_size), tensor_at), axis=1)
        mlp_others[tensor_size - 1], after = lax.optimization_barrier((mlp_others[tensor_size - 1], after))
        after = send_along(2, send_along(1, after))
        after, marks = steps([out_moved[backward[0]]], after)
        hold = hold + marks
        rgrads = jnp.concatenate([one[1] for one in gate_list], axis=0)
        igrads = jnp.concatenate([one[2] for one in gate_list], axis=0)
        rows = jnp.concatenate([one[3] for one in gate_list], axis=1)
        decay_row = rows[3:4] * (8.0 * jax.nn.sigmoid(-decay_rates))
        rows = jnp.concatenate([rows[4:8], rows[0:3], decay_row], axis=0)
        small_low, small_high = [], []
        if merged:
            small_target = fixed((half, 2 * BLOCK))

            def small_grads(*args, **sizes):
                small_grads_kernel(*args, sub=sub, local_blocks=local_blocks, chunks=tensor_size)
            small_halves = call(
                small_grads, 1, [SCALARS, gate_spec, gate_spec, fixed((kinds, channels))], [small_target] * tensor_size,
                [shaped(half, 2 * BLOCK, kind=bf16)] * tensor_size, [], hold=hold,
            )(places, rgrads, igrads, rows)
            small_low, small_high = small_halves[0::2], small_halves[1::2]
        else:
            gate_grads = jnp.stack([rgrads, igrads], axis=0).reshape(2, tensor_size, local_blocks, dp_size, sub, BLOCK)
            gate_grads = gate_grads.transpose(3, 0, 2, 4, 1, 5).reshape(dp_size, gate_rows, tensor_size * BLOCK)
            gate_grads = jnp.take(gate_grads, natural_at, axis=0)
            rows = rows.reshape(kinds, tensor_size, local_blocks, BLOCK).transpose(0, 2, 1, 3).reshape(1, vector_rows, -1)
            rest = small_rows - gate_rows - vector_rows
            pieces = [
                gate_grads,
                jnp.broadcast_to(rows, (dp_size,) + rows.shape[1:]),
                jnp.zeros((dp_size, rest, tensor_size * BLOCK), f32),
            ]
            small_grads = jnp.concatenate(pieces, axis=1).reshape(dp_size * small_rows, -1).astype(bf16)
            small_own, small_other = jnp.split(small_grads, 2, axis=0)
        if not merged:
            small_moved = Scatter(small_own, small_other, order_one, small_rows)

        in_parts = {}
        for step, pair in enumerate(backward):
            low, high = in_pairs[pair]
            lanes = slice(pair * pair_width, (pair + 1) * pair_width)
            smalls = [small_low[pair], small_high[pair]] if merged else []
            moved_width = pair_width + 2 * BLOCK * merged

            def branch_back(*refs, count=len(smalls)):
                branch_back_kernel(*refs[:7], refs[7 : 7 + count], *refs[7 + count :], groups=groups)

            last = groups - 1
            normed_grad, low_grad, high_grad = call(
                branch_back,
                moved_width // GROUP,
                [lanes_until(length, last), lanes_until(8, last), lanes_until(8, last), turned, lanes_until(half, last), lanes_until(half, last), whole]
                + [fixed((half, GROUP))] * len(smalls),
                [whole, lanes_of(half), lanes_of(half)],
                [shaped(length, model), shaped(half, moved_width, kind=bf16), shaped(half, moved_width, kind=bf16)],
                [pltpu.VMEM((length + 8, GROUP), f32), pltpu.VMEM((length, GROUP), bf16)],
                hold=hold,
            )(gate_backs[pair][0], after[:, lanes], table[:, lanes], normed_one_t, low, high, normed_grad, *smalls)
            in_parts[pair] = Scatter(low_grad, high_grad, orders[step % 2], block_rows)
            if step == 0:
                normed_grad, hold = steps([moved[3], out_moved[backward[1]], out_moved[backward[0]]], normed_grad)
            else:
                normed_grad, hold = steps([out_moved[backward[1]], in_parts[backward[0]], in_parts[backward[1]]], normed_grad)

        hidden_grad, gain_one = call(
            final_kernel, 1, [SCALARS, whole, whole, whole, fixed((2, model))], [whole, fixed((1, model))],
            [shaped(length, model), shaped(1, model)], [pltpu.VMEM((length, model), f32)],
            hold=hold,
        )(places, hidden_low, normed_grad, middle_grad, gains)
        in_list = [in_parts[pair] for pair in backward]
        gain_one, = round_of(in_list, gain_one)
        late = [gain_one]
        gain_parts = jnp.concatenate([gain_one, gain_two], axis=0).reshape(2, dp_size, block_rows)
        if not fast:
            gain_parts = jnp.take(gain_parts, natural_at, axis=1)
        gain_parts = jnp.pad(gain_parts.transpose(1, 0, 2), ((0, 0), (0, 6), (0, BLOCK - block_rows)))
        gain_parts = gain_parts.reshape(8 * dp_size, BLOCK)
        gains_moved = Scatter(gain_parts[: 4 * dp_size], gain_parts[4 * dp_size :], order_one, 8)
        out_parts = [part for pair in range(pairs) for part in separate(out_moved[pair].finish())]
        out_others = {other: swap_tensor(out_parts[other], other) for other in range(tensor_size - 1, 0, -1)}
        mlp_columns = [[((3 * at + which) * GROUP, GROUP) for at in range(mlp_groups)] for which in range(3)]
        mlp_grads = join_parts(moved[-1].finish(), mlp_others, mlp_columns, late)
        far, near = out_others[tensor_size - 1], out_others[tensor_size - 2]
        far, near = round_of(in_list + [gains_moved], far, near)
        out_others.update({tensor_size - 1: far, tensor_size - 2: near})
        round_of([one for one in in_list] + [gains_moved])
        out_columns = [[(0, chunk)], [(chunk, chunk)]]
        gate_grad, out_grad = join_parts(out_parts[0], out_others, out_columns, late)

        def in_chunks(values):
            if not merged:
                return split_lanes(values, 2)
            one, two = values[:, :chunk], values[:, chunk:pair_width]
            small_one, small_two = split_lanes(values[:, pair_width:], 2)
            return [jnp.concatenate([one, small_one], axis=1), jnp.concatenate([two, small_two], axis=1)]

        in_sum, in_far = join_tensor([part for pair in range(pairs) for part in in_chunks(in_parts[pair].finish())])
        gain_sum = gains_moved.finish()
        gain_sum = sum(spread_tensor(gain_sum)[1:], gain_sum)
        gain_rows = block_rows // tensor_size
        gain_sum = lax.dynamic_slice(gain_sum, (0, tensor_at * gain_rows), (2, gain_rows)).T

        hidden_grad = features(hidden_grad, True)
        if merged:
            in_sum, small_sum = in_sum[:, :chunk], in_sum[:, chunk:]
        else:
            small_sum, _ = join_tensor(split_lanes(small_moved.finish(), tensor_size))

        gate_sum = small_sum[:gate_rows].reshape(2, local_blocks, sub, BLOCK).transpose(0, 2, 1, 3)
        vector_sum = lax.dynamic_slice(small_sum, (gate_rows, dp_at * sub), (vector_rows, sub))
        vector_sum = vector_sum.reshape(kinds, local_blocks, sub)

        return (
            hidden_out,
            hidden_grad,
            gain_sum,
            in_sum,
            gate_grad,
            out_grad,
            gate_sum[1],
            gate_sum[0],
            vector_sum[:CONV].transpose(2, 0, 1),
            vector_sum[4].T,
            vector_sum[5].T,
            vector_sum[6].T,
            vector_sum[7].T,
            mlp_grads[0],
            mlp_grads[1],
            mlp_grads[2],
        )

    return per_device


def solution(mesh):
    rows = P(("dp", "tensor"), None)
    matrix = P("dp", "tensor")
    gate = P("dp", "tensor", None)
    kernel = P("dp", None, "tensor")
    placed = (rows, rows, P("dp", None), matrix, matrix, matrix, gate, gate, kernel) + (matrix,) * 7
    made = (rows, rows, rows, matrix, matrix, matrix, gate, gate, kernel) + (matrix,) * 7
    return jax.shard_map(
        make_per_device(mesh.shape["dp"], mesh.shape["tensor"]),
        mesh=mesh,
        in_specs=placed,
        out_specs=made,
        check_vma=False,
    )
```
